256 devices in a mesh: group: 8 (over z), tensor: 32 (over x, y, core).
Axes of the slice: x: 4, y: 4, z: 8, core: 2. Of those that a mesh axis runs over, the one named last changes fastest.
Arguments:
- residual_in: bfloat16 [8192, 2048], P(('group', 'tensor')), parts along dimension 0, may hold values from -22 to 22
- attn_gain: float32 [2048], replicated, may hold values from 0.5 to 1.5
- w_query: bfloat16 [2048, 4096], P(None, 'tensor'), may hold values from -0.125 to 0.125
- w_keyval: bfloat16 [1024, 2048], P('tensor'), may hold values from -0.125 to 0.125
- query_gain: float32 [128], replicated, may hold values from 0.1 to 1.9
- key_gain: float32 [128], replicated, may hold values from 0.1 to 1.9
- w_out: bfloat16 [4096, 2048], P('tensor'), may hold values from -0.09375 to 0.09375
- ffn_gain: float32 [2048], replicated, may hold values from 0.5 to 1.5
- w_gate: bfloat16 [32, 768, 2048], P('tensor'), may hold values from -0.125 to 0.125
- w_up: bfloat16 [32, 768, 2048], P('tensor'), may hold values from -0.125 to 0.125
- w_down: bfloat16 [32, 768, 2048], P('tensor'), may hold values from -0.21875 to 0.21875
- key_cache: bfloat16 [256, 1024, 512], P(('group', 'tensor')), parts along dimension 0, may hold values from -110 to 110
- value_cache: bfloat16 [256, 1024, 512], P(('group', 'tensor')), parts along dimension 0, may hold values from -18 to 18
- prefix_lens: int32 [256], P(('group', 'tensor')), parts along dimension 0, may hold values from 1 to 992
- accepted: int32 [256], P(('group', 'tensor')), parts along dimension 0, may hold values from 1 to 8
- accept_path: int32 [256, 8], P(('group', 'tensor')), parts along dimension 0, may hold values from 0 to 14, as said below
- parents: int32 [256, 32], P(('group', 'tensor')), parts along dimension 0, may hold values from -1 to 30, as said below
- slot_kinds: int32 [256], P(('group', 'tensor')), parts along dimension 0, may hold values from 0 to 1
- expert_ids: int32 [8192, 8], P('group'), parts along dimension 0, may hold values from 0 to 127, as said below
- gate_probs: float32 [8192, 8], P('group'), parts along dimension 0, may hold values from 0.1 to 1
Outputs:
- mixed: bfloat16 [8192, 2048], P(('group', 'tensor')), parts along dimension 0
The draws below stay inside these ranges and needn't reach their ends.
There are 8 independent parts, one for each index of `group`. The reference program is written for one: setup_inputs(seed, part) draws one part's arguments, and reference() takes and returns one part's arrays. A program takes and returns all parts, laid end to end along the dimension named above; an argument that names none is the same for every part. Nothing has to cross between parts.
Inputs may be any that keep to these rules, and one draw needn't show every extreme that they name: `expert_ids`: the tokens of each slot name each of the 128 experts exactly 32 * 8 // 128 times; a token never names one expert twice. `accept_path`: each row starts at 0 and rises by 1 or 2 from one entry to the next. `parents`: node 0 of every slot has parent -1; every other node's parent is an earlier node of the same slot.
All inputs are finite; a program needn't handle non-finite values.
Results may differ from the reference program's by a relative error of at most 0.02.
Values may be sent and summed in bfloat16 or wider, within the bound.
A program may use at most 128 MiB of HBM per device.

```python
import math
import jax
import jax.numpy as jnp
from jax import lax

D = 2048
HQ = 32
KVH = 4
HD = 128
FF = 768
EXPERTS = 128
TOPK = 8
NEW = 32
CACHE = 1024
ACC = 8
SINK = 4
WIN = 512
SLOTS = 32
TOK = 1024
EXP_WIN = 32
PER = 2


def draw_residual_in(key, part):
    key_base, key_rows, key_cols = jax.random.split(jax.random.fold_in(key, 11), 3)
    base_draw = jax.random.truncated_normal(key_base, -6.0, 6.0, (TOK, D), jnp.float32)
    row_scale = jnp.exp(jax.random.uniform(key_rows, (TOK, 1), jnp.float32, math.log(0.3), math.log(3.0)))
    col_scale = jnp.exp(jax.random.uniform(key_cols, (1, D), jnp.float32, math.log(0.5), math.log(2.0)))
    return (0.6 * base_draw * row_scale * col_scale).astype(jnp.bfloat16)


def draw_key_cache(key, part):
    key_base = jax.random.fold_in(jax.random.fold_in(key, 23), 0)
    shape_all = (SLOTS, CACHE, KVH * HD)
    base_draw = jax.random.truncated_normal(key_base, -6.0, 6.0, shape_all, jnp.float32)
    return base_draw.astype(jnp.bfloat16)


def draw_prefix_lens(key, part):
    key_first, key_second, key_pick = jax.random.split(jax.random.fold_in(key, 37), 3)
    span_rows = CACHE - NEW
    first_draw = jax.random.randint(key_first, (SLOTS,), 0, span_rows)
    second_draw = jax.random.randint(key_second, (SLOTS,), 0, span_rows)
    lengths = 1 + first_draw * second_draw // max(span_rows - 1, 1)
    chosen_slot = jax.random.randint(key_pick, (), 0, SLOTS)
    return jnp.where(jnp.arange(SLOTS) == chosen_slot, span_rows, lengths).astype(jnp.int32)


def draw_accepted(key, part):
    counts_drawn = jax.random.randint(jax.random.fold_in(key, 41), (SLOTS,), 1, ACC + 1)
    return counts_drawn.at[SLOTS - 1].set(ACC).astype(jnp.int32)


def draw_accept_path(key, part):
    step_sizes = jax.random.randint(jax.random.fold_in(key, 53), (SLOTS, ACC), 1, 3)
    step_sizes = step_sizes.at[0].set(2)
    step_sizes = step_sizes.at[:, 0].set(0)
    return jnp.cumsum(step_sizes, axis=1).astype(jnp.int32)


def draw_parents(key, part):
    raw_draw = jax.random.randint(jax.random.fold_in(key, 67), (SLOTS, NEW), 0, 1 << 20)
    node_index = jnp.arange(NEW, dtype=jnp.int32)[None, :]
    picked = raw_draw % jnp.maximum(node_index, 1)
    picked = jnp.where(node_index == 0, -1, picked)
    return picked.at[0, NEW - 1].set(NEW - 2).astype(jnp.int32)


def draw_expert_ids(key, part):
    slot_keys = jax.random.split(jax.random.fold_in(key, 79), SLOTS)

    def one_order(slot_key):
        return jax.random.permutation(slot_key, EXPERTS)
    orders = jax.vmap(one_order)(slot_keys)
    tiled = jnp.tile(orders, (1, NEW * TOPK // EXPERTS))
    return tiled.reshape(SLOTS * NEW, TOPK).astype(jnp.int32)


def plant(values, stream_key, smallest, largest):
    longest = values.shape.index(max(values.shape))
    spots = []
    for shift in (0, 1):
        where = [jax.random.randint(jax.random.fold_in(stream_key, axis), (), 0, length) for axis, length in enumerate(values.shape)]
        where[longest] = (where[longest] + shift) % values.shape[longest]
        spots.append(tuple(where))
    return values.at[spots[0]].set(smallest).at[spots[1]].set(largest)


def levels(key, shape, cuts, least, high):
    def one(dim, parts):
        heights = jax.random.uniform(jax.random.fold_in(jax.random.fold_in(key, 6), dim), (parts,), jnp.float32, least / len(cuts), high / len(cuts))
        return jnp.repeat(jnp.exp(heights), shape[dim] // parts).reshape((-1,) + (1,) * (len(shape) - dim - 1))

    gain = one(*cuts[0])
    for cut in cuts[1:]:
        gain = gain * one(*cut)
    return gain


def centred(rng, extent, width, limit, cuts=(), kind=jnp.bfloat16):
    values = width * jax.random.normal(rng, extent, jnp.float32)
    if cuts:
        values = values * levels(rng, extent, cuts, -0.22, 0.18)
    return jnp.clip(values, -limit, limit).astype(kind)


def setup_inputs(seed: int = 0, part: int = 0) -> dict:
    arg_keys = jax.random.split(jax.random.key(seed), 21)
    own_keys = jax.random.split(jax.random.fold_in(arg_keys[20], part), 21)
    return {
        "residual_in": draw_residual_in(jax.random.fold_in(jax.random.fold_in(arg_keys[20], part), 71), part),
        "attn_gain": jnp.clip(1.0 + 0.1 * jax.random.normal(arg_keys[1], (D,), jnp.float32), 0.5, 1.5),
        "w_query": centred(arg_keys[2], (D, HQ * HD), D ** -0.5, 0.125, ((1, 32),)),
        "w_keyval": centred(arg_keys[3], (2 * KVH * HD, D), D ** -0.5, 0.125, ((0, 32),)),
        "query_gain": jnp.clip(1.0 + 0.18 * jax.random.normal(arg_keys[4], (HD,), jnp.float32), 0.1, 1.9),
        "key_gain": jnp.clip(1.0 + 0.18 * jax.random.normal(arg_keys[5], (HD,), jnp.float32), 0.1, 1.9),
        "w_out": centred(arg_keys[6], (HQ * HD, D), (HQ * HD) ** -0.5, 0.09375, ((0, 32),)),
        "ffn_gain": jnp.clip(1.0 + 0.1 * jax.random.normal(arg_keys[7], (D,), jnp.float32), 0.5, 1.5),
        "w_gate": centred(arg_keys[8], (EXP_WIN, FF, D), D ** -0.5, 0.125, ((0, 32),)),
        "w_up": centred(arg_keys[9], (EXP_WIN, FF, D), D ** -0.5, 0.125, ((0, 32),)),
        "w_down": centred(arg_keys[10], (EXP_WIN, FF, D), FF ** -0.5, 0.21875, ((0, 32),)),
        "key_cache": draw_key_cache(jax.random.fold_in(jax.random.fold_in(arg_keys[20], part), 71), part),
        "value_cache": centred(own_keys[12], (SLOTS, CACHE, KVH * HD), 3.0, 18.0, ((0, 32),)),
        "prefix_lens": draw_prefix_lens(jax.random.fold_in(jax.random.fold_in(arg_keys[20], part), 71), part),
        "accepted": draw_accepted(jax.random.fold_in(jax.random.fold_in(arg_keys[20], part), 71), part),
        "accept_path": draw_accept_path(jax.random.fold_in(jax.random.fold_in(arg_keys[20], part), 71), part),
        "parents": draw_parents(jax.random.fold_in(jax.random.fold_in(arg_keys[20], part), 71), part),
        "slot_kinds": plant(jax.random.randint(own_keys[17], (SLOTS,), 0, 2), jax.random.fold_in(own_keys[17], 1), 0, 1).astype(jnp.int32),
        "expert_ids": draw_expert_ids(jax.random.fold_in(jax.random.fold_in(arg_keys[20], part), 71), part),
        "gate_probs": jnp.clip(jax.random.uniform(own_keys[19], (TOK, TOPK), jnp.float32, 0.1, 1.0), 0.1, 1.0),
    }


EPSILON = 1e-06
NEG_FILL = -1e+30
ROPE_BASE = 1000000.0

def rms_rows(values, weight_gain):
    return values * lax.rsqrt(lax.optimization_barrier(jnp.mean(values * values, axis=-1, keepdims=True)) + EPSILON) * weight_gain

def rotate(values, angles):
    half_dim = values.shape[-1] // 2
    cosine = jnp.cos(angles)[:, None, :]
    sine_val = jnp.sin(angles)[:, None, :]
    lower_half = values[..., :half_dim]
    upper_half = values[..., half_dim:]
    return jnp.concatenate([lower_half * cosine - upper_half * sine_val, upper_half * cosine + lower_half * sine_val], axis=-1)

def ancestors(parent_row, count_new):
    parent_link = jax.nn.one_hot(parent_row, count_new, dtype=jnp.float32)
    reach_mat = jnp.eye(count_new, dtype=jnp.float32) + parent_link
    for unused in range((count_new - 1).bit_length()):
        reach_mat = jnp.minimum(jnp.dot(reach_mat, reach_mat, precision=lax.Precision.HIGHEST), 1.0)
    return reach_mat

def attend(query_raw, keyval_raw, key_cache, value_cache, prefix_len, accepted_len, path_row, parent_row, kind_value, query_gain, key_gain):
    count_new = query_raw.shape[0]
    head_dim = query_gain.shape[0]
    kv_heads = key_cache.shape[-1] // head_dim
    q_heads = query_raw.shape[-1] // head_dim
    group_size = q_heads // kv_heads
    cache_len = key_cache.shape[0]
    acc_count = path_row.shape[0]
    total_len = prefix_len + accepted_len
    reach_mat = ancestors(parent_row, count_new)
    index_row = jnp.arange(count_new)
    causal = (index_row[None, :] <= index_row[:, None]).astype(jnp.float32)
    is_tree = kind_value == 1
    allowed = jnp.where(is_tree, reach_mat, causal) > 0.5
    depth_used = jnp.where(is_tree, lax.optimization_barrier(jnp.sum(reach_mat, axis=1)) - 1.0, index_row.astype(jnp.float32))
    position = total_len.astype(jnp.float32) + depth_used
    half_dim = head_dim // 2
    freq_table = jnp.exp(-(2.0 * jnp.arange(half_dim, dtype=jnp.float32) / head_dim) * math.log(ROPE_BASE))
    angles = position[:, None] * freq_table[None, :]
    query_rot = rotate(rms_rows(query_raw.astype(jnp.float32).reshape(count_new, q_heads, head_dim), query_gain), angles).astype(jnp.bfloat16)
    key_width = kv_heads * head_dim
    key_new = rotate(rms_rows(keyval_raw[:, :key_width].astype(jnp.float32).reshape(count_new, kv_heads, head_dim), key_gain), angles).astype(jnp.bfloat16)
    value_new = keyval_raw[:, key_width:].reshape(count_new, kv_heads, head_dim)
    acc_rows = (prefix_len + path_row).astype(jnp.int32)
    key_acc = jnp.take(key_cache, acc_rows, axis=0).reshape(acc_count, kv_heads, head_dim)
    value_acc = jnp.take(value_cache, acc_rows, axis=0).reshape(acc_count, kv_heads, head_dim)
    cache_pos = jnp.arange(cache_len)
    seen_old = (cache_pos < prefix_len) & ((cache_pos < SINK) | (cache_pos >= total_len - WIN))
    acc_index = jnp.arange(acc_count)
    acc_pos = prefix_len + acc_index
    seen_acc = (acc_index < accepted_len) & ((acc_pos < SINK) | (acc_pos >= total_len - WIN))
    keys_all = jnp.concatenate([key_cache.reshape(cache_len, kv_heads, head_dim), key_acc, key_new], axis=0)
    values_all = jnp.concatenate([value_cache.reshape(cache_len, kv_heads, head_dim), value_acc, value_new], axis=0)
    seen_all = jnp.concatenate([jnp.broadcast_to(seen_old[None, :], (count_new, cache_len)), jnp.broadcast_to(seen_acc[None, :], (count_new, acc_count)), allowed], axis=1)
    query_group = query_rot.astype(jnp.float32).reshape(count_new, kv_heads, group_size, head_dim)
    scores = jnp.einsum('nkgd,mkd->kgnm', query_group, keys_all.astype(jnp.float32)) * head_dim ** (-0.5)
    scores = jnp.where(seen_all[None, None], scores, NEG_FILL)
    row_max = lax.optimization_barrier(jnp.max(scores, axis=-1, keepdims=True))
    expo_all = jnp.exp(scores - row_max)
    probs_bf = (expo_all / lax.optimization_barrier(jnp.sum(expo_all, axis=-1, keepdims=True))).astype(jnp.bfloat16)
    result = jnp.einsum('kgnm,mkd->nkgd', probs_bf.astype(jnp.float32), values_all.astype(jnp.float32))
    return result.reshape(count_new, q_heads * head_dim).astype(jnp.bfloat16)

def reference(residual_in, attn_gain, w_query, w_keyval, query_gain, key_gain, w_out, ffn_gain, w_gate, w_up, w_down, key_cache, value_cache, prefix_lens, accepted, accept_path, parents, slot_kinds, expert_ids, gate_probs):
    normed = rms_rows(residual_in.astype(jnp.float32), attn_gain).astype(jnp.bfloat16)
    query_raw = jnp.dot(normed, w_query, preferred_element_type=jnp.float32).astype(jnp.bfloat16)
    keyval_raw = jnp.dot(normed, jnp.transpose(w_keyval), preferred_element_type=jnp.float32).astype(jnp.bfloat16)

    def slot_attend(packed):
        return attend(*packed, query_gain, key_gain)
    attn_out = lax.map(slot_attend, (query_raw.reshape(SLOTS, NEW, -1), keyval_raw.reshape(SLOTS, NEW, -1), key_cache, value_cache, prefix_lens, accepted, accept_path, parents, slot_kinds))
    attn_out = attn_out.reshape(TOK, HQ * HD)
    hidden_mid = residual_in.astype(jnp.float32) + jnp.dot(attn_out, w_out, preferred_element_type=jnp.float32)
    normed_ffn = rms_rows(hidden_mid, ffn_gain).astype(jnp.bfloat16)
    count_rows = SLOTS * PER

    def expert_step(running, expert):
        hit_mask = expert_ids == expert
        weights = lax.optimization_barrier(jnp.sum(jnp.where(hit_mask, gate_probs, 0.0), axis=1))
        named_int = jnp.any(hit_mask, axis=1).astype(jnp.int32)
        chosen = jnp.argsort(1 - named_int, stable=True)[:count_rows].astype(jnp.int32)
        picked = normed_ffn[chosen]
        gate_val = jnp.dot(picked, jnp.transpose(w_gate[expert]), preferred_element_type=jnp.float32)
        up_val = jnp.dot(picked, jnp.transpose(w_up[expert]), preferred_element_type=jnp.float32)
        inner_act = (jax.nn.silu(gate_val) * up_val).astype(jnp.bfloat16)
        result = jnp.dot(inner_act, w_down[expert], preferred_element_type=jnp.float32)
        return (running.at[chosen].add(result * weights[chosen][:, None]), None)
    moe_total, unused = lax.scan(expert_step, jnp.zeros((TOK, D), jnp.float32), jnp.arange(EXP_WIN, dtype=jnp.int32))
    return (hidden_mid + moe_total).astype(jnp.bfloat16)
```

```python
import functools
import math

import jax
import jax.numpy as jnp
import numpy as np
from jax import lax
from jax.experimental import pallas as pl
from jax.experimental.pallas import tpu as pltpu
from jax.sharding import PartitionSpec as P

SINK = 4
WIN = 512
EPSILON = 1e-06
NEG_FILL = -1e30
ROPE_BASE = 1000000.0

N = 32
TOKS = 32
D = 2048
HD = 128
FF = 768
CACHE = 1024
SCALE = HD**-0.5
LOG2E = math.log2(math.e)

BF = jnp.bfloat16
F32 = jnp.float32
MESH = pl.DeviceIdType.MESH
NT = (((1,), (1,)), ((), ()))
TN = (((0,), (0,)), ((), ()))


def dot(a, b, dims=(((1,), (0,)), ((), ()))):
    return lax.dot_general(a, b, dims, preferred_element_type=F32)


def layer_kernel(
    freq_ref, attn_gain, query_gain, key_gain, ffn_gain, parents, prefix, accepted, path, kind,
    res_hbm, wq_hbm, wkv_hbm, wo_hbm, wg_hbm, wu_hbm, wd_hbm, kc_hbm, vc_hbm, ids_hbm, gates_hbm,
    out_ref,
    res, wq, wkv, wo, wg, wu, wd, kc, vc, ids, gates,
    ag, qsend, qrecv, asend, ain,
    part, s1, r1, s2, r2, u1, v1, u2, v2, rsum,
    fs, xs, dsend, drecv, ysend, yrecv, sel_ref, comb_ref, cos_ref, sin_ref, allow_ref,
    lsem, wsend, wrecv, gs, ga, gh, gb, gbh, hs, qs, qr, asem, ar,
    t1s, t1r, t2s, t2r, p1s, p1r, p2s, p2r, ds, dr, ys, yr,
):
    t = lax.axis_index("tensor")
    core = lax.rem(t, 2)
    chip = t // 2
    cx = chip // 4
    cy = lax.rem(chip, 4)
    a = cx * (1 - core) + cy * core
    b = cy * (1 - core) + cx * core
    step_a = 8 - 6 * core
    step_b = 2 + 6 * core

    def dev(a_, b_):
        return a_ * step_a + b_ * step_b + core

    def ring(v, k):
        return lax.rem(v + k, 4)

    def remote(src, dst, ssem, rsem, to):
        return pltpu.make_async_remote_copy(
            src_ref=src, dst_ref=dst, send_sem=ssem, recv_sem=rsem,
            device_id={"tensor": to}, device_id_type=MESH,
        )

    def await_bytes(ref, sem):
        pltpu.make_async_copy(ref, ref, sem).wait()

    load_res = pltpu.make_async_copy(res_hbm, res, lsem.at[0])
    load_res.start()
    wkv[...] = jnp.zeros_like(wkv)
    lane0 = pl.multiple_of(core * HD, HD)
    kv_row = pl.multiple_of(lax.rem(chip, 2) * 64 + core * 32, 32)
    lane_win = pl.multiple_of((t // 4) * HD, HD)
    loads = [
        pltpu.make_async_copy(wq_hbm, wq.at[:, pl.ds(lane0, HD)], lsem.at[1]),
        pltpu.make_async_copy(wkv_hbm, wkv.at[pl.ds(kv_row, 32)], lsem.at[2]),
        pltpu.make_async_copy(ids_hbm.at[:, pl.ds(lane_win, HD)], ids, lsem.at[3]),
        pltpu.make_async_copy(gates_hbm.at[:, pl.ds(lane_win, HD)], gates, lsem.at[4]),
        pltpu.make_async_copy(wo_hbm, wo.at[pl.ds(lane0, HD)], lsem.at[5]),
        pltpu.make_async_copy(kc_hbm.at[0], kc, lsem.at[6]),
        pltpu.make_async_copy(vc_hbm.at[0], vc, lsem.at[7]),
        pltpu.make_async_copy(wg_hbm.at[0], wg, lsem.at[8]),
        pltpu.make_async_copy(wu_hbm.at[0], wu, lsem.at[9]),
        pltpu.make_async_copy(wd_hbm.at[0], wd, lsem.at[10]),
    ]
    for load in loads:
        load.start()

    barrier = pltpu.get_barrier_semaphore()

    def greet(k, carry):
        pl.semaphore_signal(
            barrier, inc=1, device_id={"tensor": lax.rem(t + k, N)}, device_id_type=MESH
        )
        return carry

    lax.fori_loop(1, N, greet, 0)

    load_res.wait()
    own = b * 4 + a
    xv = res[...].astype(F32)
    inv = lax.rsqrt(jnp.mean(xv * xv, axis=-1, keepdims=True) + EPSILON)
    ag[own] = (xv * inv * attn_gain[...][None, :]).astype(BF)

    pl.semaphore_wait(barrier, N - 1)

    up_a, down_a = dev(ring(a, 1), b), dev(ring(a, 3), b)
    up_b, down_b = dev(a, ring(b, 1)), dev(a, ring(b, 3))

    def blk(a_, b_):
        return ag.at[b_ * 4 + a_]

    def half(a_, b_, h):
        return ag.at[b_ * 4 + a_, pl.ds(16 * h, 16)]

    sends = []

    def go(copy):
        copy.start()
        sends.append(copy)

    def spread_b(j, a_):
        go(remote(blk(a_, b), blk(a_, b), gs.at[2 + 2 * j], gb.at[j, 0], up_b))
        go(remote(blk(a_, b), blk(a_, b), gs.at[3 + 2 * j], gb.at[j, 1], down_b))

    go(remote(blk(a, b), blk(a, b), gs.at[0], ga.at[0], up_a))
    go(remote(blk(a, b), blk(a, b), gs.at[1], ga.at[1], down_a))
    spread_b(0, a)

    sibling = t + 1 - 2 * core
    go(remote(wq_hbm, wq.at[:, pl.ds(lane0, HD)], wsend.at[0], wrecv.at[0], sibling))
    go(remote(wkv_hbm, wkv.at[pl.ds(kv_row, 32)], wsend.at[1], wrecv.at[1], sibling))
    go(remote(wo_hbm, wo.at[pl.ds(lane0, HD)], wsend.at[2], wrecv.at[2], sibling))

    am, ap, af = ring(a, 3), ring(a, 1), ring(a, 2)
    bm, bp, bf = ring(b, 3), ring(b, 1), ring(b, 2)

    await_bytes(blk(am, b), ga.at[0])
    go(remote(half(am, b, 0), half(am, b, 0), hs.at[0], gh.at[0], up_a))
    spread_b(1, am)
    await_bytes(blk(ap, b), ga.at[1])
    go(remote(half(ap, b, 1), half(ap, b, 1), hs.at[1], gh.at[1], down_a))
    spread_b(2, ap)

    def relay_b(j, a_):
        await_bytes(blk(a_, bm), gb.at[j, 0])
        go(remote(half(a_, bm, 0), half(a_, bm, 0), hs.at[2 + 2 * j], gbh.at[j, 0], up_b))
        await_bytes(blk(a_, bp), gb.at[j, 1])
        go(remote(half(a_, bp, 1), half(a_, bp, 1), hs.at[3 + 2 * j], gbh.at[j, 1], down_b))

    relay_b(0, a)
    await_bytes(half(af, b, 0), gh.at[0])
    await_bytes(half(af, b, 1), gh.at[1])
    spread_b(3, af)

    for load in loads[:2]:
        load.wait()
    other_lane = pl.multiple_of(HD - core * HD, HD)
    other_row = pl.multiple_of(lax.rem(chip, 2) * 64 + 32 - core * 32, 32)
    await_bytes(wq.at[:, pl.ds(other_lane, HD)], wrecv.at[0])
    await_bytes(wkv.at[pl.ds(other_row, 32)], wrecv.at[1])

    def project(b_):
        rows = ag[pl.ds(b_ * 4, 4)].reshape(4 * TOKS, D)
        q = dot(rows, wq[...])
        kv = dot(rows, wkv[...], NT)
        qsend[pl.ds(b_ * 4, 4), :, 0 : 2 * HD] = q.astype(BF).reshape(4, TOKS, 2 * HD)
        qsend[pl.ds(b_ * 4, 4), :, 2 * HD :] = kv.astype(BF).reshape(4, TOKS, HD)

    def post_queries(b_, first):
        for k in range(first, 4):
            a_ = ring(a, k)
            copy = remote(
                qsend.at[b_ * 4 + a_], qrecv.at[chip], qs, qr, dev(a_, b_)
            )
            copy.start()

    project(b)
    qrecv[chip] = qsend[own]
    post_queries(b, 1)

    relay_b(1, am)
    relay_b(2, ap)

    for load in loads[2:4]:
        load.wait()
    line = lax.broadcasted_iota(jnp.int32, (2 * N, TOKS), 0)
    expert = line // 2
    named = jnp.zeros((2 * N, TOKS), F32)
    weight = jnp.zeros((2 * N, TOKS), F32)
    turn_lanes = lax.rem(HD - lax.rem(t, 4) * TOKS, HD)
    idv = pltpu.roll(ids[...], turn_lanes, 1)[:, 0:TOKS]
    gv = pltpu.roll(gates[...], turn_lanes, 1)[:, 0:TOKS]
    for k in range(8):
        hit = jnp.broadcast_to(idv[k : k + 1], (2 * N, TOKS)) == expert
        named = jnp.where(hit, 1.0, named)
        weight = weight + jnp.where(hit, jnp.broadcast_to(gv[k : k + 1], (2 * N, TOKS)), 0.0)
    ri = lax.broadcasted_iota(jnp.int32, (TOKS, TOKS), 0)
    ci = lax.broadcasted_iota(jnp.int32, (TOKS, TOKS), 1)
    before = dot(named.astype(BF), jnp.where(ri < ci, 1.0, 0.0).astype(BF))
    turn = lax.rem(line, 2).astype(F32)
    taken = (named > 0.5) & (jnp.abs(before - turn) < 0.5)
    sel_ref[...] = jnp.where(taken, 1.0, 0.0).astype(BF)
    comb_ref[...] = jnp.where(taken, weight, 0.0)

    link = jnp.where((ri == jnp.broadcast_to(parents[...], (TOKS, TOKS))) | (ri == ci), 1.0, 0.0)
    for unused in range(5):
        link = jnp.minimum(dot(link.astype(BF), link.astype(BF)), 1.0)
    eye = jnp.where(ri == ci, 1.0, 0.0).astype(BF)
    reach = dot(link.astype(BF), eye, TN)
    is_tree = kind[0, 0] == 1
    causal = jnp.where(ci <= ri, 1.0, 0.0)
    allowed = jnp.where(is_tree, reach, causal)
    allow_ref[...] = allowed
    depth = jnp.sum(allowed, axis=1, keepdims=True) - 1.0
    total = prefix[0, 0] + accepted[0, 0]
    angle = (total.astype(F32) + depth) * freq_ref[...]
    cos_ref[...] = jnp.cos(angle)
    lane_row = lax.broadcasted_iota(jnp.int32, (TOKS, HD), 1)
    sine = jnp.sin(angle)
    sin_ref[...] = jnp.where(lane_row < HD // 2, -sine, sine)

    relay_b(3, af)
    project(bm)
    post_queries(bm, 0)
    project(bp)
    post_queries(bp, 0)

    for j, a_ in enumerate((a, am, ap, af)):
        await_bytes(half(a_, bf, 0), gbh.at[j, 0])
        await_bytes(half(a_, bf, 1), gbh.at[j, 1])
    project(bf)
    post_queries(bf, 0)

    row = lax.broadcasted_iota(jnp.int32, (1, CACHE), 1)
    seen = (row < prefix[0, 0]) & ((row < SINK) | (row >= total - WIN))
    for m in range(8):
        seen = seen | ((row == prefix[0, 0] + path[0, m]) & (accepted[0, 0] > m))
    for load in loads[5:7]:
        load.wait()
    await_bytes(qrecv.at[pl.ds(0, 15)], qr)

    def rope(v, gain):
        v = v * lax.rsqrt(jnp.mean(v * v, axis=-1, keepdims=True) + EPSILON) * gain
        return (v * cos_ref[...] + pltpu.roll(v, HD // 2, 1) * sin_ref[...]).astype(BF)

    def heads(g, carry):
        qgain = query_gain[...][None, :]
        qg = jnp.concatenate(
            [
                rope(qrecv[4 * g + i, :, HD * j : HD * (j + 1)].astype(F32), qgain)
                for i in range(4)
                for j in range(2)
            ],
            axis=0,
        )
        kraw = qrecv[2 * g, :, 2 * HD :].astype(F32) + qrecv[2 * g + 1, :, 2 * HD :].astype(F32)
        knew = rope(kraw, key_gain[...][None, :])
        vnew = qrecv[8 + 2 * g, :, 2 * HD :] + qrecv[9 + 2 * g, :, 2 * HD :]
        cols = pl.ds(pl.multiple_of(g * HD, HD), HD)
        s_old = dot(qg, kc[:, cols], NT)
        s_new = dot(qg, knew, NT)
        s_old = jnp.where(jnp.broadcast_to(seen, s_old.shape), s_old, NEG_FILL)
        allow = jnp.concatenate([allow_ref[...]] * 8, axis=0)
        s_new = jnp.where(allow > 0.5, s_new, NEG_FILL)
        top = jnp.maximum(
            jnp.max(s_old, axis=-1, keepdims=True), jnp.max(s_new, axis=-1, keepdims=True)
        )
        e_old = jnp.exp2((s_old - top) * (SCALE * LOG2E))
        e_new = jnp.exp2((s_new - top) * (SCALE * LOG2E))
        denom = jnp.sum(e_old, axis=-1, keepdims=True) + jnp.sum(e_new, axis=-1, keepdims=True)
        o = dot(e_old.astype(BF), vc[:, cols]) + dot(e_new.astype(BF), vnew)
        o = (o / denom).astype(BF)
        for i in range(4):
            to = 4 * g + i
            for j in range(2):
                r0 = (2 * i + j) * TOKS
                asend[to, :, HD * j : HD * (j + 1)] = o[r0 : r0 + TOKS]

            @pl.when(to != chip)
            def _():
                remote(asend.at[to], ain.at[own], asem, ar.at[b], 2 * to + core).start()

        return carry

    lax.fori_loop(0, 4, heads, 0)
    ain[own] = asend[chip]

    loads[4].wait()
    await_bytes(wo.at[pl.ds(other_lane, HD)], wrecv.at[2])
    order = (bf, bp, bm, b)
    for k, b_ in enumerate(order):
        await_bytes(ain.at[pl.ds(b_ * 4, 3 if k == 3 else 4)], ar.at[b_])
        part[k] = dot(ain[pl.ds(b_ * 4, 4)].reshape(4 * TOKS, 2 * HD), wo[...])
        far = pl.multiple_of(af * TOKS, TOKS)
        s1[k, 0] = part[k, pl.ds(far, 16), :].astype(BF)
        go(remote(s1.at[k, 0], r1.at[k, 0], t1s.at[k, 0], t1r.at[k, 0], up_a))
        s1[k, 1] = part[k, pl.ds(far + 16, 16), :].astype(BF)
        go(remote(s1.at[k, 1], r1.at[k, 1], t1s.at[k, 1], t1r.at[k, 1], down_a))
    for k in range(4):
        to_up = pl.multiple_of(ap * TOKS, TOKS)
        await_bytes(r1.at[k, 0], t1r.at[k, 0])
        s2[k, 0, 0:16] = (part[k, pl.ds(to_up, 16), :] + r1[k, 0].astype(F32)).astype(BF)
        s2[k, 0, 16:32] = part[k, pl.ds(to_up + 16, 16), :].astype(BF)
        go(remote(s2.at[k, 0], r2.at[k, 0], t2s.at[k, 0], t2r.at[k, 0], up_a))
        to_down = pl.multiple_of(am * TOKS, TOKS)
        await_bytes(r1.at[k, 1], t1r.at[k, 1])
        s2[k, 1, 0:16] = part[k, pl.ds(to_down, 16), :].astype(BF)
        s2[k, 1, 16:32] = (part[k, pl.ds(to_down + 16, 16), :] + r1[k, 1].astype(F32)).astype(BF)
        go(remote(s2.at[k, 1], r2.at[k, 1], t2s.at[k, 1], t2r.at[k, 1], down_a))
    mine = pl.multiple_of(a * TOKS, TOKS)
    for k in range(4):
        await_bytes(r2.at[k, 0], t2r.at[k, 0])
        await_bytes(r2.at[k, 1], t2r.at[k, 1])
        rs = part[k, pl.ds(mine, TOKS), :] + r2[k, 0].astype(F32) + r2[k, 1].astype(F32)
        if k == 0:
            u1[0] = rs[0:16].astype(BF)
            u1[1] = rs[16:32].astype(BF)
            go(remote(u1.at[0], v1.at[0], p1s.at[0], p1r.at[0], up_b))
            go(remote(u1.at[1], v1.at[1], p1s.at[1], p1r.at[1], down_b))
        elif k == 1:
            await_bytes(v1.at[0], p1r.at[0])
            u2[0, 0:16] = (rs[0:16] + v1[0].astype(F32)).astype(BF)
            u2[0, 16:32] = rs[16:32].astype(BF)
            go(remote(u2.at[0], v2.at[0], p2s.at[0], p2r.at[0], up_b))
        elif k == 2:
            await_bytes(v1.at[1], p1r.at[1])
            u2[1, 0:16] = rs[0:16].astype(BF)
            u2[1, 16:32] = (rs[16:32] + v1[1].astype(F32)).astype(BF)
            go(remote(u2.at[1], v2.at[1], p2s.at[1], p2r.at[1], down_b))
        else:
            rsum[...] = rs
    await_bytes(v2.at[0], p2r.at[0])
    await_bytes(v2.at[1], p2r.at[1])
    hidden = res[...].astype(F32) + (
        rsum[...] + v2[0].astype(F32) + v2[1].astype(F32)
    )
    rsum[...] = hidden
    inv = lax.rsqrt(jnp.mean(hidden * hidden, axis=-1, keepdims=True) + EPSILON)
    normed = (hidden * inv * ffn_gain[...][None, :]).astype(BF)

    picked = dot(sel_ref[...], normed)
    for j in range(16):
        fs[pl.ds(j, 64, stride=16), :] = picked[:, HD * j : HD * (j + 1)]
    dsend[...] = fs[...].astype(BF).reshape(N, 32, HD)

    def post(src, dst, ssem, rsem):
        def one(k, carry):
            to = lax.rem(t + k, N)
            remote(src.at[to], dst.at[t], ssem, rsem, to).start()
            return carry

        lax.fori_loop(1, N, one, 0)

    post(dsend, drecv, ds, dr)
    drecv[t] = dsend[t]
    for load in loads[7:]:
        load.wait()
    await_bytes(drecv.at[pl.ds(0, N - 1)], dr)
    fs[...] = drecv[...].reshape(1024, HD).astype(F32)
    for j in range(16):
        xs[:, HD * j : HD * (j + 1)] = fs[pl.ds(j, 64, stride=16), :].astype(BF)
    gate = dot(xs[...], wg[...], NT)
    up = dot(xs[...], wu[...], NT)
    inner = (gate / (1.0 + jnp.exp(-gate)) * up).astype(BF)
    y = dot(inner, wd[...])
    for j in range(16):
        fs[pl.ds(j, 64, stride=16), :] = y[:, HD * j : HD * (j + 1)]
    ysend[...] = fs[...].astype(BF).reshape(N, 32, HD)
    post(ysend, yrecv, ys, yr)
    yrecv[t] = ysend[t]
    await_bytes(yrecv.at[pl.ds(0, N - 1)], yr)
    fs[...] = yrecv[...].reshape(1024, HD).astype(F32)
    comb = comb_ref[...]
    comb_hi = comb.astype(BF)
    comb_lo = (comb - comb_hi.astype(F32)).astype(BF)
    for j in range(16):
        yj = fs[pl.ds(j, 64, stride=16), :].astype(BF)
        moe = dot(comb_hi, yj, TN) + dot(comb_lo, yj, TN)
        cols = slice(HD * j, HD * (j + 1))
        out_ref[:, cols] = (rsum[:, cols] + moe).astype(BF)

    for copy in sends:
        copy.wait_send()
    await_bytes(qsend.at[pl.ds(0, 15)], qs)
    await_bytes(asend.at[pl.ds(0, 15)], asem)
    await_bytes(dsend.at[pl.ds(0, N - 1)], ds)
    await_bytes(ysend.at[pl.ds(0, N - 1)], ys)


def body(
    residual_in, attn_gain, w_query, w_keyval, query_gain, key_gain, w_out, ffn_gain,
    w_gate, w_up, w_down, key_cache, value_cache, prefix_lens, accepted, accept_path,
    parents, slot_kinds, expert_ids, gate_probs,
):
    half = np.arange(HD // 2, dtype=np.float64)
    freq = np.exp(-(2.0 * half / HD) * math.log(ROPE_BASE)).astype(np.float32)
    freq = jnp.asarray(np.concatenate([freq, freq])[None, :])
    vmem = pl.BlockSpec(memory_space=pltpu.VMEM)
    smem = pl.BlockSpec(memory_space=pltpu.SMEM)
    hbm = pl.BlockSpec(memory_space=pltpu.HBM)
    dma = pltpu.SemaphoreType.DMA
    vm = pltpu.VMEM
    return pl.pallas_call(
        layer_kernel,
        out_shape=jax.ShapeDtypeStruct((TOKS, D), BF),
        in_specs=[vmem] * 6 + [smem] * 4 + [hbm] * 11,
        out_specs=vmem,
        scratch_shapes=[
            vm((TOKS, D), BF),
            vm((D, 2 * HD), BF),
            vm((HD, D), BF),
            vm((2 * HD, D), BF),
            vm((FF, D), BF),
            vm((FF, D), BF),
            vm((FF, D), BF),
            vm((CACHE, 4 * HD), BF),
            vm((CACHE, 4 * HD), BF),
            vm((8, HD), jnp.int32),
            vm((8, HD), F32),
            vm((16, TOKS, D), BF),
            vm((16, TOKS, 3 * HD), BF),
            vm((16, TOKS, 3 * HD), BF),
            vm((16, TOKS, 2 * HD), BF),
            vm((16, TOKS, 2 * HD), BF),
            vm((4, 4 * TOKS, D), F32),
            vm((4, 2, 16, D), BF),
            vm((4, 2, 16, D), BF),
            vm((4, 2, TOKS, D), BF),
            vm((4, 2, TOKS, D), BF),
            vm((2, 16, D), BF),
            vm((2, 16, D), BF),
            vm((2, TOKS, D), BF),
            vm((2, TOKS, D), BF),
            vm((TOKS, D), F32),
            vm((1024, HD), F32),
            vm((2 * N, D), BF),
            vm((N, 32, HD), BF),
            vm((N, 32, HD), BF),
            vm((N, 32, HD), BF),
            vm((N, 32, HD), BF),
            vm((2 * N, TOKS), BF),
            vm((2 * N, TOKS), F32),
            vm((TOKS, HD), F32),
            vm((TOKS, HD), F32),
            vm((TOKS, TOKS), F32),
            dma((11,)),
            dma((3,)), dma((3,)),
            dma((10,)),
            dma((2,)), dma((2,)),
            dma((4, 2)), dma((4, 2)),
            dma((10,)),
            dma(()), dma(()),
            dma(()), dma((4,)),
            dma((4, 2)), dma((4, 2)), dma((4, 2)), dma((4, 2)),
            dma((2,)), dma((2,)), dma((2,)), dma((2,)),
            dma(()), dma(()), dma(()), dma(()),
        ],
        compiler_params=pltpu.CompilerParams(
            collective_id=0, has_side_effects=True, vmem_limit_bytes=56 * 1024 * 1024
        ),
        name="layer",
    )(
        freq, attn_gain, query_gain, key_gain, ffn_gain, parents,
        prefix_lens[None], accepted[None], accept_path, slot_kinds[None],
        residual_in, w_query, w_keyval, w_out, w_gate, w_up, w_down,
        key_cache, value_cache, expert_ids.T, gate_probs.T,
    )


def solution(mesh):
    in_specs = (
        P(("group", "tensor"), None),
        P(),
        P(None, "tensor"),
        P("tensor", None),
        P(),
        P(),
        P("tensor", None),
        P(),
        P("tensor", None, None),
        P("tensor", None, None),
        P("tensor", None, None),
        P(("group", "tensor"), None, None),
        P(("group", "tensor"), None, None),
        P(("group", "tensor")),
        P(("group", "tensor")),
        P(("group", "tensor"), None),
        P(("group", "tensor"), None),
        P(("group", "tensor")),
        P("group", None),
        P("group", None),
    )
    out_specs = P(("group", "tensor"), None)
    return jax.shard_map(body, mesh=mesh, in_specs=in_specs, out_specs=out_specs, check_vma=False)
```

```python
import functools
import math

import jax
import jax.numpy as jnp
import numpy as np
from jax import lax
from jax.experimental import pallas as pl
from jax.experimental.pallas import tpu as pltpu
from jax.sharding import PartitionSpec as P

SINK = 4
WIN = 512
EPSILON = 1e-06
NEG_FILL = -1e30
ROPE_BASE = 1000000.0

N = 32
TOKS = 32
D = 2048
HD = 128
FF = 768
CACHE = 1024
SCALE = HD**-0.5
LOG2E = math.log2(math.e)

BF = jnp.bfloat16
F32 = jnp.float32
MESH = pl.DeviceIdType.MESH
FAR_FIRST = sorted(
    ((i, j) for i in range(4) for j in range(4)),
    key=lambda ij: -(min(ij[0], 4 - ij[0]) + min(ij[1], 4 - ij[1])),
)
NT = (((1,), (1,)), ((), ()))
TN = (((0,), (0,)), ((), ()))


def dot(a, b, dims=(((1,), (0,)), ((), ()))):
    return lax.dot_general(a, b, dims, preferred_element_type=F32)


def layer_kernel(
    freq_hbm, again_hbm, qgain_hbm, kgain_hbm, fgain_hbm, par_hbm, prefix_hbm, acc_hbm, path_hbm, kind_hbm,
    res_hbm, wq_hbm, wkv_hbm, wo_hbm, wg_hbm, wu_hbm, wd_hbm, kc_hbm, vc_hbm, ids_hbm, gates_hbm,
    out_ref,
    freq_ref, attn_gain, query_gain, key_gain, ffn_gain, parents, prefix, accepted, path, kind,
    res, wq, wkv, wo, wg, wu, wd, kc, vc, ids, gates,
    ag, qsend, qrecv, asend, ain,
    part, s1, r1, s2, r2, u1, v1, u2, v2, rsum,
    fs, xs, dsend, drecv, ysend, yrecv, sel_ref, comb_ref, cos_ref, sin_ref, allow_ref,
    lsem, isem, meet, wsend, wrecv, gs, ga, gh, gb, gbh, hs, qs, qr, asem, ar,
    t1s, t1r, t2s, t2r, p1s, p1r, p2s, p2r, ds, dr, ys, yr,
):
    t = lax.axis_index("tensor")
    core = lax.rem(t, 2)
    chip = t // 2
    cx = chip // 4
    cy = lax.rem(chip, 4)
    a = cx * (1 - core) + cy * core
    b = cy * (1 - core) + cx * core
    step_a = 8 - 6 * core
    step_b = 2 + 6 * core

    def dev(a_, b_):
        return a_ * step_a + b_ * step_b + core

    def ring(v, k):
        return lax.rem(v + k, 4)

    def remote(src, dst, ssem, rsem, to):
        return pltpu.make_async_remote_copy(
            src_ref=src, dst_ref=dst, send_sem=ssem, recv_sem=rsem,
            device_id={"tensor": to}, device_id_type=MESH,
        )

    def await_bytes(ref, sem):
        pltpu.make_async_copy(ref, ref, sem).wait()

    load_res = pltpu.make_async_copy(res_hbm, res, lsem.at[0])
    load_res.start()
    small = [
        pltpu.make_async_copy(src, dst, isem.at[i])
        for i, (src, dst) in enumerate(
            (
                (again_hbm, attn_gain), (freq_hbm, freq_ref), (qgain_hbm, query_gain),
                (kgain_hbm, key_gain), (fgain_hbm, ffn_gain), (par_hbm, parents),
                (prefix_hbm, prefix), (acc_hbm, accepted), (path_hbm, path), (kind_hbm, kind),
            )
        )
    ]
    small[0].start()
    wkv[...] = jnp.zeros_like(wkv)
    lane0 = pl.multiple_of(core * HD, HD)
    kv_row = pl.multiple_of(lax.rem(chip, 2) * 64 + core * 32, 32)
    lane_win = pl.multiple_of((t // 4) * HD, HD)
    loads = [
        pltpu.make_async_copy(wq_hbm, wq.at[:, pl.ds(lane0, HD)], lsem.at[1]),
        pltpu.make_async_copy(wkv_hbm, wkv.at[pl.ds(kv_row, 32)], lsem.at[2]),
        pltpu.make_async_copy(ids_hbm.at[:, pl.ds(lane_win, HD)], ids, lsem.at[3]),
        pltpu.make_async_copy(gates_hbm.at[:, pl.ds(lane_win, HD)], gates, lsem.at[4]),
        pltpu.make_async_copy(wo_hbm, wo.at[pl.ds(lane0, HD)], lsem.at[5]),
        pltpu.make_async_copy(kc_hbm.at[0], kc, lsem.at[6]),
        pltpu.make_async_copy(vc_hbm.at[0], vc, lsem.at[7]),
        pltpu.make_async_copy(wg_hbm.at[0], wg, lsem.at[8]),
        pltpu.make_async_copy(wu_hbm.at[0], wu, lsem.at[9]),
        pltpu.make_async_copy(wd_hbm.at[0], wd, lsem.at[10]),
    ]
    for load in loads[:2] + small[1:] + loads[2:]:
        load.start()

    barrier = pltpu.get_barrier_semaphore()

    sibling = t + 1 - 2 * core
    line = [dev(ring(a, k), b) for k in (1, 2, 3)] + [dev(a, ring(b, k)) for k in (1, 2, 3)]
    for to in line + [sibling]:
        pl.semaphore_signal(barrier, inc=1, device_id={"tensor": to}, device_id_type=MESH)

    load_res.wait()
    small[0].wait()
    own = b * 4 + a
    xv = res[...].astype(F32)
    inv = lax.rsqrt(jnp.mean(xv * xv, axis=-1, keepdims=True) + EPSILON)
    ag[own] = (xv * inv * attn_gain[...][None, :]).astype(BF)

    pl.semaphore_wait(barrier, 7)

    up_a, down_a = dev(ring(a, 1), b), dev(ring(a, 3), b)
    up_b, down_b = dev(a, ring(b, 1)), dev(a, ring(b, 3))

    def blk(a_, b_):
        return ag.at[b_ * 4 + a_]

    def half(a_, b_, h):
        return ag.at[b_ * 4 + a_, pl.ds(16 * h, 16)]

    sends = []

    def go(copy):
        copy.start()
        sends.append(copy)

    def spread_b(j, a_):
        go(remote(blk(a_, b), blk(a_, b), gs.at[2 + 2 * j], gb.at[j, 0], up_b))
        go(remote(blk(a_, b), blk(a_, b), gs.at[3 + 2 * j], gb.at[j, 1], down_b))

    go(remote(blk(a, b), blk(a, b), gs.at[0], ga.at[0], up_a))
    go(remote(blk(a, b), blk(a, b), gs.at[1], ga.at[1], down_a))
    spread_b(0, a)

    go(remote(wq_hbm, wq.at[:, pl.ds(lane0, HD)], wsend.at[0], wrecv.at[0], sibling))
    go(remote(wkv_hbm, wkv.at[pl.ds(kv_row, 32)], wsend.at[1], wrecv.at[1], sibling))
    go(remote(wo_hbm, wo.at[pl.ds(lane0, HD)], wsend.at[2], wrecv.at[2], sibling))

    am, ap, af = ring(a, 3), ring(a, 1), ring(a, 2)
    bm, bp, bf = ring(b, 3), ring(b, 1), ring(b, 2)

    await_bytes(blk(am, b), ga.at[0])
    go(remote(half(am, b, 0), half(am, b, 0), hs.at[0], gh.at[0], up_a))
    spread_b(1, am)
    await_bytes(blk(ap, b), ga.at[1])
    go(remote(half(ap, b, 1), half(ap, b, 1), hs.at[1], gh.at[1], down_a))
    spread_b(2, ap)

    def relay_b(j, a_):
        await_bytes(blk(a_, bm), gb.at[j, 0])
        go(remote(half(a_, bm, 0), half(a_, bm, 0), hs.at[2 + 2 * j], gbh.at[j, 0], up_b))
        await_bytes(blk(a_, bp), gb.at[j, 1])
        go(remote(half(a_, bp, 1), half(a_, bp, 1), hs.at[3 + 2 * j], gbh.at[j, 1], down_b))

    relay_b(0, a)
    await_bytes(half(af, b, 0), gh.at[0])
    await_bytes(half(af, b, 1), gh.at[1])
    spread_b(3, af)

    for load in loads[:2]:
        load.wait()
    other_lane = pl.multiple_of(HD - core * HD, HD)
    other_row = pl.multiple_of(lax.rem(chip, 2) * 64 + 32 - core * 32, 32)
    await_bytes(wq.at[:, pl.ds(other_lane, HD)], wrecv.at[0])
    await_bytes(wkv.at[pl.ds(other_row, 32)], wrecv.at[1])

    def project(b_):
        rows = ag[pl.ds(b_ * 4, 4)].reshape(4 * TOKS, D)
        q = dot(rows, wq[...])
        kv = dot(rows, wkv[...], NT)
        qsend[pl.ds(b_ * 4, 4), :, 0 : 2 * HD] = q.astype(BF).reshape(4, TOKS, 2 * HD)
        qsend[pl.ds(b_ * 4, 4), :, 2 * HD :] = kv.astype(BF).reshape(4, TOKS, HD)

    def post_queries(b_, first):
        for k in (2, 1, 3, 0)[: 4 - first]:
            a_ = ring(a, k)
            copy = remote(
                qsend.at[b_ * 4 + a_], qrecv.at[chip], qs, qr, dev(a_, b_)
            )
            copy.start()

    project(b)
    qrecv[chip] = qsend[own]
    post_queries(b, 1)

    relay_b(1, am)
    relay_b(2, ap)

    for load in loads[2:4] + small[1:]:
        load.wait()
    line = lax.broadcasted_iota(jnp.int32, (2 * N, TOKS), 0)
    expert = line // 2
    named = jnp.zeros((2 * N, TOKS), F32)
    weight = jnp.zeros((2 * N, TOKS), F32)
    turn_lanes = lax.rem(HD - lax.rem(t, 4) * TOKS, HD)
    idv = pltpu.roll(ids[...], turn_lanes, 1)[:, 0:TOKS]
    gv = pltpu.roll(gates[...], turn_lanes, 1)[:, 0:TOKS]
    for k in range(8):
        hit = jnp.broadcast_to(idv[k : k + 1], (2 * N, TOKS)) == expert
        named = jnp.where(hit, 1.0, named)
        weight = weight + jnp.where(hit, jnp.broadcast_to(gv[k : k + 1], (2 * N, TOKS)), 0.0)
    ri = lax.broadcasted_iota(jnp.int32, (TOKS, TOKS), 0)
    ci = lax.broadcasted_iota(jnp.int32, (TOKS, TOKS), 1)
    before = dot(named.astype(BF), jnp.where(ri < ci, 1.0, 0.0).astype(BF))
    turn = lax.rem(line, 2).astype(F32)
    taken = (named > 0.5) & (jnp.abs(before - turn) < 0.5)
    sel_ref[...] = jnp.where(taken, 1.0, 0.0).astype(BF)
    comb_ref[...] = jnp.where(taken, weight, 0.0)

    link = jnp.where((ri == jnp.broadcast_to(parents[...], (TOKS, TOKS))) | (ri == ci), 1.0, 0.0)
    for unused in range(5):
        link = jnp.minimum(dot(link.astype(BF), link.astype(BF)), 1.0)
    eye = jnp.where(ri == ci, 1.0, 0.0).astype(BF)
    reach = dot(link.astype(BF), eye, TN)
    is_tree = kind[0] == 1
    causal = jnp.where(ci <= ri, 1.0, 0.0)
    allowed = jnp.where(is_tree, reach, causal)
    allow_ref[...] = allowed
    depth = jnp.sum(allowed, axis=1, keepdims=True) - 1.0
    total = prefix[0] + accepted[0]
    angle = (total.astype(F32) + depth) * freq_ref[...]
    cos_ref[...] = jnp.cos(angle)
    lane_row = lax.broadcasted_iota(jnp.int32, (TOKS, HD), 1)
    sine = jnp.sin(angle)
    sin_ref[...] = jnp.where(lane_row < HD // 2, -sine, sine)

    relay_b(3, af)
    project(bm)
    post_queries(bm, 0)
    project(bp)
    post_queries(bp, 0)

    for j, a_ in enumerate((a, am, ap, af)):
        await_bytes(half(a_, bf, 0), gbh.at[j, 0])
        await_bytes(half(a_, bf, 1), gbh.at[j, 1])
    pl.semaphore_signal(meet, inc=1, device_id={"tensor": sibling}, device_id_type=MESH)
    project(bf)
    post_queries(bf, 0)

    row = lax.broadcasted_iota(jnp.int32, (1, CACHE), 1)
    seen = (row < prefix[0]) & ((row < SINK) | (row >= total - WIN))
    for m in range(8):
        seen = seen | ((row == prefix[0] + path[0, m]) & (accepted[0] > m))
    for load in loads[5:7]:
        load.wait()
    await_bytes(qrecv.at[pl.ds(0, 15)], qr)

    def rope(v, gain):
        v = v * lax.rsqrt(jnp.mean(v * v, axis=-1, keepdims=True) + EPSILON) * gain
        return (v * cos_ref[...] + pltpu.roll(v, HD // 2, 1) * sin_ref[...]).astype(BF)

    def heads(g, carry):
        qgain = query_gain[...][None, :]
        qg = jnp.concatenate(
            [
                rope(qrecv[4 * g + i, :, HD * j : HD * (j + 1)].astype(F32), qgain)
                for i in range(4)
                for j in range(2)
            ],
            axis=0,
        )
        kraw = qrecv[2 * g, :, 2 * HD :].astype(F32) + qrecv[2 * g + 1, :, 2 * HD :].astype(F32)
        knew = rope(kraw, key_gain[...][None, :])
        vnew = qrecv[8 + 2 * g, :, 2 * HD :] + qrecv[9 + 2 * g, :, 2 * HD :]
        cols = pl.ds(pl.multiple_of(g * HD, HD), HD)
        s_old = dot(qg, kc[:, cols], NT)
        s_new = dot(qg, knew, NT)
        s_old = jnp.where(jnp.broadcast_to(seen, s_old.shape), s_old, NEG_FILL)
        allow = jnp.concatenate([allow_ref[...]] * 8, axis=0)
        s_new = jnp.where(allow > 0.5, s_new, NEG_FILL)
        top = jnp.maximum(
            jnp.max(s_old, axis=-1, keepdims=True), jnp.max(s_new, axis=-1, keepdims=True)
        )
        e_old = jnp.exp2((s_old - top) * (SCALE * LOG2E))
        e_new = jnp.exp2((s_new - top) * (SCALE * LOG2E))
        denom = jnp.sum(e_old, axis=-1, keepdims=True) + jnp.sum(e_new, axis=-1, keepdims=True)
        o = dot(e_old.astype(BF), vc[:, cols]) + dot(e_new.astype(BF), vnew)
        o = (o / denom).astype(BF)
        for i in range(4):
            to = 4 * g + i
            for j in range(2):
                r0 = (2 * i + j) * TOKS
                asend[to, :, HD * j : HD * (j + 1)] = o[r0 : r0 + TOKS]

            @pl.when(to != chip)
            def _():
                remote(asend.at[to], ain.at[own], asem, ar.at[b], 2 * to + core).start()

        return carry

    lax.fori_loop(0, 4, heads, 0)
    ain[own] = asend[chip]

    loads[4].wait()
    await_bytes(wo.at[pl.ds(other_lane, HD)], wrecv.at[2])
    order = (bf, bp, bm, b)
    for k, b_ in enumerate(order):
        await_bytes(ain.at[pl.ds(b_ * 4, 3 if k == 3 else 4)], ar.at[b_])
        part[k] = dot(ain[pl.ds(b_ * 4, 4)].reshape(4 * TOKS, 2 * HD), wo[...])
        far = pl.multiple_of(af * TOKS, TOKS)
        s1[k, 0] = part[k, pl.ds(far, 16), :].astype(BF)
        go(remote(s1.at[k, 0], r1.at[k, 0], t1s.at[k, 0], t1r.at[k, 0], up_a))
        s1[k, 1] = part[k, pl.ds(far + 16, 16), :].astype(BF)
        go(remote(s1.at[k, 1], r1.at[k, 1], t1s.at[k, 1], t1r.at[k, 1], down_a))
    for k in range(4):
        to_up = pl.multiple_of(ap * TOKS, TOKS)
        await_bytes(r1.at[k, 0], t1r.at[k, 0])
        s2[k, 0, 0:16] = (part[k, pl.ds(to_up, 16), :] + r1[k, 0].astype(F32)).astype(BF)
        s2[k, 0, 16:32] = part[k, pl.ds(to_up + 16, 16), :].astype(BF)
        go(remote(s2.at[k, 0], r2.at[k, 0], t2s.at[k, 0], t2r.at[k, 0], up_a))
        to_down = pl.multiple_of(am * TOKS, TOKS)
        await_bytes(r1.at[k, 1], t1r.at[k, 1])
        s2[k, 1, 0:16] = part[k, pl.ds(to_down, 16), :].astype(BF)
        s2[k, 1, 16:32] = (part[k, pl.ds(to_down + 16, 16), :] + r1[k, 1].astype(F32)).astype(BF)
        go(remote(s2.at[k, 1], r2.at[k, 1], t2s.at[k, 1], t2r.at[k, 1], down_a))
    mine = pl.multiple_of(a * TOKS, TOKS)
    for k in range(4):
        await_bytes(r2.at[k, 0], t2r.at[k, 0])
        await_bytes(r2.at[k, 1], t2r.at[k, 1])
        rs = part[k, pl.ds(mine, TOKS), :] + r2[k, 0].astype(F32) + r2[k, 1].astype(F32)
        if k == 0:
            u1[0] = rs[0:16].astype(BF)
            u1[1] = rs[16:32].astype(BF)
            go(remote(u1.at[0], v1.at[0], p1s.at[0], p1r.at[0], up_b))
            go(remote(u1.at[1], v1.at[1], p1s.at[1], p1r.at[1], down_b))
        elif k == 1:
            await_bytes(v1.at[0], p1r.at[0])
            u2[0, 0:16] = (rs[0:16] + v1[0].astype(F32)).astype(BF)
            u2[0, 16:32] = rs[16:32].astype(BF)
            go(remote(u2.at[0], v2.at[0], p2s.at[0], p2r.at[0], up_b))
        elif k == 2:
            await_bytes(v1.at[1], p1r.at[1])
            u2[1, 0:16] = rs[0:16].astype(BF)
            u2[1, 16:32] = (rs[16:32] + v1[1].astype(F32)).astype(BF)
            go(remote(u2.at[1], v2.at[1], p2s.at[1], p2r.at[1], down_b))
        else:
            rsum[...] = rs
    await_bytes(v2.at[0], p2r.at[0])
    await_bytes(v2.at[1], p2r.at[1])
    hidden = res[...].astype(F32) + (
        rsum[...] + v2[0].astype(F32) + v2[1].astype(F32)
    )
    rsum[...] = hidden
    inv = lax.rsqrt(jnp.mean(hidden * hidden, axis=-1, keepdims=True) + EPSILON)
    normed = (hidden * inv * ffn_gain[...][None, :]).astype(BF)

    picked = dot(sel_ref[...], normed)
    for j in range(16):
        fs[pl.ds(j, 64, stride=16), :] = picked[:, HD * j : HD * (j + 1)]
    dsend[...] = fs[...].astype(BF).reshape(N, 32, HD)

    def post(src, dst, ssem, rsem):
        for da, db in FAR_FIRST:
            for other in range(2):
                if (da, db, other) == (0, 0, 0):
                    continue
                to = dev(ring(a, da), ring(b, db)) + other * (1 - 2 * core)
                remote(src.at[to], dst.at[t], ssem, rsem, to).start()

    pl.semaphore_wait(meet, 1)
    post(dsend, drecv, ds, dr)
    drecv[t] = dsend[t]
    for load in loads[7:]:
        load.wait()
    await_bytes(drecv.at[pl.ds(0, N - 1)], dr)
    fs[...] = drecv[...].reshape(1024, HD).astype(F32)
    for j in range(16):
        xs[:, HD * j : HD * (j + 1)] = fs[pl.ds(j, 64, stride=16), :].astype(BF)
    gate = dot(xs[...], wg[...], NT)
    up = dot(xs[...], wu[...], NT)
    inner = (gate / (1.0 + jnp.exp(-gate)) * up).astype(BF)
    y = dot(inner, wd[...])
    for j in range(16):
        fs[pl.ds(j, 64, stride=16), :] = y[:, HD * j : HD * (j + 1)]
    ysend[...] = fs[...].astype(BF).reshape(N, 32, HD)
    post(ysend, yrecv, ys, yr)
    yrecv[t] = ysend[t]
    await_bytes(yrecv.at[pl.ds(0, N - 1)], yr)
    fs[...] = yrecv[...].reshape(1024, HD).astype(F32)
    comb = comb_ref[...]
    comb_hi = comb.astype(BF)
    comb_lo = (comb - comb_hi.astype(F32)).astype(BF)
    for j in range(16):
        yj = fs[pl.ds(j, 64, stride=16), :].astype(BF)
        moe = dot(comb_hi, yj, TN) + dot(comb_lo, yj, TN)
        cols = slice(HD * j, HD * (j + 1))
        out_ref[:, cols] = (rsum[:, cols] + moe).astype(BF)

    for copy in sends:
        copy.wait_send()
    await_bytes(qsend.at[pl.ds(0, 15)], qs)
    await_bytes(asend.at[pl.ds(0, 15)], asem)
    await_bytes(dsend.at[pl.ds(0, N - 1)], ds)
    await_bytes(ysend.at[pl.ds(0, N - 1)], ys)


def body(
    residual_in, attn_gain, w_query, w_keyval, query_gain, key_gain, w_out, ffn_gain,
    w_gate, w_up, w_down, key_cache, value_cache, prefix_lens, accepted, accept_path,
    parents, slot_kinds, expert_ids, gate_probs,
):
    half = np.arange(HD // 2, dtype=np.float64)
    freq = np.exp(-(2.0 * half / HD) * math.log(ROPE_BASE)).astype(np.float32)
    freq = jnp.asarray(np.concatenate([freq, freq])[None, :])
    vmem = pl.BlockSpec(memory_space=pltpu.VMEM)
    sm = pltpu.SMEM
    hbm = pl.BlockSpec(memory_space=pltpu.HBM)
    dma = pltpu.SemaphoreType.DMA
    vm = pltpu.VMEM
    return pl.pallas_call(
        layer_kernel,
        out_shape=jax.ShapeDtypeStruct((TOKS, D), BF),
        in_specs=[hbm] * 21,
        out_specs=vmem,
        scratch_shapes=[
            vm((1, HD), F32),
            vm((D,), F32), vm((HD,), F32), vm((HD,), F32), vm((D,), F32),
            vm((1, TOKS), jnp.int32),
            sm((1,), jnp.int32), sm((1,), jnp.int32), sm((1, 8), jnp.int32), sm((1,), jnp.int32),
            vm((TOKS, D), BF),
            vm((D, 2 * HD), BF),
            vm((HD, D), BF),
            vm((2 * HD, D), BF),
            vm((FF, D), BF),
            vm((FF, D), BF),
            vm((FF, D), BF),
            vm((CACHE, 4 * HD), BF),
            vm((CACHE, 4 * HD), BF),
            vm((8, HD), jnp.int32),
            vm((8, HD), F32),
            vm((16, TOKS, D), BF),
            vm((16, TOKS, 3 * HD), BF),
            vm((16, TOKS, 3 * HD), BF),
            vm((16, TOKS, 2 * HD), BF),
            vm((16, TOKS, 2 * HD), BF),
            vm((4, 4 * TOKS, D), F32),
            vm((4, 2, 16, D), BF),
            vm((4, 2, 16, D), BF),
            vm((4, 2, TOKS, D), BF),
            vm((4, 2, TOKS, D), BF),
            vm((2, 16, D), BF),
            vm((2, 16, D), BF),
            vm((2, TOKS, D), BF),
            vm((2, TOKS, D), BF),
            vm((TOKS, D), F32),
            vm((1024, HD), F32),
            vm((2 * N, D), BF),
            vm((N, 32, HD), BF),
            vm((N, 32, HD), BF),
            vm((N, 32, HD), BF),
            vm((N, 32, HD), BF),
            vm((2 * N, TOKS), BF),
            vm((2 * N, TOKS), F32),
            vm((TOKS, HD), F32),
            vm((TOKS, HD), F32),
            vm((TOKS, TOKS), F32),
            dma((11,)),
            dma((10,)),
            pltpu.SemaphoreType.REGULAR,
            dma((3,)), dma((3,)),
            dma((10,)),
            dma((2,)), dma((2,)),
            dma((4, 2)), dma((4, 2)),
            dma((10,)),
            dma(()), dma(()),
            dma(()), dma((4,)),
            dma((4, 2)), dma((4, 2)), dma((4, 2)), dma((4, 2)),
            dma((2,)), dma((2,)), dma((2,)), dma((2,)),
            dma(()), dma(()), dma(()), dma(()),
        ],
        compiler_params=pltpu.CompilerParams(
            collective_id=0, has_side_effects=True, vmem_limit_bytes=56 * 1024 * 1024
        ),
        name="layer",
    )(
        freq, attn_gain, query_gain, key_gain, ffn_gain, parents,
        prefix_lens, accepted, accept_path, slot_kinds,
        residual_in, w_query, w_keyval, w_out, w_gate, w_up, w_down,
        key_cache, value_cache, expert_ids.T, gate_probs.T,
    )


def solution(mesh):
    in_specs = (
        P(("group", "tensor"), None),
        P(),
        P(None, "tensor"),
        P("tensor", None),
        P(),
        P(),
        P("tensor", None),
        P(),
        P("tensor", None, None),
        P("tensor", None, None),
        P("tensor", None, None),
        P(("group", "tensor"), None, None),
        P(("group", "tensor"), None, None),
        P(("group", "tensor")),
        P(("group", "tensor")),
        P(("group", "tensor"), None),
        P(("group", "tensor"), None),
        P(("group", "tensor")),
        P("group", None),
        P("group", None),
    )
    out_specs = P(("group", "tensor"), None)
    return jax.shard_map(body, mesh=mesh, in_specs=in_specs, out_specs=out_specs, check_vma=False)
```

```python
import functools
import math

import jax
import jax.numpy as jnp
import numpy as np
from jax import lax
from jax.experimental import pallas as pl
from jax.experimental.pallas import tpu as pltpu
from jax.sharding import PartitionSpec as P

SINK = 4
WIN = 512
EPSILON = 1e-06
NEG_FILL = -1e30
ROPE_BASE = 1000000.0

N = 32
TOKS = 32
HT = 16
D = 2048
HD = 128
FF = 768
CACHE = 1024
SCALE = HD**-0.5
LOG2E = math.log2(math.e)

BF = jnp.bfloat16
F32 = jnp.float32
MESH = pl.DeviceIdType.MESH
FAR_FIRST = sorted(
    ((i, j) for i in range(4) for j in range(4)),
    key=lambda ij: -(min(ij[0], 4 - ij[0]) + min(ij[1], 4 - ij[1])),
)
NT = (((1,), (1,)), ((), ()))
TN = (((0,), (0,)), ((), ()))


def dot(a, b, dims=(((1,), (0,)), ((), ()))):
    return lax.dot_general(a, b, dims, preferred_element_type=F32)


def layer_kernel(
    freq_hbm, again_hbm, qgain_hbm, kgain_hbm, fgain_hbm, par_hbm, prefix_hbm, acc_hbm, path_hbm, kind_hbm,
    res_hbm, wq_hbm, wkv_hbm, wo_hbm, wg_hbm, wu_hbm, wd_hbm, kc_hbm, vc_hbm, ids_hbm, gates_hbm,
    out_ref,
    freq_ref, attn_gain, query_gain, key_gain, ffn_gain, parents, prefix, accepted, path, kind,
    res, wq, wkv, wo, wg, wu, wd, kc, vc, ids, gates,
    ag, qsend, qrecv, knew, vnew, asend, ain,
    part, s1, r1, s2, r2, u1, v1, u2, v2, rown, hid, nffn,
    fs, xs, dsend, drecv, ysend, yrecv, sel_ref, comb_ref, cos_ref, sin_ref, allow_ref, seen_ref,
    lsem, isem, meet, snd, rcv, qs, qr, asem, ar, ds, dr, ys, yr,
):
    t = lax.axis_index("tensor")
    core = lax.rem(t, 2)
    chip = t // 2
    cx = chip // 4
    cy = lax.rem(chip, 4)
    a = cx * (1 - core) + cy * core
    b = cy * (1 - core) + cx * core
    step_a = 8 - 6 * core
    step_b = 2 + 6 * core

    def dev(a_, b_):
        return a_ * step_a + b_ * step_b + core

    def ring(v, k):
        return lax.rem(v + k, 4)

    def remote(src, dst, ssem, rsem, to):
        return pltpu.make_async_remote_copy(
            src_ref=src, dst_ref=dst, send_sem=ssem, recv_sem=rsem,
            device_id={"tensor": to}, device_id_type=MESH,
        )

    def await_bytes(ref, sem):
        pltpu.make_async_copy(ref, ref, sem).wait()

    sends = []
    slots = {}

    def slot(key):
        return slots.setdefault(key, len(slots))

    def go(key, src, dst, to):
        copy = remote(src, dst, snd.at[len(sends)], rcv.at[slot(key)], to)
        copy.start()
        sends.append(copy)

    def come(key, ref):
        await_bytes(ref, rcv.at[slot(key)])

    load_res = pltpu.make_async_copy(res_hbm, res, lsem.at[0])
    load_res.start()
    small = [
        pltpu.make_async_copy(src, dst, isem.at[i])
        for i, (src, dst) in enumerate(
            (
                (again_hbm, attn_gain), (freq_hbm, freq_ref), (qgain_hbm, query_gain),
                (kgain_hbm, key_gain), (fgain_hbm, ffn_gain), (par_hbm, parents),
                (prefix_hbm, prefix), (acc_hbm, accepted), (path_hbm, path), (kind_hbm, kind),
            )
        )
    ]
    small[0].start()

    barrier = pltpu.get_barrier_semaphore()
    sibling = t + 1 - 2 * core
    wkv[...] = jnp.zeros_like(wkv)
    line = [dev(ring(a, k), b) for k in (1, 2, 3)] + [dev(a, ring(b, k)) for k in (1, 2, 3)]
    for to in line + [sibling]:
        pl.semaphore_signal(barrier, inc=1, device_id={"tensor": to}, device_id_type=MESH)

    lane0 = pl.multiple_of(core * HD, HD)
    kv_row = pl.multiple_of(lax.rem(chip, 2) * 64 + core * 32, 32)
    lane_win = pl.multiple_of((t // 4) * HD, HD)
    loads = [
        pltpu.make_async_copy(wq_hbm, wq.at[:, pl.ds(lane0, HD)], lsem.at[1]),
        pltpu.make_async_copy(wkv_hbm, wkv.at[pl.ds(kv_row, 32)], lsem.at[2]),
        pltpu.make_async_copy(ids_hbm.at[:, pl.ds(lane_win, HD)], ids, lsem.at[3]),
        pltpu.make_async_copy(gates_hbm.at[:, pl.ds(lane_win, HD)], gates, lsem.at[4]),
        pltpu.make_async_copy(wo_hbm, wo.at[pl.ds(lane0, HD)], lsem.at[5]),
        pltpu.make_async_copy(kc_hbm.at[0], kc, lsem.at[6]),
        pltpu.make_async_copy(vc_hbm.at[0], vc, lsem.at[7]),
        pltpu.make_async_copy(wg_hbm.at[0], wg, lsem.at[8]),
        pltpu.make_async_copy(wu_hbm.at[0], wu, lsem.at[9]),
        pltpu.make_async_copy(wd_hbm.at[0], wd, lsem.at[10]),
    ]
    for load in small[1:] + loads[2:4] + loads[:2] + loads[4:]:
        load.start()

    load_res.wait()
    small[0].wait()
    own = b * 4 + a
    xv = res[...].astype(F32)
    inv = lax.rsqrt(jnp.mean(xv * xv, axis=-1, keepdims=True) + EPSILON)
    normed = (xv * inv * attn_gain[...][None, :]).astype(BF)
    for h in range(2):
        ag[h, own] = normed[HT * h : HT * (h + 1)]

    for load in loads[2:4] + small[1:]:
        load.wait()
    line_no = lax.broadcasted_iota(jnp.int32, (2 * N, TOKS), 0)
    expert = line_no // 2
    named = jnp.zeros((2 * N, TOKS), F32)
    weight = jnp.zeros((2 * N, TOKS), F32)
    turn_lanes = lax.rem(HD - lax.rem(t, 4) * TOKS, HD)
    idv = pltpu.roll(ids[...], turn_lanes, 1)[:, 0:TOKS]
    gv = pltpu.roll(gates[...], turn_lanes, 1)[:, 0:TOKS]
    for k in range(8):
        hit = jnp.broadcast_to(idv[k : k + 1], (2 * N, TOKS)) == expert
        named = jnp.where(hit, 1.0, named)
        weight = weight + jnp.where(hit, jnp.broadcast_to(gv[k : k + 1], (2 * N, TOKS)), 0.0)
    ri = lax.broadcasted_iota(jnp.int32, (TOKS, TOKS), 0)
    ci = lax.broadcasted_iota(jnp.int32, (TOKS, TOKS), 1)
    before = dot(named.astype(BF), jnp.where(ri < ci, 1.0, 0.0).astype(BF))
    turn = lax.rem(line_no, 2).astype(F32)
    taken = (named > 0.5) & (jnp.abs(before - turn) < 0.5)
    sel_ref[...] = jnp.where(taken, 1.0, 0.0).astype(BF)
    comb_ref[...] = jnp.where(taken, weight, 0.0)

    link = jnp.where((ri == jnp.broadcast_to(parents[...], (TOKS, TOKS))) | (ri == ci), 1.0, 0.0)
    for unused in range(5):
        link = jnp.minimum(dot(link.astype(BF), link.astype(BF)), 1.0)
    eye = jnp.where(ri == ci, 1.0, 0.0).astype(BF)
    reach = dot(link.astype(BF), eye, TN)
    is_tree = kind[0] == 1
    causal = jnp.where(ci <= ri, 1.0, 0.0)
    allowed = jnp.where(is_tree, reach, causal)
    allow_ref[...] = allowed
    depth = jnp.sum(allowed, axis=1, keepdims=True) - 1.0
    total = prefix[0] + accepted[0]
    angle = (total.astype(F32) + depth) * freq_ref[...]
    cos_ref[...] = jnp.cos(angle)
    lane_row = lax.broadcasted_iota(jnp.int32, (TOKS, HD), 1)
    sine = jnp.sin(angle)
    sin_ref[...] = jnp.where(lane_row < HD // 2, -sine, sine)
    row = lax.broadcasted_iota(jnp.int32, (1, CACHE), 1)
    seen = (row < prefix[0]) & ((row < SINK) | (row >= total - WIN))
    for m in range(8):
        seen = seen | ((row == prefix[0] + path[0, m]) & (accepted[0] > m))
    seen_ref[...] = jnp.where(seen, 1.0, 0.0)

    pl.semaphore_wait(barrier, 7)

    up_a, down_a = dev(ring(a, 1), b), dev(ring(a, 3), b)
    up_b, down_b = dev(a, ring(b, 1)), dev(a, ring(b, 3))
    am, ap, af = ring(a, 3), ring(a, 1), ring(a, 2)
    bm, bp, bf = ring(b, 3), ring(b, 1), ring(b, 2)
    lo, hi = pl.ds(0, D // 2), pl.ds(D // 2, D // 2)

    def blk(h, a_, b_):
        return ag.at[h, b_ * 4 + a_]

    def side(h, a_, b_, cols):
        return ag.at[h, b_ * 4 + a_, :, cols]

    def start_a(h):
        go(("a", h, 0), blk(h, a, b), blk(h, a, b), up_a)
        go(("a", h, 1), blk(h, a, b), blk(h, a, b), down_a)

    def spread_b(h, j, a_):
        go(("b", h, j, 0), blk(h, a_, b), blk(h, a_, b), up_b)
        go(("b", h, j, 1), blk(h, a_, b), blk(h, a_, b), down_b)

    def relay_a(h):
        come(("a", h, 0), blk(h, am, b))
        go(("ah", h, 0), side(h, am, b, lo), side(h, am, b, lo), up_a)
        spread_b(h, 1, am)
        come(("a", h, 1), blk(h, ap, b))
        go(("ah", h, 1), side(h, ap, b, hi), side(h, ap, b, hi), down_a)
        spread_b(h, 2, ap)

    def far_a(h):
        come(("ah", h, 0), side(h, af, b, lo))
        come(("ah", h, 1), side(h, af, b, hi))
        spread_b(h, 3, af)

    def relay_b(h, j, a_):
        come(("b", h, j, 0), blk(h, a_, bm))
        go(("bh", h, j, 0), side(h, a_, bm, lo), side(h, a_, bm, lo), up_b)
        come(("b", h, j, 1), blk(h, a_, bp))
        go(("bh", h, j, 1), side(h, a_, bp, hi), side(h, a_, bp, hi), down_b)

    def far_b(h):
        for j, a_ in enumerate((a, am, ap, af)):
            come(("bh", h, j, 0), side(h, a_, bf, lo))
            come(("bh", h, j, 1), side(h, a_, bf, hi))

    def project(h, groups):
        rows = jnp.concatenate(
            [ag[h, pl.ds(b_ * 4, 4)].reshape(4 * HT, D) for b_ in groups], axis=0
        )
        q = dot(rows, wq[...]).astype(BF)
        kv = dot(rows, wkv[...], NT).astype(BF)
        for i, b_ in enumerate(groups):
            r = slice(4 * HT * i, 4 * HT * (i + 1))
            qsend[h, pl.ds(b_ * 4, 4), :, 0 : 2 * HD] = q[r].reshape(4, HT, 2 * HD)
            qsend[h, pl.ds(b_ * 4, 4), :, 2 * HD :] = kv[r].reshape(4, HT, HD)

    def post_queries(h, b_, steps=(2, 1, 3, 0)):
        for k in steps:
            a_ = ring(a, k)
            remote(
                qsend.at[h, b_ * 4 + a_], qrecv.at[h, chip], qs.at[h], qr.at[h], dev(a_, b_)
            ).start()

    def project_own(h):
        project(h, (b,))
        qrecv[h, chip] = qsend[h, own]
        post_queries(h, b, (2, 1, 3))

    def project_near(h):
        project(h, (bm, bp))
        post_queries(h, bm)
        post_queries(h, bp)

    def project_far(h):
        project(h, (bf,))
        post_queries(h, bf)

    start_a(0)
    spread_b(0, 0, a)
    start_a(1)
    spread_b(1, 0, a)
    go("wq", wq_hbm, wq.at[:, pl.ds(lane0, HD)], sibling)
    go("wkv", wkv_hbm, wkv.at[pl.ds(kv_row, 32)], sibling)
    go("wo", wo_hbm, wo.at[pl.ds(lane0, HD)], sibling)
    other_lane = pl.multiple_of(HD - core * HD, HD)
    other_row = pl.multiple_of(lax.rem(chip, 2) * 64 + 32 - core * 32, 32)

    relay_a(0)
    relay_b(0, 0, a)
    relay_a(1)
    far_a(0)
    relay_b(1, 0, a)
    for load in loads[:2]:
        load.wait()
    come("wq", wq.at[:, pl.ds(other_lane, HD)])
    come("wkv", wkv.at[pl.ds(other_row, 32)])
    project_own(0)
    relay_b(0, 1, am)
    far_a(1)
    relay_b(0, 2, ap)
    relay_b(0, 3, af)
    project_near(0)
    relay_b(1, 1, am)
    far_b(0)
    project_far(0)
    relay_b(1, 2, ap)
    relay_b(1, 3, af)
    project_own(1)
    project_near(1)
    far_b(1)
    pl.semaphore_signal(meet, inc=1, device_id={"tensor": sibling}, device_id_type=MESH)
    project_far(1)

    for load in loads[5:7]:
        load.wait()

    def attend(h):
        await_bytes(qrecv.at[h, pl.ds(0, 15)], qr.at[h])
        mine = slice(HT * h, HT * (h + 1))
        count = HT * (h + 1)
        cosv, sinv = cos_ref[mine], sin_ref[mine]

        def rope(v, gain):
            v = v * lax.rsqrt(jnp.mean(v * v, axis=-1, keepdims=True) + EPSILON) * gain
            return (v * cosv + pltpu.roll(v, HD // 2, 1) * sinv).astype(BF)

        def heads(g, carry):
            qgain = query_gain[...][None, :]
            qg = jnp.concatenate(
                [
                    rope(qrecv[h, 4 * g + i, :, HD * j : HD * (j + 1)].astype(F32), qgain)
                    for i in range(4)
                    for j in range(2)
                ],
                axis=0,
            )
            kraw = qrecv[h, 2 * g, :, 2 * HD :].astype(F32) + qrecv[h, 2 * g + 1, :, 2 * HD :].astype(F32)
            knew[g, mine] = rope(kraw, key_gain[...][None, :])
            vnew[g, mine] = qrecv[h, 8 + 2 * g, :, 2 * HD :] + qrecv[h, 9 + 2 * g, :, 2 * HD :]
            cols = pl.ds(pl.multiple_of(g * HD, HD), HD)
            s_old = dot(qg, kc[:, cols], NT)
            s_new = dot(qg, knew[g, 0:count], NT)
            s_old = jnp.where(jnp.broadcast_to(seen_ref[...], s_old.shape) > 0.5, s_old, NEG_FILL)
            allow = jnp.concatenate([allow_ref[mine, 0:count]] * 8, axis=0)
            s_new = jnp.where(allow > 0.5, s_new, NEG_FILL)
            top = jnp.maximum(
                jnp.max(s_old, axis=-1, keepdims=True), jnp.max(s_new, axis=-1, keepdims=True)
            )
            e_old = jnp.exp2((s_old - top) * (SCALE * LOG2E))
            e_new = jnp.exp2((s_new - top) * (SCALE * LOG2E))
            denom = jnp.sum(e_old, axis=-1, keepdims=True) + jnp.sum(e_new, axis=-1, keepdims=True)
            o = dot(e_old.astype(BF), vc[:, cols]) + dot(e_new.astype(BF), vnew[g, 0:count])
            o = (o / denom).astype(BF)
            for i in range(4):
                to = 4 * g + i
                for j in range(2):
                    r0 = (2 * i + j) * HT
                    asend[h, to, :, HD * j : HD * (j + 1)] = o[r0 : r0 + HT]

                @pl.when(to != chip)
                def _():
                    remote(
                        asend.at[h, to], ain.at[h, own], asem.at[h], ar.at[h, b], 2 * to + core
                    ).start()

            return carry

        lax.fori_loop(0, 4, heads, 0)
        ain[h, own] = asend[h, chip]

    order = (bf, bp, bm, b)
    left, right = slice(0, D // 2), slice(D // 2, D)

    def piece(h, k, a_):
        return part[h, k, pl.ds(pl.multiple_of(a_ * HT, HT), HT), :]

    def sum_first(h):
        for k, b_ in enumerate(order):
            await_bytes(ain.at[h, pl.ds(b_ * 4, 3 if k == 3 else 4)], ar.at[h, b_])
            part[h, k] = dot(ain[h, pl.ds(b_ * 4, 4)].reshape(4 * HT, 2 * HD), wo[...])
            far = piece(h, k, af).astype(BF)
            s1[h, k, 0] = far[:, left]
            go(("s", h, k, 0), s1.at[h, k, 0], r1.at[h, k, 0], up_a)
            s1[h, k, 1] = far[:, right]
            go(("s", h, k, 1), s1.at[h, k, 1], r1.at[h, k, 1], down_a)

    def sum_second(h):
        for k in range(4):
            come(("s", h, k, 0), r1.at[h, k, 0])
            to_up = piece(h, k, ap)
            s2[h, k, 0, :, left] = (to_up[:, left] + r1[h, k, 0].astype(F32)).astype(BF)
            s2[h, k, 0, :, right] = to_up[:, right].astype(BF)
            go(("t", h, k, 0), s2.at[h, k, 0], r2.at[h, k, 0], up_a)
            come(("s", h, k, 1), r1.at[h, k, 1])
            to_down = piece(h, k, am)
            s2[h, k, 1, :, left] = to_down[:, left].astype(BF)
            s2[h, k, 1, :, right] = (to_down[:, right] + r1[h, k, 1].astype(F32)).astype(BF)
            go(("t", h, k, 1), s2.at[h, k, 1], r2.at[h, k, 1], down_a)

    def sum_third(h):
        for k in range(4):
            come(("t", h, k, 0), r2.at[h, k, 0])
            come(("t", h, k, 1), r2.at[h, k, 1])
            rs = piece(h, k, a) + r2[h, k, 0].astype(F32) + r2[h, k, 1].astype(F32)
            if k == 0:
                u1[h, 0] = rs[:, left].astype(BF)
                u1[h, 1] = rs[:, right].astype(BF)
                go(("u", h, 0), u1.at[h, 0], v1.at[h, 0], up_b)
                go(("u", h, 1), u1.at[h, 1], v1.at[h, 1], down_b)
            elif k == 1:
                come(("u", h, 0), v1.at[h, 0])
                u2[h, 0, :, left] = (rs[:, left] + v1[h, 0].astype(F32)).astype(BF)
                u2[h, 0, :, right] = rs[:, right].astype(BF)
                go(("v", h, 0), u2.at[h, 0], v2.at[h, 0], up_b)
            elif k == 2:
                come(("u", h, 1), v1.at[h, 1])
                u2[h, 1, :, left] = rs[:, left].astype(BF)
                u2[h, 1, :, right] = (rs[:, right] + v1[h, 1].astype(F32)).astype(BF)
                go(("v", h, 1), u2.at[h, 1], v2.at[h, 1], down_b)
            else:
                rown[h] = rs

    def finish(h):
        mine = slice(HT * h, HT * (h + 1))
        come(("v", h, 0), v2.at[h, 0])
        come(("v", h, 1), v2.at[h, 1])
        hidden = res[mine].astype(F32) + (
            rown[h] + v2[h, 0].astype(F32) + v2[h, 1].astype(F32)
        )
        hid[mine] = hidden
        scale = lax.rsqrt(jnp.mean(hidden * hidden, axis=-1, keepdims=True) + EPSILON)
        nffn[mine] = (hidden * scale * ffn_gain[...][None, :]).astype(BF)

    attend(0)
    loads[4].wait()
    come("wo", wo.at[pl.ds(other_lane, HD)])
    sum_first(0)
    attend(1)
    sum_second(0)
    sum_first(1)
    sum_third(0)
    sum_second(1)
    finish(0)
    sum_third(1)
    finish(1)

    picked = dot(sel_ref[...], nffn[...])
    for j in range(16):
        fs[pl.ds(j, 64, stride=16), :] = picked[:, HD * j : HD * (j + 1)]
    dsend[...] = fs[...].astype(BF).reshape(N, 32, HD)

    def post(src, dst, ssem, rsem):
        for da, db in FAR_FIRST:
            for other in range(2):
                if (da, db, other) == (0, 0, 0):
                    continue
                to = dev(ring(a, da), ring(b, db)) + other * (1 - 2 * core)
                remote(src.at[to], dst.at[t], ssem, rsem, to).start()

    pl.semaphore_wait(meet, 1)
    post(dsend, drecv, ds, dr)
    drecv[t] = dsend[t]
    for load in loads[7:]:
        load.wait()
    await_bytes(drecv.at[pl.ds(0, N - 1)], dr)
    fs[...] = drecv[...].reshape(1024, HD).astype(F32)
    for j in range(16):
        xs[:, HD * j : HD * (j + 1)] = fs[pl.ds(j, 64, stride=16), :].astype(BF)
    gate = dot(xs[...], wg[...], NT)
    up = dot(xs[...], wu[...], NT)
    inner = (gate / (1.0 + jnp.exp(-gate)) * up).astype(BF)
    y = dot(inner, wd[...])
    for j in range(16):
        fs[pl.ds(j, 64, stride=16), :] = y[:, HD * j : HD * (j + 1)]
    ysend[...] = fs[...].astype(BF).reshape(N, 32, HD)
    post(ysend, yrecv, ys, yr)
    yrecv[t] = ysend[t]
    await_bytes(yrecv.at[pl.ds(0, N - 1)], yr)
    fs[...] = yrecv[...].reshape(1024, HD).astype(F32)
    comb = comb_ref[...]
    comb_hi = comb.astype(BF)
    comb_lo = (comb - comb_hi.astype(F32)).astype(BF)
    for j in range(16):
        yj = fs[pl.ds(j, 64, stride=16), :].astype(BF)
        moe = dot(comb_hi, yj, TN) + dot(comb_lo, yj, TN)
        cols = slice(HD * j, HD * (j + 1))
        out_ref[:, cols] = (hid[:, cols] + moe).astype(BF)

    for copy in sends:
        copy.wait_send()
    for h in range(2):
        await_bytes(qsend.at[h, pl.ds(0, 15)], qs.at[h])
        await_bytes(asend.at[h, pl.ds(0, 15)], asem.at[h])
    await_bytes(dsend.at[pl.ds(0, N - 1)], ds)
    await_bytes(ysend.at[pl.ds(0, N - 1)], ys)


def body(
    residual_in, attn_gain, w_query, w_keyval, query_gain, key_gain, w_out, ffn_gain,
    w_gate, w_up, w_down, key_cache, value_cache, prefix_lens, accepted, accept_path,
    parents, slot_kinds, expert_ids, gate_probs,
):
    half = np.arange(HD // 2, dtype=np.float64)
    freq = np.exp(-(2.0 * half / HD) * math.log(ROPE_BASE)).astype(np.float32)
    freq = jnp.asarray(np.concatenate([freq, freq])[None, :])
    vmem = pl.BlockSpec(memory_space=pltpu.VMEM)
    sm = pltpu.SMEM
    hbm = pl.BlockSpec(memory_space=pltpu.HBM)
    dma = pltpu.SemaphoreType.DMA
    vm = pltpu.VMEM
    return pl.pallas_call(
        layer_kernel,
        out_shape=jax.ShapeDtypeStruct((TOKS, D), BF),
        in_specs=[hbm] * 21,
        out_specs=vmem,
        scratch_shapes=[
            vm((1, HD), F32),
            vm((D,), F32), vm((HD,), F32), vm((HD,), F32), vm((D,), F32),
            vm((1, TOKS), jnp.int32),
            sm((1,), jnp.int32), sm((1,), jnp.int32), sm((1, 8), jnp.int32), sm((1,), jnp.int32),
            vm((TOKS, D), BF),
            vm((D, 2 * HD), BF),
            vm((HD, D), BF),
            vm((2 * HD, D), BF),
            vm((FF, D), BF),
            vm((FF, D), BF),
            vm((FF, D), BF),
            vm((CACHE, 4 * HD), BF),
            vm((CACHE, 4 * HD), BF),
            vm((8, HD), jnp.int32),
            vm((8, HD), F32),
            vm((2, 16, HT, D), BF),
            vm((2, 16, HT, 3 * HD), BF),
            vm((2, 16, HT, 3 * HD), BF),
            vm((4, TOKS, HD), BF),
            vm((4, TOKS, HD), BF),
            vm((2, 16, HT, 2 * HD), BF),
            vm((2, 16, HT, 2 * HD), BF),
            vm((2, 4, 4 * HT, D), F32),
            vm((2, 4, 2, HT, D // 2), BF),
            vm((2, 4, 2, HT, D // 2), BF),
            vm((2, 4, 2, HT, D), BF),
            vm((2, 4, 2, HT, D), BF),
            vm((2, 2, HT, D // 2), BF),
            vm((2, 2, HT, D // 2), BF),
            vm((2, 2, HT, D), BF),
            vm((2, 2, HT, D), BF),
            vm((2, HT, D), F32),
            vm((TOKS, D), F32),
            vm((TOKS, D), BF),
            vm((1024, HD), F32),
            vm((2 * N, D), BF),
            vm((N, 32, HD), BF),
            vm((N, 32, HD), BF),
            vm((N, 32, HD), BF),
            vm((N, 32, HD), BF),
            vm((2 * N, TOKS), BF),
            vm((2 * N, TOKS), F32),
            vm((TOKS, HD), F32),
            vm((TOKS, HD), F32),
            vm((TOKS, TOKS), F32),
            vm((1, CACHE), F32),
            dma((11,)),
            dma((10,)),
            pltpu.SemaphoreType.REGULAR,
            dma((83,)), dma((83,)),
            dma((2,)), dma((2,)),
            dma((2,)), dma((2, 4)),
            dma(()), dma(()), dma(()), dma(()),
        ],
        compiler_params=pltpu.CompilerParams(
            collective_id=0, has_side_effects=True, vmem_limit_bytes=56 * 1024 * 1024
        ),
        name="layer",
    )(
        freq, attn_gain, query_gain, key_gain, ffn_gain, parents,
        prefix_lens, accepted, accept_path, slot_kinds,
        residual_in, w_query, w_keyval, w_out, w_gate, w_up, w_down,
        key_cache, value_cache, expert_ids.T, gate_probs.T,
    )


def solution(mesh):
    in_specs = (
        P(("group", "tensor"), None),
        P(),
        P(None, "tensor"),
        P("tensor", None),
        P(),
        P(),
        P("tensor", None),
        P(),
        P("tensor", None, None),
        P("tensor", None, None),
        P("tensor", None, None),
        P(("group", "tensor"), None, None),
        P(("group", "tensor"), None, None),
        P(("group", "tensor")),
        P(("group", "tensor")),
        P(("group", "tensor"), None),
        P(("group", "tensor"), None),
        P(("group", "tensor")),
        P("group", None),
        P("group", None),
    )
    out_specs = P(("group", "tensor"), None)
    return jax.shard_map(body, mesh=mesh, in_specs=in_specs, out_specs=out_specs, check_vma=False)
```

```python
import functools
import math

import jax
import jax.numpy as jnp
import numpy as np
from jax import lax
from jax.experimental import pallas as pl
from jax.experimental.pallas import tpu as pltpu
from jax.sharding import PartitionSpec as P

SINK = 4
WIN = 512
EPSILON = 1e-06
NEG_FILL = -1e30
ROPE_BASE = 1000000.0

N = 32
TOKS = 32
D = 2048
HD = 128
FF = 768
CACHE = 1024
SCALE = HD**-0.5
LOG2E = math.log2(math.e)

BF = jnp.bfloat16
F32 = jnp.float32
MESH = pl.DeviceIdType.MESH
FAR_FIRST = sorted(
    ((i, j) for i in range(4) for j in range(4)),
    key=lambda ij: -(min(ij[0], 4 - ij[0]) + min(ij[1], 4 - ij[1])),
)
NT = (((1,), (1,)), ((), ()))
TN = (((0,), (0,)), ((), ()))


def dot(a, b, dims=(((1,), (0,)), ((), ()))):
    return lax.dot_general(a, b, dims, preferred_element_type=F32)


def layer_kernel(
    freq_hbm, again_hbm, qgain_hbm, kgain_hbm, fgain_hbm, par_hbm, prefix_hbm, acc_hbm, path_hbm, kind_hbm,
    res_hbm, wq_hbm, wkv_hbm, wo_hbm, wg_hbm, wu_hbm, wd_hbm, kc_hbm, vc_hbm, ids_hbm, gates_hbm,
    out_ref,
    freq_ref, attn_gain, query_gain, key_gain, ffn_gain, parents, prefix, accepted, path, kind,
    res, wq, wkv, wo, wg, wu, wd, kc, vc, ids, gates,
    ag, qsend, qrecv, asend, ain,
    pup, pdown, pown, s1, r1, s2, r2, v1, v2, hid,
    fs, xs, dsend, drecv, ysend, yrecv, sel_ref, comb_ref, link_ref,
    qcos, qsin, kcos, ksin, allow_ref, seen_ref,
    lsem, isem, meet, snd, rcv, qs, qr, asem, ar, ds, dr, ys, yr,
):
    t = lax.axis_index("tensor")
    core = lax.rem(t, 2)
    chip = t // 2
    cx = chip // 4
    cy = lax.rem(chip, 4)
    a = cx * (1 - core) + cy * core
    b = cy * (1 - core) + cx * core
    step_a = 8 - 6 * core
    step_b = 2 + 6 * core

    def dev(a_, b_):
        return a_ * step_a + b_ * step_b + core

    def ring(v, k):
        return lax.rem(v + k, 4)

    def remote(src, dst, ssem, rsem, to):
        return pltpu.make_async_remote_copy(
            src_ref=src, dst_ref=dst, send_sem=ssem, recv_sem=rsem,
            device_id={"tensor": to}, device_id_type=MESH,
        )

    def await_bytes(ref, sem):
        pltpu.make_async_copy(ref, ref, sem).wait()

    sends = []
    slots = {}

    def slot(key):
        return slots.setdefault(key, len(slots))

    def go(key, src, dst, to):
        copy = remote(src, dst, snd.at[len(sends)], rcv.at[slot(key)], to)
        copy.start()
        sends.append(copy)

    def come(key, ref):
        await_bytes(ref, rcv.at[slot(key)])

    load_res = pltpu.make_async_copy(res_hbm, res, lsem.at[0])
    load_res.start()
    small = [
        pltpu.make_async_copy(src, dst, isem.at[i])
        for i, (src, dst) in enumerate(
            (
                (again_hbm, attn_gain), (freq_hbm, freq_ref), (qgain_hbm, query_gain),
                (kgain_hbm, key_gain), (fgain_hbm, ffn_gain), (par_hbm, parents),
                (prefix_hbm, prefix), (acc_hbm, accepted), (path_hbm, path), (kind_hbm, kind),
            )
        )
    ]
    small[0].start()
    wkv[...] = jnp.zeros_like(wkv)
    lane0 = pl.multiple_of(core * HD, HD)
    kv_row = pl.multiple_of(lax.rem(chip, 2) * 64 + core * 32, 32)
    lane_win = pl.multiple_of((t // 4) * HD, HD)
    loads = [
        pltpu.make_async_copy(wq_hbm, wq.at[:, pl.ds(lane0, HD)], lsem.at[1]),
        pltpu.make_async_copy(wkv_hbm, wkv.at[pl.ds(kv_row, 32)], lsem.at[2]),
        pltpu.make_async_copy(ids_hbm.at[:, pl.ds(lane_win, HD)], ids, lsem.at[3]),
        pltpu.make_async_copy(gates_hbm.at[:, pl.ds(lane_win, HD)], gates, lsem.at[4]),
        pltpu.make_async_copy(wo_hbm, wo.at[pl.ds(lane0, HD)], lsem.at[5]),
        pltpu.make_async_copy(kc_hbm.at[0], kc, lsem.at[6]),
        pltpu.make_async_copy(vc_hbm.at[0], vc, lsem.at[7]),
        pltpu.make_async_copy(wg_hbm.at[0], wg, lsem.at[8]),
        pltpu.make_async_copy(wu_hbm.at[0], wu, lsem.at[9]),
        pltpu.make_async_copy(wd_hbm.at[0], wd, lsem.at[10]),
    ]
    for load in loads[2:4] + small[1:] + loads[:2] + loads[4:]:
        load.start()

    barrier = pltpu.get_barrier_semaphore()

    sibling = t + 1 - 2 * core
    line = [dev(ring(a, k), b) for k in (1, 2, 3)] + [dev(a, ring(b, k)) for k in (1, 2, 3)]
    for to in line + [sibling]:
        pl.semaphore_signal(barrier, inc=1, device_id={"tensor": to}, device_id_type=MESH)

    load_res.wait()
    small[0].wait()
    own = b * 4 + a
    xv = res[...].astype(F32)
    inv = lax.rsqrt(jnp.mean(xv * xv, axis=-1, keepdims=True) + EPSILON)
    ag[own] = (xv * inv * attn_gain[...][None, :]).astype(BF)

    for load in loads[2:4] + small[1:]:
        load.wait()
    line = lax.broadcasted_iota(jnp.int32, (2 * N, TOKS), 0)
    expert = line // 2
    named = jnp.zeros((2 * N, TOKS), F32)
    weight = jnp.zeros((2 * N, TOKS), F32)
    turn_lanes = lax.rem(HD - lax.rem(t, 4) * TOKS, HD)
    idv = pltpu.roll(ids[...], turn_lanes, 1)[:, 0:TOKS]
    gv = pltpu.roll(gates[...], turn_lanes, 1)[:, 0:TOKS]
    for k in range(8):
        hit = jnp.broadcast_to(idv[k : k + 1], (2 * N, TOKS)) == expert
        named = jnp.where(hit, 1.0, named)
        weight = weight + jnp.where(hit, jnp.broadcast_to(gv[k : k + 1], (2 * N, TOKS)), 0.0)
    ri = lax.broadcasted_iota(jnp.int32, (TOKS, TOKS), 0)
    ci = lax.broadcasted_iota(jnp.int32, (TOKS, TOKS), 1)
    before = dot(named.astype(BF), jnp.where(ri < ci, 1.0, 0.0).astype(BF))
    turn = lax.rem(line, 2).astype(F32)
    taken = (named > 0.5) & (jnp.abs(before - turn) < 0.5)
    sel_ref[...] = jnp.where(taken, 1.0, 0.0).astype(BF)
    comb_ref[...] = jnp.where(taken, weight, 0.0)

    link = jnp.where((ri == jnp.broadcast_to(parents[...], (TOKS, TOKS))) | (ri == ci), 1.0, 0.0)
    for unused in range(5):
        link = jnp.minimum(dot(link.astype(BF), link.astype(BF)), 1.0)
    link_ref[...] = link.astype(BF)

    pl.semaphore_wait(barrier, 7)

    up_a, down_a = dev(ring(a, 1), b), dev(ring(a, 3), b)
    up_b, down_b = dev(a, ring(b, 1)), dev(a, ring(b, 3))

    def blk(a_, b_):
        return ag.at[b_ * 4 + a_]

    def half(a_, b_, h):
        return ag.at[b_ * 4 + a_, pl.ds(16 * h, 16)]

    def spread_b(j, a_):
        go(("b", j, 0), blk(a_, b), blk(a_, b), up_b)
        go(("b", j, 1), blk(a_, b), blk(a_, b), down_b)

    am, ap, af = ring(a, 3), ring(a, 1), ring(a, 2)
    bm, bp, bf = ring(b, 3), ring(b, 1), ring(b, 2)
    go(("a", 0), blk(a, b), blk(a, b), up_a)
    go(("a", 1), blk(a, b), blk(a, b), down_a)
    spread_b(0, a)
    go(("a", 2), blk(a, b), blk(a, b), dev(af, b))
    go("wq", wq_hbm, wq.at[:, pl.ds(lane0, HD)], sibling)
    go("wkv", wkv_hbm, wkv.at[pl.ds(kv_row, 32)], sibling)
    go("wo", wo_hbm, wo.at[pl.ds(lane0, HD)], sibling)

    eye = jnp.where(ri == ci, 1.0, 0.0).astype(BF)
    reach = dot(link_ref[...], eye, TN)
    allowed = jnp.where(kind[0] == 1, reach, jnp.where(ci <= ri, 1.0, 0.0))
    allow_ref[...] = jnp.where(allowed > 0.5, 0.0, NEG_FILL)
    depth = jnp.sum(allowed, axis=1, keepdims=True) - 1.0
    total = prefix[0] + accepted[0]
    angle = (total.astype(F32) + depth) * freq_ref[...]
    cosine = jnp.cos(angle)
    lane = lax.broadcasted_iota(jnp.int32, (TOKS, HD), 1)
    sine = jnp.sin(angle)
    sine = jnp.where(lane < HD // 2, -sine, sine)
    for gain_ref, cos_ref, sin_ref in ((query_gain, qcos, qsin), (key_gain, kcos, ksin)):
        gain = jnp.broadcast_to(gain_ref[...][None, :], (TOKS, HD))
        cos_ref[...] = cosine * gain
        sin_ref[...] = sine * pltpu.roll(gain, HD // 2, 1)
    row = lax.broadcasted_iota(jnp.int32, (1, CACHE), 1)
    seen = (row < prefix[0]) & ((row < SINK) | (row >= total - WIN))
    for m in range(8):
        seen = seen | ((row == prefix[0] + path[0, m]) & (accepted[0] > m))
    seen_ref[...] = jnp.where(seen, 0.0, NEG_FILL)

    come(("a", 0), blk(am, b))
    spread_b(1, am)
    come(("a", 1), blk(ap, b))
    spread_b(2, ap)

    def relay_b(j, a_):
        come(("b", j, 0), blk(a_, bm))
        go(("bh", j, 0), half(a_, bm, 0), half(a_, bm, 0), up_b)
        come(("b", j, 1), blk(a_, bp))
        go(("bh", j, 1), half(a_, bp, 1), half(a_, bp, 1), down_b)

    relay_b(0, a)
    come(("a", 2), blk(af, b))
    spread_b(3, af)
    go(("b", 3, 2), blk(af, b), blk(af, b), dev(a, bf))

    for load in loads[:2]:
        load.wait()
    other_lane = pl.multiple_of(HD - core * HD, HD)
    other_row = pl.multiple_of(lax.rem(chip, 2) * 64 + 32 - core * 32, 32)
    come("wq", wq.at[:, pl.ds(other_lane, HD)])
    come("wkv", wkv.at[pl.ds(other_row, 32)])

    def project(b_):
        rows = ag[pl.ds(b_ * 4, 4)].reshape(4 * TOKS, D)
        q = dot(rows, wq[...])
        kv = dot(rows, wkv[...], NT)
        qsend[pl.ds(b_ * 4, 4), :, 0 : 2 * HD] = q.astype(BF).reshape(4, TOKS, 2 * HD)
        qsend[pl.ds(b_ * 4, 4), :, 2 * HD :] = kv.astype(BF).reshape(4, TOKS, HD)

    def post_queries(b_, first):
        for k in (2, 1, 3, 0)[: 4 - first]:
            a_ = ring(a, k)
            copy = remote(
                qsend.at[b_ * 4 + a_], qrecv.at[chip], qs, qr, dev(a_, b_)
            )
            copy.start()

    project(b)
    qrecv[chip] = qsend[own]
    post_queries(b, 1)

    relay_b(1, am)
    relay_b(2, ap)
    come(("b", 3, 0), blk(af, bm))
    project(bm)
    post_queries(bm, 0)
    come(("b", 3, 1), blk(af, bp))
    project(bp)
    post_queries(bp, 0)
    for j, a_ in enumerate((a, am, ap)):
        come(("bh", j, 0), half(a_, bf, 0))
        come(("bh", j, 1), half(a_, bf, 1))
    come(("b", 3, 2), blk(af, bf))
    pl.semaphore_signal(meet, inc=1, device_id={"tensor": sibling}, device_id_type=MESH)
    project(bf)
    post_queries(bf, 0)

    for load in loads[5:7]:
        load.wait()
    await_bytes(qrecv.at[pl.ds(0, 15)], qr)

    ones = jnp.ones((HD, HD), BF)

    def rope(v, cosv, sinv):
        count = v.shape[0]
        v = v.reshape(count * TOKS, HD)
        square = v * v
        upper = square.astype(BF)
        lower = (square - upper.astype(F32)).astype(BF)
        mean = (dot(upper, ones) + dot(lower, ones)) * (1.0 / HD)
        turned = (
            v.reshape(count, TOKS, HD) * cosv[...][None]
            + pltpu.roll(v, HD // 2, 1).reshape(count, TOKS, HD) * sinv[...][None]
        )
        return (turned.reshape(count * TOKS, HD) * lax.rsqrt(mean + EPSILON)).astype(BF)

    def heads(g, carry):
        qraw = [
            qrecv[4 * g + i, :, HD * j : HD * (j + 1)] for i in range(4) for j in range(2)
        ]
        qg = rope(jnp.stack(qraw, axis=0).astype(F32), qcos, qsin)
        kraw = qrecv[2 * g, :, 2 * HD :].astype(F32) + qrecv[2 * g + 1, :, 2 * HD :].astype(F32)
        knew = rope(kraw[None], kcos, ksin)
        vnew = qrecv[8 + 2 * g, :, 2 * HD :] + qrecv[9 + 2 * g, :, 2 * HD :]
        cols = pl.ds(pl.multiple_of(g * HD, HD), HD)
        s_old = dot(qg, kc[:, cols], NT) + seen_ref[...]
        s_new = dot(qg, knew, NT)
        s_new = (s_new.reshape(8, TOKS, TOKS) + allow_ref[...][None]).reshape(8 * TOKS, TOKS)
        top = jnp.maximum(
            jnp.max(s_old, axis=-1, keepdims=True), jnp.max(s_new, axis=-1, keepdims=True)
        )
        e_old = jnp.exp2((s_old - top) * (SCALE * LOG2E))
        e_new = jnp.exp2((s_new - top) * (SCALE * LOG2E))
        denom = jnp.sum(e_old, axis=-1, keepdims=True) + jnp.sum(e_new, axis=-1, keepdims=True)
        o = dot(e_old.astype(BF), vc[:, cols]) + dot(e_new.astype(BF), vnew)
        o = (o / denom).astype(BF)
        for i in range(4):
            to = 4 * g + i
            for j in range(2):
                r0 = (2 * i + j) * TOKS
                asend[to, :, HD * j : HD * (j + 1)] = o[r0 : r0 + TOKS]

            @pl.when(to != chip)
            def _():
                remote(asend.at[to], ain.at[own], asem, ar.at[b], 2 * to + core).start()

        return carry

    lax.fori_loop(0, 4, heads, 0)
    ain[own] = asend[chip]

    loads[4].wait()
    come("wo", wo.at[pl.ds(other_lane, HD)])
    order = (bf, bp, bm, b)
    for k, b_ in enumerate(order):
        await_bytes(ain.at[pl.ds(b_ * 4, 3 if k == 3 else 4)], ar.at[b_])

    def share(a_):
        rows = jnp.concatenate([ain[b_ * 4 + a_] for b_ in order], axis=0)
        return dot(rows, wo[...])

    s1[...] = share(af).astype(BF).reshape(4, TOKS, D)
    top_half, low_half = pl.ds(0, 16), pl.ds(16, 16)
    for k in range(4):
        go(("s", k, 0), s1.at[k, top_half], r1.at[k, top_half], up_a)
        go(("s", k, 1), s1.at[k, low_half], r1.at[k, low_half], down_a)
    pup[...] = share(ap).reshape(4, TOKS, D)
    pdown[...] = share(am).reshape(4, TOKS, D)
    pown[...] = share(a).reshape(4, TOKS, D)
    for k in range(4):
        come(("s", k, 0), r1.at[k, top_half])
        s2[k, 0, 0:16] = (pup[k, 0:16] + r1[k, 0:16].astype(F32)).astype(BF)
        s2[k, 0, 16:32] = pup[k, 16:32].astype(BF)
        go(("t", k, 0), s2.at[k, 0], r2.at[k, 0], up_a)
        come(("s", k, 1), r1.at[k, low_half])
        s2[k, 1, 0:16] = pdown[k, 0:16].astype(BF)
        s2[k, 1, 16:32] = (pdown[k, 16:32] + r1[k, 16:32].astype(F32)).astype(BF)
        go(("t", k, 1), s2.at[k, 1], r2.at[k, 1], down_a)
    for k, b_ in enumerate(order):
        come(("t", k, 0), r2.at[k, 0])
        come(("t", k, 1), r2.at[k, 1])
        rs = pown[k] + r2[k, 0].astype(F32) + r2[k, 1].astype(F32)
        if k < 3:
            v1[k] = rs.astype(BF)
            go(("v", k), v1.at[k], v2.at[k], dev(a, b_))
        else:
            hid[...] = res[...].astype(F32) + rs
    for k in range(3):
        come(("v", k), v2.at[k])
    hidden = hid[...] + (v2[0].astype(F32) + v2[1].astype(F32) + v2[2].astype(F32))
    hid[...] = hidden
    inv = lax.rsqrt(jnp.mean(hidden * hidden, axis=-1, keepdims=True) + EPSILON)
    normed = (hidden * inv * ffn_gain[...][None, :]).astype(BF)

    picked = dot(sel_ref[...], normed)
    for j in range(16):
        fs[pl.ds(j, 64, stride=16), :] = picked[:, HD * j : HD * (j + 1)]
    dsend[...] = fs[...].astype(BF).reshape(N, 32, HD)

    def post(src, dst, ssem, rsem):
        for da, db in FAR_FIRST:
            for other in range(2):
                if (da, db, other) == (0, 0, 0):
                    continue
                to = dev(ring(a, da), ring(b, db)) + other * (1 - 2 * core)
                remote(src.at[to], dst.at[t], ssem, rsem, to).start()

    pl.semaphore_wait(meet, 1)
    post(dsend, drecv, ds, dr)
    drecv[t] = dsend[t]
    for load in loads[7:]:
        load.wait()
    await_bytes(drecv.at[pl.ds(0, N - 1)], dr)
    fs[...] = drecv[...].reshape(1024, HD).astype(F32)
    for j in range(16):
        xs[:, HD * j : HD * (j + 1)] = fs[pl.ds(j, 64, stride=16), :].astype(BF)
    gate = dot(wg[...], xs[...], NT)
    up = dot(wu[...], xs[...], NT)
    inner = (gate / (1.0 + jnp.exp(-gate)) * up).astype(BF)
    y = dot(inner, wd[...], TN)
    for j in range(16):
        fs[pl.ds(j, 64, stride=16), :] = y[:, HD * j : HD * (j + 1)]
    ysend[...] = fs[...].astype(BF).reshape(N, 32, HD)
    post(ysend, yrecv, ys, yr)
    yrecv[t] = ysend[t]
    await_bytes(yrecv.at[pl.ds(0, N - 1)], yr)
    fs[...] = yrecv[...].reshape(1024, HD).astype(F32)
    comb = comb_ref[...]
    comb_hi = comb.astype(BF)
    comb_lo = (comb - comb_hi.astype(F32)).astype(BF)
    for j in range(16):
        yj = fs[pl.ds(j, 64, stride=16), :].astype(BF)
        moe = dot(comb_hi, yj, TN) + dot(comb_lo, yj, TN)
        cols = slice(HD * j, HD * (j + 1))
        out_ref[:, cols] = (hid[:, cols] + moe).astype(BF)

    for copy in sends:
        copy.wait_send()
    await_bytes(qsend.at[pl.ds(0, 15)], qs)
    await_bytes(asend.at[pl.ds(0, 15)], asem)
    await_bytes(dsend.at[pl.ds(0, N - 1)], ds)
    await_bytes(ysend.at[pl.ds(0, N - 1)], ys)


def body(
    residual_in, attn_gain, w_query, w_keyval, query_gain, key_gain, w_out, ffn_gain,
    w_gate, w_up, w_down, key_cache, value_cache, prefix_lens, accepted, accept_path,
    parents, slot_kinds, expert_ids, gate_probs,
):
    half = np.arange(HD // 2, dtype=np.float64)
    freq = np.exp(-(2.0 * half / HD) * math.log(ROPE_BASE)).astype(np.float32)
    freq = jnp.asarray(np.concatenate([freq, freq])[None, :])
    vmem = pl.BlockSpec(memory_space=pltpu.VMEM)
    sm = pltpu.SMEM
    hbm = pl.BlockSpec(memory_space=pltpu.HBM)
    dma = pltpu.SemaphoreType.DMA
    vm = pltpu.VMEM
    return pl.pallas_call(
        layer_kernel,
        out_shape=jax.ShapeDtypeStruct((TOKS, D), BF),
        in_specs=[hbm] * 21,
        out_specs=vmem,
        scratch_shapes=[
            vm((1, HD), F32),
            vm((D,), F32), vm((HD,), F32), vm((HD,), F32), vm((D,), F32),
            vm((1, TOKS), jnp.int32),
            sm((1,), jnp.int32), sm((1,), jnp.int32), sm((1, 8), jnp.int32), sm((1,), jnp.int32),
            vm((TOKS, D), BF),
            vm((D, 2 * HD), BF),
            vm((HD, D), BF),
            vm((2 * HD, D), BF),
            vm((FF, D), BF),
            vm((FF, D), BF),
            vm((FF, D), BF),
            vm((CACHE, 4 * HD), BF),
            vm((CACHE, 4 * HD), BF),
            vm((8, HD), jnp.int32),
            vm((8, HD), F32),
            vm((16, TOKS, D), BF),
            vm((16, TOKS, 3 * HD), BF),
            vm((16, TOKS, 3 * HD), BF),
            vm((16, TOKS, 2 * HD), BF),
            vm((16, TOKS, 2 * HD), BF),
            vm((4, TOKS, D), F32),
            vm((4, TOKS, D), F32),
            vm((4, TOKS, D), F32),
            vm((4, TOKS, D), BF),
            vm((4, TOKS, D), BF),
            vm((4, 2, TOKS, D), BF),
            vm((4, 2, TOKS, D), BF),
            vm((3, TOKS, D), BF),
            vm((3, TOKS, D), BF),
            vm((TOKS, D), F32),
            vm((1024, HD), F32),
            vm((2 * N, D), BF),
            vm((N, 32, HD), BF),
            vm((N, 32, HD), BF),
            vm((N, 32, HD), BF),
            vm((N, 32, HD), BF),
            vm((2 * N, TOKS), BF),
            vm((2 * N, TOKS), F32),
            vm((TOKS, TOKS), BF),
            vm((TOKS, HD), F32), vm((TOKS, HD), F32), vm((TOKS, HD), F32), vm((TOKS, HD), F32),
            vm((TOKS, TOKS), F32),
            vm((1, CACHE), F32),
            dma((11,)),
            dma((10,)),
            pltpu.SemaphoreType.REGULAR,
            dma((40,)), dma((40,)),
            dma(()), dma(()),
            dma(()), dma((4,)),
            dma(()), dma(()), dma(()), dma(()),
        ],
        compiler_params=pltpu.CompilerParams(
            collective_id=0, has_side_effects=True, vmem_limit_bytes=56 * 1024 * 1024
        ),
        name="layer",
    )(
        freq, attn_gain, query_gain, key_gain, ffn_gain, parents,
        prefix_lens, accepted, accept_path, slot_kinds,
        residual_in, w_query, w_keyval, w_out, w_gate, w_up, w_down,
        key_cache, value_cache, expert_ids.T, gate_probs.T,
    )


def solution(mesh):
    in_specs = (
        P(("group", "tensor"), None),
        P(),
        P(None, "tensor"),
        P("tensor", None),
        P(),
        P(),
        P("tensor", None),
        P(),
        P("tensor", None, None),
        P("tensor", None, None),
        P("tensor", None, None),
        P(("group", "tensor"), None, None),
        P(("group", "tensor"), None, None),
        P(("group", "tensor")),
        P(("group", "tensor")),
        P(("group", "tensor"), None),
        P(("group", "tensor"), None),
        P(("group", "tensor")),
        P("group", None),
        P("group", None),
    )
    out_specs = P(("group", "tensor"), None)
    return jax.shard_map(body, mesh=mesh, in_specs=in_specs, out_specs=out_specs, check_vma=False)
```

```python
import functools
import math

import jax
import jax.numpy as jnp
import numpy as np
from jax import lax
from jax.experimental import pallas as pl
from jax.experimental.pallas import tpu as pltpu
from jax.sharding import PartitionSpec as P

SINK = 4
WIN = 512
EPSILON = 1e-06
NEG_FILL = -1e30
ROPE_BASE = 1000000.0

N = 32
TOKS = 32
D = 2048
HD = 128
FF = 768
CACHE = 1024
SCALE = HD**-0.5
LOG2E = math.log2(math.e)

BF = jnp.bfloat16
F32 = jnp.float32
MESH = pl.DeviceIdType.MESH
FAR_FIRST = sorted(
    ((i, j) for i in range(4) for j in range(4)),
    key=lambda ij: -(min(ij[0], 4 - ij[0]) + min(ij[1], 4 - ij[1])),
)
NT = (((1,), (1,)), ((), ()))
TN = (((0,), (0,)), ((), ()))


def dot(a, b, dims=(((1,), (0,)), ((), ()))):
    return lax.dot_general(a, b, dims, preferred_element_type=F32)


def layer_kernel(
    freq_hbm, again_hbm, qgain_hbm, kgain_hbm, fgain_hbm, par_hbm, prefix_hbm, acc_hbm, path_hbm, kind_hbm,
    res_hbm, wq_hbm, wkv_hbm, wo_hbm, wg_hbm, wu_hbm, wd_hbm, kc_hbm, vc_hbm, ids_hbm, gates_hbm,
    out_ref,
    freq_ref, attn_gain, query_gain, key_gain, ffn_gain, parents, prefix, accepted, path, kind,
    res, wq, wkv, wo, wg, wu, wd, kc, vc, ids, gates,
    ag, qsend, qrecv, asend, ain,
    pup, pdown, pown, s1, r1, s2, r2, v1, v2, hid,
    fs, xs, dsend, drecv, ysend, yrecv, sel_ref, comb_ref,
    qcos, qsin, kcos, ksin, allow_ref, seen_ref,
    lsem, isem, meet, snd, rcv, qs, qr, asem, ar, ds, dr, ys, yr,
):
    t = lax.axis_index("tensor")
    core = lax.rem(t, 2)
    chip = t // 2
    cx = chip // 4
    cy = lax.rem(chip, 4)
    a = cx * (1 - core) + cy * core
    b = cy * (1 - core) + cx * core
    step_a = 8 - 6 * core
    step_b = 2 + 6 * core

    def dev(a_, b_):
        return a_ * step_a + b_ * step_b + core

    def ring(v, k):
        return lax.rem(v + k, 4)

    def remote(src, dst, ssem, rsem, to):
        return pltpu.make_async_remote_copy(
            src_ref=src, dst_ref=dst, send_sem=ssem, recv_sem=rsem,
            device_id={"tensor": to}, device_id_type=MESH,
        )

    def await_bytes(ref, sem):
        pltpu.make_async_copy(ref, ref, sem).wait()

    sends = []
    slots = {}

    def slot(key):
        return slots.setdefault(key, len(slots))

    def go(key, src, dst, to):
        copy = remote(src, dst, snd.at[len(sends)], rcv.at[slot(key)], to)
        copy.start()
        sends.append(copy)

    def come(key, ref):
        await_bytes(ref, rcv.at[slot(key)])

    load_res = pltpu.make_async_copy(res_hbm, res, lsem.at[0])
    load_res.start()
    small = [
        pltpu.make_async_copy(src, dst, isem.at[i])
        for i, (src, dst) in enumerate(
            (
                (again_hbm, attn_gain), (freq_hbm, freq_ref), (qgain_hbm, query_gain),
                (kgain_hbm, key_gain), (fgain_hbm, ffn_gain), (par_hbm, parents),
                (prefix_hbm, prefix), (acc_hbm, accepted), (path_hbm, path), (kind_hbm, kind),
            )
        )
    ]
    small[0].start()
    wkv[...] = jnp.zeros_like(wkv)
    lane0 = pl.multiple_of(core * HD, HD)
    kv_row = pl.multiple_of(lax.rem(chip, 2) * 64 + core * 32, 32)
    lane_win = pl.multiple_of((t // 4) * HD, HD)
    loads = [
        pltpu.make_async_copy(wq_hbm, wq.at[:, pl.ds(lane0, HD)], lsem.at[1]),
        pltpu.make_async_copy(wkv_hbm, wkv.at[pl.ds(kv_row, 32)], lsem.at[2]),
        pltpu.make_async_copy(ids_hbm.at[:, pl.ds(lane_win, HD)], ids, lsem.at[3]),
        pltpu.make_async_copy(gates_hbm.at[:, pl.ds(lane_win, HD)], gates, lsem.at[4]),
        pltpu.make_async_copy(wo_hbm, wo.at[pl.ds(lane0, HD)], lsem.at[5]),
        pltpu.make_async_copy(kc_hbm.at[0], kc, lsem.at[6]),
        pltpu.make_async_copy(vc_hbm.at[0], vc, lsem.at[7]),
        pltpu.make_async_copy(wg_hbm.at[0], wg, lsem.at[8]),
        pltpu.make_async_copy(wu_hbm.at[0], wu, lsem.at[9]),
        pltpu.make_async_copy(wd_hbm.at[0], wd, lsem.at[10]),
    ]
    for load in loads[2:4] + small[1:] + loads[:2] + loads[4:]:
        load.start()

    barrier = pltpu.get_barrier_semaphore()

    sibling = t + 1 - 2 * core
    line = [dev(ring(a, k), b) for k in (1, 2, 3)] + [dev(a, ring(b, k)) for k in (1, 2, 3)]
    for to in line + [sibling]:
        pl.semaphore_signal(barrier, inc=1, device_id={"tensor": to}, device_id_type=MESH)

    load_res.wait()
    small[0].wait()
    own = b * 4 + a
    xv = res[...].astype(F32)
    inv = lax.rsqrt(jnp.mean(xv * xv, axis=-1, keepdims=True) + EPSILON)
    ag[own] = (xv * inv * attn_gain[...][None, :]).astype(BF)

    pl.semaphore_wait(barrier, 7)

    up_a, down_a = dev(ring(a, 1), b), dev(ring(a, 3), b)
    up_b, down_b = dev(a, ring(b, 1)), dev(a, ring(b, 3))

    def blk(a_, b_):
        return ag.at[b_ * 4 + a_]

    def half(a_, b_, h):
        return ag.at[b_ * 4 + a_, pl.ds(16 * h, 16)]

    def spread_b(j, a_):
        go(("b", j, 0), blk(a_, b), blk(a_, b), up_b)
        go(("b", j, 1), blk(a_, b), blk(a_, b), down_b)

    am, ap, af = ring(a, 3), ring(a, 1), ring(a, 2)
    bm, bp, bf = ring(b, 3), ring(b, 1), ring(b, 2)
    go(("a", 0), blk(a, b), blk(a, b), up_a)
    go(("a", 1), blk(a, b), blk(a, b), down_a)
    spread_b(0, a)
    go(("a", 2), blk(a, b), blk(a, b), dev(af, b))
    go("wq", wq_hbm, wq.at[:, pl.ds(lane0, HD)], sibling)
    go("wkv", wkv_hbm, wkv.at[pl.ds(kv_row, 32)], sibling)
    go("wo", wo_hbm, wo.at[pl.ds(lane0, HD)], sibling)

    for load in small[1:]:
        load.wait()
    ri = lax.broadcasted_iota(jnp.int32, (TOKS, TOKS), 0)
    ci = lax.broadcasted_iota(jnp.int32, (TOKS, TOKS), 1)
    link = jnp.where((ri == jnp.broadcast_to(parents[...], (TOKS, TOKS))) | (ri == ci), 1.0, 0.0)
    for unused in range(5):
        link = jnp.minimum(dot(link.astype(BF), link.astype(BF)), 1.0)
    eye = jnp.where(ri == ci, 1.0, 0.0).astype(BF)
    reach = dot(link.astype(BF), eye, TN)
    allowed = jnp.where(kind[0] == 1, reach, jnp.where(ci <= ri, 1.0, 0.0))
    allow_ref[...] = jnp.where(allowed > 0.5, 0.0, NEG_FILL)
    depth = jnp.sum(allowed, axis=1, keepdims=True) - 1.0
    total = prefix[0] + accepted[0]
    angle = (total.astype(F32) + depth) * freq_ref[...]
    cosine = jnp.cos(angle)
    lane = lax.broadcasted_iota(jnp.int32, (TOKS, HD), 1)
    sine = jnp.sin(angle)
    sine = jnp.where(lane < HD // 2, -sine, sine)
    for gain_ref, cos_ref, sin_ref in ((query_gain, qcos, qsin), (key_gain, kcos, ksin)):
        gain = jnp.broadcast_to(gain_ref[...][None, :], (TOKS, HD))
        cos_ref[...] = cosine * gain
        sin_ref[...] = sine * pltpu.roll(gain, HD // 2, 1)
    row = lax.broadcasted_iota(jnp.int32, (1, CACHE), 1)
    seen = (row < prefix[0]) & ((row < SINK) | (row >= total - WIN))
    for m in range(8):
        seen = seen | ((row == prefix[0] + path[0, m]) & (accepted[0] > m))
    seen_ref[...] = jnp.where(seen, 0.0, NEG_FILL)

    come(("a", 0), blk(am, b))
    spread_b(1, am)
    come(("a", 1), blk(ap, b))
    spread_b(2, ap)

    def relay_b(j, a_):
        come(("b", j, 0), blk(a_, bm))
        go(("bh", j, 0), half(a_, bm, 0), half(a_, bm, 0), up_b)
        come(("b", j, 1), blk(a_, bp))
        go(("bh", j, 1), half(a_, bp, 1), half(a_, bp, 1), down_b)

    relay_b(0, a)
    come(("a", 2), blk(af, b))
    spread_b(3, af)
    go(("b", 3, 2), blk(af, b), blk(af, b), dev(a, bf))

    for load in loads[:2]:
        load.wait()
    other_lane = pl.multiple_of(HD - core * HD, HD)
    other_row = pl.multiple_of(lax.rem(chip, 2) * 64 + 32 - core * 32, 32)
    come("wq", wq.at[:, pl.ds(other_lane, HD)])
    come("wkv", wkv.at[pl.ds(other_row, 32)])

    def project(b_):
        rows = ag[pl.ds(b_ * 4, 4)].reshape(4 * TOKS, D)
        q = dot(rows, wq[...])
        kv = dot(rows, wkv[...], NT)
        qsend[pl.ds(b_ * 4, 4), :, 0 : 2 * HD] = q.astype(BF).reshape(4, TOKS, 2 * HD)
        qsend[pl.ds(b_ * 4, 4), :, 2 * HD :] = kv.astype(BF).reshape(4, TOKS, HD)

    def post_queries(b_, first):
        for k in (2, 1, 3, 0)[: 4 - first]:
            a_ = ring(a, k)
            copy = remote(
                qsend.at[b_ * 4 + a_], qrecv.at[chip], qs, qr, dev(a_, b_)
            )
            copy.start()

    project(b)
    qrecv[chip] = qsend[own]
    post_queries(b, 1)

    relay_b(1, am)
    relay_b(2, ap)
    come(("b", 3, 0), blk(af, bm))
    project(bm)
    post_queries(bm, 0)
    come(("b", 3, 1), blk(af, bp))
    project(bp)
    post_queries(bp, 0)
    for j, a_ in enumerate((a, am, ap)):
        come(("bh", j, 0), half(a_, bf, 0))
        come(("bh", j, 1), half(a_, bf, 1))
    come(("b", 3, 2), blk(af, bf))
    pl.semaphore_signal(meet, inc=1, device_id={"tensor": sibling}, device_id_type=MESH)
    project(bf)
    post_queries(bf, 0)

    for load in loads[5:7]:
        load.wait()
    await_bytes(qrecv.at[pl.ds(0, 15)], qr)

    ones = jnp.ones((HD, HD), BF)

    def rope(v, cosv, sinv):
        count = v.shape[0]
        v = v.reshape(count * TOKS, HD)
        square = v * v
        upper = square.astype(BF)
        lower = (square - upper.astype(F32)).astype(BF)
        mean = (dot(upper, ones) + dot(lower, ones)) * (1.0 / HD)
        turned = (
            v.reshape(count, TOKS, HD) * cosv[...][None]
            + pltpu.roll(v, HD // 2, 1).reshape(count, TOKS, HD) * sinv[...][None]
        )
        return (turned.reshape(count * TOKS, HD) * lax.rsqrt(mean + EPSILON)).astype(BF)

    def heads(off):
        g = ring(cx, off)
        qraw = [
            qrecv[4 * g + i, :, HD * j : HD * (j + 1)] for i in range(4) for j in range(2)
        ]
        qg = rope(jnp.stack(qraw, axis=0).astype(F32), qcos, qsin)
        kraw = qrecv[2 * g, :, 2 * HD :].astype(F32) + qrecv[2 * g + 1, :, 2 * HD :].astype(F32)
        knew = rope(kraw[None], kcos, ksin)
        vnew = qrecv[8 + 2 * g, :, 2 * HD :] + qrecv[9 + 2 * g, :, 2 * HD :]
        cols = pl.ds(pl.multiple_of(g * HD, HD), HD)
        s_old = dot(qg, kc[:, cols], NT) + seen_ref[...]
        s_new = dot(qg, knew, NT)
        s_new = (s_new.reshape(8, TOKS, TOKS) + allow_ref[...][None]).reshape(8 * TOKS, TOKS)
        top = jnp.maximum(
            jnp.max(s_old, axis=-1, keepdims=True), jnp.max(s_new, axis=-1, keepdims=True)
        )
        e_old = jnp.exp2((s_old - top) * (SCALE * LOG2E))
        e_new = jnp.exp2((s_new - top) * (SCALE * LOG2E))
        denom = jnp.sum(e_old, axis=-1, keepdims=True) + jnp.sum(e_new, axis=-1, keepdims=True)
        o = dot(e_old.astype(BF), vc[:, cols]) + dot(e_new.astype(BF), vnew)
        o = (o / denom).astype(BF)
        for i in range(4):
            to = 4 * g + i
            for j in range(2):
                r0 = (2 * i + j) * TOKS
                asend[to, :, HD * j : HD * (j + 1)] = o[r0 : r0 + TOKS]

            def send():
                remote(asend.at[to], ain.at[own], asem, ar.at[b], 2 * to + core).start()

            if off == 0:
                pl.when(to != chip)(send)
            else:
                send()

    for off in (2, 1, 3, 0):
        heads(off)
    ain[own] = asend[chip]

    loads[4].wait()
    come("wo", wo.at[pl.ds(other_lane, HD)])
    order = (bf, bp, bm, b)
    for k, b_ in enumerate(order):
        await_bytes(ain.at[pl.ds(b_ * 4, 3 if k == 3 else 4)], ar.at[b_])

    def share(a_):
        rows = jnp.concatenate([ain[b_ * 4 + a_] for b_ in order], axis=0)
        return dot(rows, wo[...])

    s1[...] = share(af).astype(BF).reshape(4, TOKS, D)
    top_half, low_half = pl.ds(0, 16), pl.ds(16, 16)
    for k in range(4):
        go(("s", k, 0), s1.at[k, top_half], r1.at[k, top_half], up_a)
        go(("s", k, 1), s1.at[k, low_half], r1.at[k, low_half], down_a)
    pup[...] = share(ap).reshape(4, TOKS, D)
    pdown[...] = share(am).reshape(4, TOKS, D)
    pown[...] = share(a).reshape(4, TOKS, D)

    for load in loads[2:4]:
        load.wait()
    line = lax.broadcasted_iota(jnp.int32, (2 * N, TOKS), 0)
    expert = line // 2
    named = jnp.zeros((2 * N, TOKS), F32)
    weight = jnp.zeros((2 * N, TOKS), F32)
    turn_lanes = lax.rem(HD - lax.rem(t, 4) * TOKS, HD)
    idv = pltpu.roll(ids[...], turn_lanes, 1)[:, 0:TOKS]
    gv = pltpu.roll(gates[...], turn_lanes, 1)[:, 0:TOKS]
    for k in range(8):
        hit = jnp.broadcast_to(idv[k : k + 1], (2 * N, TOKS)) == expert
        named = jnp.where(hit, 1.0, named)
        weight = weight + jnp.where(hit, jnp.broadcast_to(gv[k : k + 1], (2 * N, TOKS)), 0.0)
    before = dot(named.astype(BF), jnp.where(ri < ci, 1.0, 0.0).astype(BF))
    turn = lax.rem(line, 2).astype(F32)
    taken = (named > 0.5) & (jnp.abs(before - turn) < 0.5)
    sel_ref[...] = jnp.where(taken, 1.0, 0.0).astype(BF)
    comb_ref[...] = jnp.where(taken, weight, 0.0)

    for k in range(4):
        come(("s", k, 0), r1.at[k, top_half])
        s2[k, 0, 0:16] = (pup[k, 0:16] + r1[k, 0:16].astype(F32)).astype(BF)
        s2[k, 0, 16:32] = pup[k, 16:32].astype(BF)
        go(("t", k, 0), s2.at[k, 0], r2.at[k, 0], up_a)
        come(("s", k, 1), r1.at[k, low_half])
        s2[k, 1, 0:16] = pdown[k, 0:16].astype(BF)
        s2[k, 1, 16:32] = (pdown[k, 16:32] + r1[k, 16:32].astype(F32)).astype(BF)
        go(("t", k, 1), s2.at[k, 1], r2.at[k, 1], down_a)
    for k, b_ in enumerate(order):
        come(("t", k, 0), r2.at[k, 0])
        come(("t", k, 1), r2.at[k, 1])
        rs = pown[k] + r2[k, 0].astype(F32) + r2[k, 1].astype(F32)
        if k < 3:
            v1[k] = rs.astype(BF)
            go(("v", k), v1.at[k], v2.at[k], dev(a, b_))
        else:
            hid[...] = res[...].astype(F32) + rs
    for k in range(3):
        come(("v", k), v2.at[k])
    hidden = hid[...] + (v2[0].astype(F32) + v2[1].astype(F32) + v2[2].astype(F32))
    hid[...] = hidden
    inv = lax.rsqrt(jnp.mean(hidden * hidden, axis=-1, keepdims=True) + EPSILON)
    normed = (hidden * inv * ffn_gain[...][None, :]).astype(BF)

    picked = dot(sel_ref[...], normed)
    for j in range(16):
        fs[pl.ds(j, 64, stride=16), :] = picked[:, HD * j : HD * (j + 1)]
    dsend[...] = fs[...].astype(BF).reshape(N, 32, HD)

    def post(src, dst, ssem, rsem):
        for da, db in FAR_FIRST:
            for other in range(2):
                if (da, db, other) == (0, 0, 0):
                    continue
                to = dev(ring(a, da), ring(b, db)) + other * (1 - 2 * core)
                remote(src.at[to], dst.at[t], ssem, rsem, to).start()

    pl.semaphore_wait(meet, 1)
    post(dsend, drecv, ds, dr)
    drecv[t] = dsend[t]
    for load in loads[7:]:
        load.wait()
    await_bytes(drecv.at[pl.ds(0, N - 1)], dr)
    fs[...] = drecv[...].reshape(1024, HD).astype(F32)
    for j in range(16):
        xs[:, HD * j : HD * (j + 1)] = fs[pl.ds(j, 64, stride=16), :].astype(BF)
    gate = dot(wg[...], xs[...], NT)
    up = dot(wu[...], xs[...], NT)
    inner = (gate / (1.0 + jnp.exp(-gate)) * up).astype(BF)
    y = dot(inner, wd[...], TN)
    for j in range(16):
        fs[pl.ds(j, 64, stride=16), :] = y[:, HD * j : HD * (j + 1)]
    ysend[...] = fs[...].astype(BF).reshape(N, 32, HD)
    post(ysend, yrecv, ys, yr)
    yrecv[t] = ysend[t]
    await_bytes(yrecv.at[pl.ds(0, N - 1)], yr)
    fs[...] = yrecv[...].reshape(1024, HD).astype(F32)
    comb = comb_ref[...]
    comb_hi = comb.astype(BF)
    comb_lo = (comb - comb_hi.astype(F32)).astype(BF)
    for j in range(16):
        yj = fs[pl.ds(j, 64, stride=16), :].astype(BF)
        moe = dot(comb_hi, yj, TN) + dot(comb_lo, yj, TN)
        cols = slice(HD * j, HD * (j + 1))
        out_ref[:, cols] = (hid[:, cols] + moe).astype(BF)

    for copy in sends:
        copy.wait_send()
    await_bytes(qsend.at[pl.ds(0, 15)], qs)
    await_bytes(asend.at[pl.ds(0, 15)], asem)
    await_bytes(dsend.at[pl.ds(0, N - 1)], ds)
    await_bytes(ysend.at[pl.ds(0, N - 1)], ys)


def body(
    residual_in, attn_gain, w_query, w_keyval, query_gain, key_gain, w_out, ffn_gain,
    w_gate, w_up, w_down, key_cache, value_cache, prefix_lens, accepted, accept_path,
    parents, slot_kinds, expert_ids, gate_probs,
):
    half = np.arange(HD // 2, dtype=np.float64)
    freq = np.exp(-(2.0 * half / HD) * math.log(ROPE_BASE)).astype(np.float32)
    freq = jnp.asarray(np.concatenate([freq, freq])[None, :])
    vmem = pl.BlockSpec(memory_space=pltpu.VMEM)
    sm = pltpu.SMEM
    hbm = pl.BlockSpec(memory_space=pltpu.HBM)
    dma = pltpu.SemaphoreType.DMA
    vm = pltpu.VMEM
    return pl.pallas_call(
        layer_kernel,
        out_shape=jax.ShapeDtypeStruct((TOKS, D), BF),
        in_specs=[hbm] * 21,
        out_specs=vmem,
        scratch_shapes=[
            vm((1, HD), F32),
            vm((D,), F32), vm((HD,), F32), vm((HD,), F32), vm((D,), F32),
            vm((1, TOKS), jnp.int32),
            sm((1,), jnp.int32), sm((1,), jnp.int32), sm((1, 8), jnp.int32), sm((1,), jnp.int32),
            vm((TOKS, D), BF),
            vm((D, 2 * HD), BF),
            vm((HD, D), BF),
            vm((2 * HD, D), BF),
            vm((FF, D), BF),
            vm((FF, D), BF),
            vm((FF, D), BF),
            vm((CACHE, 4 * HD), BF),
            vm((CACHE, 4 * HD), BF),
            vm((8, HD), jnp.int32),
            vm((8, HD), F32),
            vm((16, TOKS, D), BF),
            vm((16, TOKS, 3 * HD), BF),
            vm((16, TOKS, 3 * HD), BF),
            vm((16, TOKS, 2 * HD), BF),
            vm((16, TOKS, 2 * HD), BF),
            vm((4, TOKS, D), F32),
            vm((4, TOKS, D), F32),
            vm((4, TOKS, D), F32),
            vm((4, TOKS, D), BF),
            vm((4, TOKS, D), BF),
            vm((4, 2, TOKS, D), BF),
            vm((4, 2, TOKS, D), BF),
            vm((3, TOKS, D), BF),
            vm((3, TOKS, D), BF),
            vm((TOKS, D), F32),
            vm((1024, HD), F32),
            vm((2 * N, D), BF),
            vm((N, 32, HD), BF),
            vm((N, 32, HD), BF),
            vm((N, 32, HD), BF),
            vm((N, 32, HD), BF),
            vm((2 * N, TOKS), BF),
            vm((2 * N, TOKS), F32),
            vm((TOKS, HD), F32), vm((TOKS, HD), F32), vm((TOKS, HD), F32), vm((TOKS, HD), F32),
            vm((TOKS, TOKS), F32),
            vm((1, CACHE), F32),
            dma((11,)),
            dma((10,)),
            pltpu.SemaphoreType.REGULAR,
            dma((40,)), dma((40,)),
            dma(()), dma(()),
            dma(()), dma((4,)),
            dma(()), dma(()), dma(()), dma(()),
        ],
        compiler_params=pltpu.CompilerParams(
            collective_id=0, has_side_effects=True, vmem_limit_bytes=56 * 1024 * 1024
        ),
        name="layer",
    )(
        freq, attn_gain, query_gain, key_gain, ffn_gain, parents,
        prefix_lens, accepted, accept_path, slot_kinds,
        residual_in, w_query, w_keyval, w_out, w_gate, w_up, w_down,
        key_cache, value_cache, expert_ids.T, gate_probs.T,
    )


def solution(mesh):
    in_specs = (
        P(("group", "tensor"), None),
        P(),
        P(None, "tensor"),
        P("tensor", None),
        P(),
        P(),
        P("tensor", None),
        P(),
        P("tensor", None, None),
        P("tensor", None, None),
        P("tensor", None, None),
        P(("group", "tensor"), None, None),
        P(("group", "tensor"), None, None),
        P(("group", "tensor")),
        P(("group", "tensor")),
        P(("group", "tensor"), None),
        P(("group", "tensor"), None),
        P(("group", "tensor")),
        P("group", None),
        P("group", None),
    )
    out_specs = P(("group", "tensor"), None)
    return jax.shard_map(body, mesh=mesh, in_specs=in_specs, out_specs=out_specs, check_vma=False)
```

```python
import functools
import math

import jax
import jax.numpy as jnp
import numpy as np
from jax import lax
from jax.experimental import pallas as pl
from jax.experimental.pallas import tpu as pltpu
from jax.sharding import PartitionSpec as P

SINK = 4
WIN = 512
EPSILON = 1e-06
NEG_FILL = -1e30
ROPE_BASE = 1000000.0

N = 32
TOKS = 32
D = 2048
HD = 128
FF = 768
CACHE = 1024
SCALE = HD**-0.5
LOG2E = math.log2(math.e)

BF = jnp.bfloat16
F32 = jnp.float32
MESH = pl.DeviceIdType.MESH
FAR_FIRST = sorted(
    ((i, j) for i in range(4) for j in range(4)),
    key=lambda ij: -(min(ij[0], 4 - ij[0]) + min(ij[1], 4 - ij[1])),
)
NT = (((1,), (1,)), ((), ()))
TN = (((0,), (0,)), ((), ()))


def dot(a, b, dims=(((1,), (0,)), ((), ()))):
    return lax.dot_general(a, b, dims, preferred_element_type=F32)


def layer_kernel(
    freq_hbm, again_hbm, qgain_hbm, kgain_hbm, fgain_hbm, par_hbm, prefix_hbm, acc_hbm, path_hbm, kind_hbm,
    res_hbm, wq_hbm, wkv_hbm, wo_hbm, wg_hbm, wu_hbm, wd_hbm, kc_hbm, vc_hbm, ids_hbm, gates_hbm,
    out_ref,
    freq_ref, attn_gain, query_gain, key_gain, ffn_gain, parents, prefix, accepted, path, kind,
    res, wq, wkv, wo, wg, wu, wd, wgt, wut, kc, vc, ids, gates,
    ag, qsend, qrecv, asend, ain,
    pup, pdown, pown, s1, r1, s2, r2, v1, v2, hid,
    fs, xs, dsend, drecv, ysend, yrecv, sel_ref, comb_ref,
    qcos, qsin, kcos, ksin, allow_ref, seen_ref,
    lsem, isem, meet, snd, rcv, qs, qr, asem, ar, ds, dr, ys, yr,
):
    t = lax.axis_index("tensor")
    core = lax.rem(t, 2)
    chip = t // 2
    cx = chip // 4
    cy = lax.rem(chip, 4)
    a = cx * (1 - core) + cy * core
    b = cy * (1 - core) + cx * core
    step_a = 8 - 6 * core
    step_b = 2 + 6 * core

    def dev(a_, b_):
        return a_ * step_a + b_ * step_b + core

    def ring(v, k):
        return lax.rem(v + k, 4)

    def remote(src, dst, ssem, rsem, to):
        return pltpu.make_async_remote_copy(
            src_ref=src, dst_ref=dst, send_sem=ssem, recv_sem=rsem,
            device_id={"tensor": to}, device_id_type=MESH,
        )

    def await_bytes(ref, sem):
        pltpu.make_async_copy(ref, ref, sem).wait()

    sends = []
    slots = {}

    def slot(key):
        return slots.setdefault(key, len(slots))

    def go(key, src, dst, to):
        copy = remote(src, dst, snd.at[len(sends)], rcv.at[slot(key)], to)
        copy.start()
        sends.append(copy)

    def come(key, ref):
        await_bytes(ref, rcv.at[slot(key)])

    load_res = pltpu.make_async_copy(res_hbm, res, lsem.at[0])
    load_res.start()
    small = [
        pltpu.make_async_copy(src, dst, isem.at[i])
        for i, (src, dst) in enumerate(
            (
                (again_hbm, attn_gain), (freq_hbm, freq_ref), (qgain_hbm, query_gain),
                (kgain_hbm, key_gain), (fgain_hbm, ffn_gain), (par_hbm, parents),
                (prefix_hbm, prefix), (acc_hbm, accepted), (path_hbm, path), (kind_hbm, kind),
            )
        )
    ]
    small[0].start()
    wkv[...] = jnp.zeros_like(wkv)
    lane0 = pl.multiple_of(core * HD, HD)
    kv_row = pl.multiple_of(lax.rem(chip, 2) * 64 + core * 32, 32)
    lane_win = pl.multiple_of((t // 4) * HD, HD)
    loads = [
        pltpu.make_async_copy(wq_hbm, wq.at[:, pl.ds(lane0, HD)], lsem.at[1]),
        pltpu.make_async_copy(wkv_hbm, wkv.at[pl.ds(kv_row, 32)], lsem.at[2]),
        pltpu.make_async_copy(ids_hbm.at[:, pl.ds(lane_win, HD)], ids, lsem.at[3]),
        pltpu.make_async_copy(gates_hbm.at[:, pl.ds(lane_win, HD)], gates, lsem.at[4]),
        pltpu.make_async_copy(wo_hbm, wo.at[pl.ds(lane0, HD)], lsem.at[5]),
        pltpu.make_async_copy(kc_hbm.at[0], kc, lsem.at[6]),
        pltpu.make_async_copy(vc_hbm.at[0], vc, lsem.at[7]),
        pltpu.make_async_copy(wg_hbm.at[0], wg, lsem.at[8]),
        pltpu.make_async_copy(wu_hbm.at[0], wu, lsem.at[9]),
        pltpu.make_async_copy(wd_hbm.at[0], wd, lsem.at[10]),
    ]
    for load in loads[2:4] + small[1:] + loads[:2] + loads[4:]:
        load.start()

    barrier = pltpu.get_barrier_semaphore()

    sibling = t + 1 - 2 * core
    line = [dev(ring(a, k), b) for k in (1, 2, 3)] + [dev(a, ring(b, k)) for k in (1, 2, 3)]
    for to in line + [sibling]:
        pl.semaphore_signal(barrier, inc=1, device_id={"tensor": to}, device_id_type=MESH)

    load_res.wait()
    small[0].wait()
    own = b * 4 + a
    xv = res[...].astype(F32)
    inv = lax.rsqrt(jnp.mean(xv * xv, axis=-1, keepdims=True) + EPSILON)
    ag[own] = (xv * inv * attn_gain[...][None, :]).astype(BF)

    pl.semaphore_wait(barrier, 7)

    up_a, down_a = dev(ring(a, 1), b), dev(ring(a, 3), b)
    up_b, down_b = dev(a, ring(b, 1)), dev(a, ring(b, 3))

    def blk(a_, b_):
        return ag.at[b_ * 4 + a_]

    def half(a_, b_, h):
        return ag.at[b_ * 4 + a_, pl.ds(16 * h, 16)]

    def spread_b(j, a_):
        go(("b", j, 0), blk(a_, b), blk(a_, b), up_b)
        go(("b", j, 1), blk(a_, b), blk(a_, b), down_b)

    am, ap, af = ring(a, 3), ring(a, 1), ring(a, 2)
    bm, bp, bf = ring(b, 3), ring(b, 1), ring(b, 2)
    go(("a", 0), blk(a, b), blk(a, b), up_a)
    go(("a", 1), blk(a, b), blk(a, b), down_a)
    spread_b(0, a)
    go(("a", 2), blk(a, b), blk(a, b), dev(af, b))
    go("wq", wq_hbm, wq.at[:, pl.ds(lane0, HD)], sibling)
    go("wkv", wkv_hbm, wkv.at[pl.ds(kv_row, 32)], sibling)
    go("wo", wo_hbm, wo.at[pl.ds(lane0, HD)], sibling)

    for load in small[1:]:
        load.wait()
    ri = lax.broadcasted_iota(jnp.int32, (TOKS, TOKS), 0)
    ci = lax.broadcasted_iota(jnp.int32, (TOKS, TOKS), 1)
    link = jnp.where((ri == jnp.broadcast_to(parents[...], (TOKS, TOKS))) | (ri == ci), 1.0, 0.0)
    for unused in range(5):
        link = jnp.minimum(dot(link.astype(BF), link.astype(BF)), 1.0)
    eye = jnp.where(ri == ci, 1.0, 0.0).astype(BF)
    reach = dot(link.astype(BF), eye, TN)
    allowed = jnp.where(kind[0] == 1, reach, jnp.where(ci <= ri, 1.0, 0.0))
    allow_ref[...] = jnp.where(allowed > 0.5, 0.0, NEG_FILL)
    depth = jnp.sum(allowed, axis=1, keepdims=True) - 1.0
    total = prefix[0] + accepted[0]
    angle = (total.astype(F32) + depth) * freq_ref[...]
    cosine = jnp.cos(angle)
    lane = lax.broadcasted_iota(jnp.int32, (TOKS, HD), 1)
    sine = jnp.sin(angle)
    sine = jnp.where(lane < HD // 2, -sine, sine)
    for gain_ref, cos_ref, sin_ref in ((query_gain, qcos, qsin), (key_gain, kcos, ksin)):
        gain = jnp.broadcast_to(gain_ref[...][None, :], (TOKS, HD))
        cos_ref[...] = cosine * gain
        sin_ref[...] = sine * pltpu.roll(gain, HD // 2, 1)
    row = lax.broadcasted_iota(jnp.int32, (1, CACHE), 1)
    seen = (row < prefix[0]) & ((row < SINK) | (row >= total - WIN))
    for m in range(8):
        seen = seen | ((row == prefix[0] + path[0, m]) & (accepted[0] > m))
    seen_ref[...] = jnp.where(seen, 0.0, NEG_FILL)

    come(("a", 0), blk(am, b))
    spread_b(1, am)
    come(("a", 1), blk(ap, b))
    spread_b(2, ap)

    def relay_b(j, a_):
        come(("b", j, 0), blk(a_, bm))
        go(("bh", j, 0), half(a_, bm, 0), half(a_, bm, 0), up_b)
        come(("b", j, 1), blk(a_, bp))
        go(("bh", j, 1), half(a_, bp, 1), half(a_, bp, 1), down_b)

    relay_b(0, a)
    come(("a", 2), blk(af, b))
    spread_b(3, af)
    go(("b", 3, 2), blk(af, b), blk(af, b), dev(a, bf))

    for load in loads[:2]:
        load.wait()
    other_lane = pl.multiple_of(HD - core * HD, HD)
    other_row = pl.multiple_of(lax.rem(chip, 2) * 64 + 32 - core * 32, 32)
    come("wq", wq.at[:, pl.ds(other_lane, HD)])
    come("wkv", wkv.at[pl.ds(other_row, 32)])

    def project(blocks):
        count = len(blocks)
        rows = jnp.concatenate([ag[b_ * 4 + a_] for a_, b_ in blocks], axis=0)
        q = dot(rows, wq[...]).astype(BF)
        kv = dot(rows, wkv[...], NT).astype(BF)
        for i in range(count):
            a_, b_ = blocks[i]
            r = slice(TOKS * i, TOKS * (i + 1))
            qsend[b_ * 4 + a_, :, 0 : 2 * HD] = q[r]
            qsend[b_ * 4 + a_, :, 2 * HD :] = kv[r]

    def post_queries(blocks):
        for a_, b_ in blocks:
            remote(qsend.at[b_ * 4 + a_], qrecv.at[chip], qs, qr, dev(a_, b_)).start()

    near = [(af, b), (ap, b), (am, b)]
    project(near + [(a, b)])
    qrecv[chip] = qsend[own]
    post_queries(near)

    relay_b(1, am)
    relay_b(2, ap)
    near = [(a_, b_) for a_ in (ap, am, a) for b_ in (bm, bp)]
    project(near)
    post_queries(near)
    come(("b", 3, 0), blk(af, bm))
    come(("b", 3, 1), blk(af, bp))
    for j, a_ in enumerate((a, am, ap)):
        come(("bh", j, 0), half(a_, bf, 0))
        come(("bh", j, 1), half(a_, bf, 1))
    come(("b", 3, 2), blk(af, bf))
    rest = [(af, bf), (ap, bf), (am, bf), (af, bm), (af, bp), (a, bf)]
    pl.semaphore_signal(meet, inc=1, device_id={"tensor": sibling}, device_id_type=MESH)
    project(rest)
    post_queries(rest)

    def turn_weights(src, dst):
        for i in range(FF // HD):
            dst[:, HD * i : HD * (i + 1)] = src[HD * i : HD * (i + 1), :].T

    loads[7].wait()
    turn_weights(wg, wgt)

    for load in loads[5:7]:
        load.wait()
    await_bytes(qrecv.at[pl.ds(0, 15)], qr)

    ones = jnp.ones((HD, HD), BF)

    def rope(v, cosv, sinv):
        count = v.shape[0]
        v = v.reshape(count * TOKS, HD)
        square = v * v
        upper = square.astype(BF)
        lower = (square - upper.astype(F32)).astype(BF)
        mean = (dot(upper, ones) + dot(lower, ones)) * (1.0 / HD)
        turned = (
            v.reshape(count, TOKS, HD) * cosv[...][None]
            + pltpu.roll(v, HD // 2, 1).reshape(count, TOKS, HD) * sinv[...][None]
        )
        return (turned.reshape(count * TOKS, HD) * lax.rsqrt(mean + EPSILON)).astype(BF)

    def heads(off):
        g = ring(cx, off)
        qraw = [
            qrecv[4 * g + i, :, HD * j : HD * (j + 1)] for i in range(4) for j in range(2)
        ]
        qg = rope(jnp.stack(qraw, axis=0).astype(F32), qcos, qsin)
        kraw = qrecv[2 * g, :, 2 * HD :].astype(F32) + qrecv[2 * g + 1, :, 2 * HD :].astype(F32)
        knew = rope(kraw[None], kcos, ksin)
        vnew = qrecv[8 + 2 * g, :, 2 * HD :] + qrecv[9 + 2 * g, :, 2 * HD :]
        cols = pl.ds(pl.multiple_of(g * HD, HD), HD)
        s_old = dot(qg, kc[:, cols], NT) + seen_ref[...]
        s_new = dot(qg, knew, NT)
        s_new = (s_new.reshape(8, TOKS, TOKS) + allow_ref[...][None]).reshape(8 * TOKS, TOKS)
        top = jnp.maximum(
            jnp.max(s_old, axis=-1, keepdims=True), jnp.max(s_new, axis=-1, keepdims=True)
        )
        e_old = jnp.exp2((s_old - top) * (SCALE * LOG2E))
        e_new = jnp.exp2((s_new - top) * (SCALE * LOG2E))
        denom = jnp.sum(e_old, axis=-1, keepdims=True) + jnp.sum(e_new, axis=-1, keepdims=True)
        o = dot(e_old.astype(BF), vc[:, cols]) + dot(e_new.astype(BF), vnew)
        o = (o / denom).astype(BF)
        for i in range(4):
            to = 4 * g + i
            for j in range(2):
                r0 = (2 * i + j) * TOKS
                asend[to, :, HD * j : HD * (j + 1)] = o[r0 : r0 + TOKS]

            def send():
                remote(asend.at[to], ain.at[own], asem, ar.at[b], 2 * to + core).start()

            if off == 0:
                pl.when(to != chip)(send)
            else:
                send()

    for off in (2, 1, 3, 0):
        heads(off)
    ain[own] = asend[chip]
    loads[8].wait()
    turn_weights(wu, wut)

    loads[4].wait()
    come("wo", wo.at[pl.ds(other_lane, HD)])
    order = (bf, bp, bm, b)
    for k, b_ in enumerate(order):
        await_bytes(ain.at[pl.ds(b_ * 4, 3 if k == 3 else 4)], ar.at[b_])

    def share(a_):
        rows = jnp.concatenate([ain[b_ * 4 + a_] for b_ in order], axis=0)
        return dot(rows, wo[...])

    s1[...] = share(af).astype(BF).reshape(4, TOKS, D)
    top_half, low_half = pl.ds(0, 16), pl.ds(16, 16)
    for k in range(4):
        go(("s", k, 0), s1.at[k, top_half], r1.at[k, top_half], up_a)
        go(("s", k, 1), s1.at[k, low_half], r1.at[k, low_half], down_a)
    pup[...] = share(ap).reshape(4, TOKS, D)
    pdown[...] = share(am).reshape(4, TOKS, D)
    pown[...] = share(a).reshape(4, TOKS, D)

    for load in loads[2:4]:
        load.wait()
    line = lax.broadcasted_iota(jnp.int32, (2 * N, TOKS), 0)
    expert = line // 2
    named = jnp.zeros((2 * N, TOKS), F32)
    weight = jnp.zeros((2 * N, TOKS), F32)
    turn_lanes = lax.rem(HD - lax.rem(t, 4) * TOKS, HD)
    idv = pltpu.roll(ids[...], turn_lanes, 1)[:, 0:TOKS]
    gv = pltpu.roll(gates[...], turn_lanes, 1)[:, 0:TOKS]
    for k in range(8):
        hit = jnp.broadcast_to(idv[k : k + 1], (2 * N, TOKS)) == expert
        named = jnp.where(hit, 1.0, named)
        weight = weight + jnp.where(hit, jnp.broadcast_to(gv[k : k + 1], (2 * N, TOKS)), 0.0)
    before = dot(named.astype(BF), jnp.where(ri < ci, 1.0, 0.0).astype(BF))
    turn = lax.rem(line, 2).astype(F32)
    taken = (named > 0.5) & (jnp.abs(before - turn) < 0.5)
    sel_ref[...] = jnp.where(taken, 1.0, 0.0).astype(BF)
    comb_ref[...] = jnp.where(taken, weight, 0.0)

    for k in range(4):
        come(("s", k, 0), r1.at[k, top_half])
        s2[k, 0, 0:16] = (pup[k, 0:16] + r1[k, 0:16].astype(F32)).astype(BF)
        s2[k, 0, 16:32] = pup[k, 16:32].astype(BF)
        go(("t", k, 0), s2.at[k, 0], r2.at[k, 0], up_a)
        come(("s", k, 1), r1.at[k, low_half])
        s2[k, 1, 0:16] = pdown[k, 0:16].astype(BF)
        s2[k, 1, 16:32] = (pdown[k, 16:32] + r1[k, 16:32].astype(F32)).astype(BF)
        go(("t", k, 1), s2.at[k, 1], r2.at[k, 1], down_a)
    for k, b_ in enumerate(order):
        come(("t", k, 0), r2.at[k, 0])
        come(("t", k, 1), r2.at[k, 1])
        rs = pown[k] + r2[k, 0].astype(F32) + r2[k, 1].astype(F32)
        if k < 3:
            v1[k] = rs.astype(BF)
            go(("v", k), v1.at[k], v2.at[k], dev(a, b_))
        else:
            hid[...] = res[...].astype(F32) + rs
    for k in range(3):
        come(("v", k), v2.at[k])
    hidden = hid[...] + (v2[0].astype(F32) + v2[1].astype(F32) + v2[2].astype(F32))
    hid[...] = hidden
    inv = lax.rsqrt(jnp.mean(hidden * hidden, axis=-1, keepdims=True) + EPSILON)
    normed = (hidden * inv * ffn_gain[...][None, :]).astype(BF)

    picked = dot(sel_ref[...], normed)
    for j in range(16):
        fs[pl.ds(j, 64, stride=16), :] = picked[:, HD * j : HD * (j + 1)]
    dsend[...] = fs[...].astype(BF).reshape(N, 32, HD)

    def post(src, dst, ssem, rsem):
        for da, db in FAR_FIRST:
            for other in range(2):
                if (da, db, other) == (0, 0, 0):
                    continue
                to = dev(ring(a, da), ring(b, db)) + other * (1 - 2 * core)
                remote(src.at[to], dst.at[t], ssem, rsem, to).start()

    pl.semaphore_wait(meet, 1)
    post(dsend, drecv, ds, dr)
    drecv[t] = dsend[t]
    loads[9].wait()
    await_bytes(drecv.at[pl.ds(0, N - 1)], dr)
    fs[...] = drecv[...].reshape(1024, HD).astype(F32)
    for j in range(16):
        xs[:, HD * j : HD * (j + 1)] = fs[pl.ds(j, 64, stride=16), :].astype(BF)
    gate = dot(xs[...], wgt[...])
    up = dot(xs[...], wut[...])
    inner = (gate / (1.0 + jnp.exp(-gate)) * up).astype(BF)
    y = dot(inner, wd[...])
    for j in range(16):
        fs[pl.ds(j, 64, stride=16), :] = y[:, HD * j : HD * (j + 1)]
    ysend[...] = fs[...].astype(BF).reshape(N, 32, HD)
    post(ysend, yrecv, ys, yr)
    yrecv[t] = ysend[t]
    await_bytes(yrecv.at[pl.ds(0, N - 1)], yr)
    fs[...] = yrecv[...].reshape(1024, HD).astype(F32)
    comb = comb_ref[...]
    comb_hi = comb.astype(BF)
    comb_lo = (comb - comb_hi.astype(F32)).astype(BF)
    for j in range(16):
        yj = fs[pl.ds(j, 64, stride=16), :].astype(BF)
        moe = dot(comb_hi, yj, TN) + dot(comb_lo, yj, TN)
        cols = slice(HD * j, HD * (j + 1))
        out_ref[:, cols] = (hid[:, cols] + moe).astype(BF)

    for copy in sends:
        copy.wait_send()
    await_bytes(qsend.at[pl.ds(0, 15)], qs)
    await_bytes(asend.at[pl.ds(0, 15)], asem)
    await_bytes(dsend.at[pl.ds(0, N - 1)], ds)
    await_bytes(ysend.at[pl.ds(0, N - 1)], ys)


def body(
    residual_in, attn_gain, w_query, w_keyval, query_gain, key_gain, w_out, ffn_gain,
    w_gate, w_up, w_down, key_cache, value_cache, prefix_lens, accepted, accept_path,
    parents, slot_kinds, expert_ids, gate_probs,
):
    half = np.arange(HD // 2, dtype=np.float64)
    freq = np.exp(-(2.0 * half / HD) * math.log(ROPE_BASE)).astype(np.float32)
    freq = jnp.asarray(np.concatenate([freq, freq])[None, :])
    vmem = pl.BlockSpec(memory_space=pltpu.VMEM)
    sm = pltpu.SMEM
    hbm = pl.BlockSpec(memory_space=pltpu.HBM)
    dma = pltpu.SemaphoreType.DMA
    vm = pltpu.VMEM
    return pl.pallas_call(
        layer_kernel,
        out_shape=jax.ShapeDtypeStruct((TOKS, D), BF),
        in_specs=[hbm] * 21,
        out_specs=vmem,
        scratch_shapes=[
            vm((1, HD), F32),
            vm((D,), F32), vm((HD,), F32), vm((HD,), F32), vm((D,), F32),
            vm((1, TOKS), jnp.int32),
            sm((1,), jnp.int32), sm((1,), jnp.int32), sm((1, 8), jnp.int32), sm((1,), jnp.int32),
            vm((TOKS, D), BF),
            vm((D, 2 * HD), BF),
            vm((HD, D), BF),
            vm((2 * HD, D), BF),
            vm((FF, D), BF),
            vm((FF, D), BF),
            vm((FF, D), BF),
            vm((D, FF), BF),
            vm((D, FF), BF),
            vm((CACHE, 4 * HD), BF),
            vm((CACHE, 4 * HD), BF),
            vm((8, HD), jnp.int32),
            vm((8, HD), F32),
            vm((16, TOKS, D), BF),
            vm((16, TOKS, 3 * HD), BF),
            vm((16, TOKS, 3 * HD), BF),
            vm((16, TOKS, 2 * HD), BF),
            vm((16, TOKS, 2 * HD), BF),
            vm((4, TOKS, D), F32),
            vm((4, TOKS, D), F32),
            vm((4, TOKS, D), F32),
            vm((4, TOKS, D), BF),
            vm((4, TOKS, D), BF),
            vm((4, 2, TOKS, D), BF),
            vm((4, 2, TOKS, D), BF),
            vm((3, TOKS, D), BF),
            vm((3, TOKS, D), BF),
            vm((TOKS, D), F32),
            vm((1024, HD), F32),
            vm((2 * N, D), BF),
            vm((N, 32, HD), BF),
            vm((N, 32, HD), BF),
            vm((N, 32, HD), BF),
            vm((N, 32, HD), BF),
            vm((2 * N, TOKS), BF),
            vm((2 * N, TOKS), F32),
            vm((TOKS, HD), F32), vm((TOKS, HD), F32), vm((TOKS, HD), F32), vm((TOKS, HD), F32),
            vm((TOKS, TOKS), F32),
            vm((1, CACHE), F32),
            dma((11,)),
            dma((10,)),
            pltpu.SemaphoreType.REGULAR,
            dma((40,)), dma((40,)),
            dma(()), dma(()),
            dma(()), dma((4,)),
            dma(()), dma(()), dma(()), dma(()),
        ],
        compiler_params=pltpu.CompilerParams(
            collective_id=0, has_side_effects=True, vmem_limit_bytes=56 * 1024 * 1024
        ),
        name="layer",
    )(
        freq, attn_gain, query_gain, key_gain, ffn_gain, parents,
        prefix_lens, accepted, accept_path, slot_kinds,
        residual_in, w_query, w_keyval, w_out, w_gate, w_up, w_down,
        key_cache, value_cache, expert_ids.T, gate_probs.T,
    )


def solution(mesh):
    in_specs = (
        P(("group", "tensor"), None),
        P(),
        P(None, "tensor"),
        P("tensor", None),
        P(),
        P(),
        P("tensor", None),
        P(),
        P("tensor", None, None),
        P("tensor", None, None),
        P("tensor", None, None),
        P(("group", "tensor"), None, None),
        P(("group", "tensor"), None, None),
        P(("group", "tensor")),
        P(("group", "tensor")),
        P(("group", "tensor"), None),
        P(("group", "tensor"), None),
        P(("group", "tensor")),
        P("group", None),
        P("group", None),
    )
    out_specs = P(("group", "tensor"), None)
    return jax.shard_map(body, mesh=mesh, in_specs=in_specs, out_specs=out_specs, check_vma=False)
```

```python
import functools
import math

import jax
import jax.numpy as jnp
import numpy as np
from jax import lax
from jax.experimental import pallas as pl
from jax.experimental.pallas import tpu as pltpu
from jax.sharding import PartitionSpec as P

SINK = 4
WIN = 512
EPSILON = 1e-06
NEG_FILL = -1e30
ROPE_BASE = 1000000.0

N = 32
TOKS = 32
D = 2048
HD = 128
FF = 768
CACHE = 1024
SCALE = HD**-0.5
LOG2E = math.log2(math.e)

BF = jnp.bfloat16
F32 = jnp.float32
MESH = pl.DeviceIdType.MESH
FAR_FIRST = sorted(
    ((i, j) for i in range(4) for j in range(4)),
    key=lambda ij: -(min(ij[0], 4 - ij[0]) + min(ij[1], 4 - ij[1])),
)
NT = (((1,), (1,)), ((), ()))
TN = (((0,), (0,)), ((), ()))


def dot(a, b, dims=(((1,), (0,)), ((), ()))):
    return lax.dot_general(a, b, dims, preferred_element_type=F32)


def layer_kernel(
    freq_hbm, again_hbm, qgain_hbm, kgain_hbm, fgain_hbm, par_hbm, prefix_hbm, acc_hbm, path_hbm, kind_hbm,
    res_hbm, wq_hbm, wkv_hbm, wo_hbm, wg_hbm, wu_hbm, wd_hbm, kc_hbm, vc_hbm, ids_hbm, gates_hbm,
    out_ref,
    freq_ref, attn_gain, query_gain, key_gain, ffn_gain, parents, prefix, accepted, path, kind,
    res, wq, wkv, wo, wg, wu, wd, wgt, wut, kc, vc, ids, gates,
    ag, qsend, qrecv, asend, ain,
    pup, pdown, pown, s1, r1, s2, r2, v1, v2, hid,
    fs, xs, dsend, drecv, ysend, yrecv, sel_ref, comb_ref,
    qcos, qsin, kcos, ksin, allow_ref, seen_ref,
    lsem, isem, meet, snd, rcv, qs, qr, asem, ar, ds, dr, ys, yr,
):
    t = lax.axis_index("tensor")
    core = lax.rem(t, 2)
    chip = t // 2
    cx = chip // 4
    cy = lax.rem(chip, 4)
    a = cx * (1 - core) + cy * core
    b = cy * (1 - core) + cx * core
    step_a = 8 - 6 * core
    step_b = 2 + 6 * core

    def dev(a_, b_):
        return a_ * step_a + b_ * step_b + core

    def ring(v, k):
        return lax.rem(v + k, 4)

    def remote(src, dst, ssem, rsem, to):
        return pltpu.make_async_remote_copy(
            src_ref=src, dst_ref=dst, send_sem=ssem, recv_sem=rsem,
            device_id={"tensor": to}, device_id_type=MESH,
        )

    def await_bytes(ref, sem):
        pltpu.make_async_copy(ref, ref, sem).wait()

    sends = []
    slots = {}

    def slot(key):
        return slots.setdefault(key, len(slots))

    def go(key, src, dst, to):
        copy = remote(src, dst, snd.at[len(sends)], rcv.at[slot(key)], to)
        copy.start()
        sends.append(copy)

    def come(key, ref):
        await_bytes(ref, rcv.at[slot(key)])

    load_res = pltpu.make_async_copy(res_hbm, res, lsem.at[0])
    load_res.start()
    small = [
        pltpu.make_async_copy(src, dst, isem.at[i])
        for i, (src, dst) in enumerate(
            (
                (again_hbm, attn_gain), (freq_hbm, freq_ref), (qgain_hbm, query_gain),
                (kgain_hbm, key_gain), (fgain_hbm, ffn_gain), (par_hbm, parents),
                (prefix_hbm, prefix), (acc_hbm, accepted), (path_hbm, path), (kind_hbm, kind),
            )
        )
    ]
    small[0].start()
    wkv[...] = jnp.zeros_like(wkv)
    lane0 = pl.multiple_of(core * HD, HD)
    kv_row = pl.multiple_of(lax.rem(chip, 2) * 64 + core * 32, 32)
    lane_win = pl.multiple_of((t // 4) * HD, HD)
    loads = [
        pltpu.make_async_copy(wq_hbm, wq.at[:, pl.ds(lane0, HD)], lsem.at[1]),
        pltpu.make_async_copy(wkv_hbm, wkv.at[pl.ds(kv_row, 32)], lsem.at[2]),
        pltpu.make_async_copy(ids_hbm.at[:, pl.ds(lane_win, HD)], ids, lsem.at[3]),
        pltpu.make_async_copy(gates_hbm.at[:, pl.ds(lane_win, HD)], gates, lsem.at[4]),
        pltpu.make_async_copy(wo_hbm, wo.at[pl.ds(lane0, HD)], lsem.at[5]),
        pltpu.make_async_copy(kc_hbm.at[0], kc, lsem.at[6]),
        pltpu.make_async_copy(vc_hbm.at[0], vc, lsem.at[7]),
        pltpu.make_async_copy(wg_hbm.at[0], wg, lsem.at[8]),
        pltpu.make_async_copy(wu_hbm.at[0], wu, lsem.at[9]),
        pltpu.make_async_copy(wd_hbm.at[0], wd, lsem.at[10]),
    ]
    for load in loads[2:4] + small[1:] + loads[:2] + loads[4:]:
        load.start()

    barrier = pltpu.get_barrier_semaphore()

    sibling = t + 1 - 2 * core
    line = [dev(ring(a, k), b) for k in (1, 2, 3)] + [dev(a, ring(b, k)) for k in (1, 2, 3)]
    for to in line + [sibling]:
        pl.semaphore_signal(barrier, inc=1, device_id={"tensor": to}, device_id_type=MESH)

    load_res.wait()
    small[0].wait()
    own = b * 4 + a
    xv = res[...].astype(F32)
    inv = lax.rsqrt(jnp.mean(xv * xv, axis=-1, keepdims=True) + EPSILON)
    ag[own] = (xv * inv * attn_gain[...][None, :]).astype(BF)

    pl.semaphore_wait(barrier, 7)

    up_a, down_a = dev(ring(a, 1), b), dev(ring(a, 3), b)
    up_b, down_b = dev(a, ring(b, 1)), dev(a, ring(b, 3))

    def blk(a_, b_):
        return ag.at[b_ * 4 + a_]

    def half(a_, b_, h):
        return ag.at[b_ * 4 + a_, pl.ds(16 * h, 16)]

    def spread_b(j, a_):
        go(("b", j, 0), blk(a_, b), blk(a_, b), up_b)
        go(("b", j, 1), blk(a_, b), blk(a_, b), down_b)

    am, ap, af = ring(a, 3), ring(a, 1), ring(a, 2)
    bm, bp, bf = ring(b, 3), ring(b, 1), ring(b, 2)
    go(("a", 0), blk(a, b), blk(a, b), up_a)
    go(("a", 1), blk(a, b), blk(a, b), down_a)
    spread_b(0, a)
    go(("a", 2), blk(a, b), blk(a, b), dev(af, b))
    go("wq", wq_hbm, wq.at[:, pl.ds(lane0, HD)], sibling)
    go("wkv", wkv_hbm, wkv.at[pl.ds(kv_row, 32)], sibling)
    go("wo", wo_hbm, wo.at[pl.ds(lane0, HD)], sibling)

    for load in small[1:]:
        load.wait()
    ri = lax.broadcasted_iota(jnp.int32, (TOKS, TOKS), 0)
    ci = lax.broadcasted_iota(jnp.int32, (TOKS, TOKS), 1)
    link = jnp.where((ri == jnp.broadcast_to(parents[...], (TOKS, TOKS))) | (ri == ci), 1.0, 0.0)
    for unused in range(5):
        link = jnp.minimum(dot(link.astype(BF), link.astype(BF)), 1.0)
    eye = jnp.where(ri == ci, 1.0, 0.0).astype(BF)
    reach = dot(link.astype(BF), eye, TN)
    allowed = jnp.where(kind[0] == 1, reach, jnp.where(ci <= ri, 1.0, 0.0))
    allow_ref[...] = jnp.where(allowed > 0.5, 0.0, NEG_FILL)
    depth = jnp.sum(allowed, axis=1, keepdims=True) - 1.0
    total = prefix[0] + accepted[0]
    angle = (total.astype(F32) + depth) * freq_ref[...]
    cosine = jnp.cos(angle)
    lane = lax.broadcasted_iota(jnp.int32, (TOKS, HD), 1)
    sine = jnp.sin(angle)
    sine = jnp.where(lane < HD // 2, -sine, sine)
    for gain_ref, cos_ref, sin_ref in ((query_gain, qcos, qsin), (key_gain, kcos, ksin)):
        gain = jnp.broadcast_to(gain_ref[...][None, :], (TOKS, HD))
        cos_ref[...] = cosine * gain
        sin_ref[...] = sine * pltpu.roll(gain, HD // 2, 1)
    row = lax.broadcasted_iota(jnp.int32, (1, CACHE), 1)
    seen = (row < prefix[0]) & ((row < SINK) | (row >= total - WIN))
    for m in range(8):
        seen = seen | ((row == prefix[0] + path[0, m]) & (accepted[0] > m))
    seen_ref[...] = jnp.where(seen, 0.0, NEG_FILL)

    come(("a", 0), blk(am, b))
    spread_b(1, am)
    come(("a", 1), blk(ap, b))
    spread_b(2, ap)

    def relay_b(j, a_):
        come(("b", j, 0), blk(a_, bm))
        go(("bh", j, 0), half(a_, bm, 0), half(a_, bm, 0), up_b)
        come(("b", j, 1), blk(a_, bp))
        go(("bh", j, 1), half(a_, bp, 1), half(a_, bp, 1), down_b)

    relay_b(0, a)
    come(("a", 2), blk(af, b))
    spread_b(3, af)
    go(("b", 3, 2), blk(af, b), blk(af, b), dev(a, bf))

    for load in loads[:2]:
        load.wait()
    other_lane = pl.multiple_of(HD - core * HD, HD)
    other_row = pl.multiple_of(lax.rem(chip, 2) * 64 + 32 - core * 32, 32)
    come("wq", wq.at[:, pl.ds(other_lane, HD)])
    come("wkv", wkv.at[pl.ds(other_row, 32)])

    def project(blocks):
        count = len(blocks)
        rows = jnp.concatenate([ag[b_ * 4 + a_] for a_, b_ in blocks], axis=0)
        q = dot(rows, wq[...]).astype(BF)
        kv = dot(rows, wkv[...], NT).astype(BF)
        for i in range(count):
            a_, b_ = blocks[i]
            r = slice(TOKS * i, TOKS * (i + 1))
            qsend[b_ * 4 + a_, :, 0 : 2 * HD] = q[r]
            qsend[b_ * 4 + a_, :, 2 * HD :] = kv[r]

    def post_queries(blocks):
        for a_, b_ in blocks:
            remote(qsend.at[b_ * 4 + a_], qrecv.at[chip], qs, qr, dev(a_, b_)).start()

    near = [(af, b), (ap, b), (am, b)]
    project(near + [(a, b)])
    qrecv[chip] = qsend[own]
    post_queries(near)

    relay_b(1, am)
    relay_b(2, ap)
    near = [(a_, b_) for a_ in (ap, am, a) for b_ in (bm, bp)]
    project(near)
    post_queries(near)
    come(("b", 3, 0), blk(af, bm))
    come(("b", 3, 1), blk(af, bp))
    for j, a_ in enumerate((a, am, ap)):
        come(("bh", j, 0), half(a_, bf, 0))
        come(("bh", j, 1), half(a_, bf, 1))
    come(("b", 3, 2), blk(af, bf))
    rest = [(af, bf), (ap, bf), (am, bf), (af, bm), (af, bp), (a, bf)]
    pl.semaphore_signal(meet, inc=1, device_id={"tensor": sibling}, device_id_type=MESH)
    project(rest)
    post_queries(rest)

    def turn_weights(src, dst):
        for i in range(FF // HD):
            dst[:, HD * i : HD * (i + 1)] = src[HD * i : HD * (i + 1), :].T

    loads[7].wait()
    turn_weights(wg, wgt)

    for load in loads[5:7]:
        load.wait()
    await_bytes(qrecv.at[pl.ds(0, 15)], qr)

    ones = jnp.ones((HD, HD), BF)

    def rope(v, cosv, sinv):
        count = v.shape[0]
        v = v.reshape(count * TOKS, HD)
        square = v * v
        upper = square.astype(BF)
        lower = (square - upper.astype(F32)).astype(BF)
        mean = (dot(upper, ones) + dot(lower, ones)) * (1.0 / HD)
        turned = (
            v.reshape(count, TOKS, HD) * cosv[...][None]
            + pltpu.roll(v, HD // 2, 1).reshape(count, TOKS, HD) * sinv[...][None]
        )
        return (turned.reshape(count * TOKS, HD) * lax.rsqrt(mean + EPSILON)).astype(BF)

    def heads(off):
        g = ring(cx, off)
        qraw = [
            qrecv[4 * g + i, :, HD * j : HD * (j + 1)] for i in range(4) for j in range(2)
        ]
        qg = rope(jnp.stack(qraw, axis=0).astype(F32), qcos, qsin)
        kraw = qrecv[2 * g, :, 2 * HD :].astype(F32) + qrecv[2 * g + 1, :, 2 * HD :].astype(F32)
        knew = rope(kraw[None], kcos, ksin)
        vnew = qrecv[8 + 2 * g, :, 2 * HD :] + qrecv[9 + 2 * g, :, 2 * HD :]
        cols = pl.ds(pl.multiple_of(g * HD, HD), HD)
        s_old = dot(qg, kc[:, cols], NT) + seen_ref[...]
        s_new = dot(qg, knew, NT)
        s_new = (s_new.reshape(8, TOKS, TOKS) + allow_ref[...][None]).reshape(8 * TOKS, TOKS)
        top = jnp.maximum(
            jnp.max(s_old, axis=-1, keepdims=True), jnp.max(s_new, axis=-1, keepdims=True)
        )
        e_old = jnp.exp2((s_old - top) * (SCALE * LOG2E))
        e_new = jnp.exp2((s_new - top) * (SCALE * LOG2E))
        denom = jnp.sum(e_old, axis=-1, keepdims=True) + jnp.sum(e_new, axis=-1, keepdims=True)
        o = dot(e_old.astype(BF), vc[:, cols]) + dot(e_new.astype(BF), vnew)
        o = (o / denom).astype(BF)
        for i in range(4):
            to = 4 * g + i
            for j in range(2):
                r0 = (2 * i + j) * TOKS
                asend[to, :, HD * j : HD * (j + 1)] = o[r0 : r0 + TOKS]

            def send():
                remote(asend.at[to], ain.at[own], asem, ar.at[b], 2 * to + core).start()

            if off == 0:
                pl.when(to != chip)(send)
            else:
                send()

    for off in (2, 1, 3, 0):
        heads(off)
    ain[own] = asend[chip]
    loads[8].wait()
    turn_weights(wu, wut)

    loads[4].wait()
    come("wo", wo.at[pl.ds(other_lane, HD)])
    order = (bf, bp, bm, b)
    for k, b_ in enumerate(order):
        await_bytes(ain.at[pl.ds(b_ * 4, 3 if k == 3 else 4)], ar.at[b_])

    def share(a_):
        rows = jnp.concatenate([ain[b_ * 4 + a_] for b_ in order], axis=0)
        return dot(rows, wo[...])

    s1[...] = share(af).astype(BF).reshape(4, TOKS, D)
    top_half, low_half = pl.ds(0, 16), pl.ds(16, 16)
    for k in range(4):
        go(("s", k, 0), s1.at[k, top_half], r1.at[k, top_half], up_a)
        go(("s", k, 1), s1.at[k, low_half], r1.at[k, low_half], down_a)
    pup[...] = share(ap).reshape(4, TOKS, D)
    pdown[...] = share(am).reshape(4, TOKS, D)
    pown[...] = share(a).reshape(4, TOKS, D)

    for load in loads[2:4]:
        load.wait()
    line = lax.broadcasted_iota(jnp.int32, (2 * N, TOKS), 0)
    expert = line // 2
    named = jnp.zeros((2 * N, TOKS), F32)
    weight = jnp.zeros((2 * N, TOKS), F32)
    turn_lanes = lax.rem(HD - lax.rem(t, 4) * TOKS, HD)
    idv = pltpu.roll(ids[...], turn_lanes, 1)[:, 0:TOKS]
    gv = pltpu.roll(gates[...], turn_lanes, 1)[:, 0:TOKS]
    for k in range(8):
        hit = jnp.broadcast_to(idv[k : k + 1], (2 * N, TOKS)) == expert
        named = jnp.where(hit, 1.0, named)
        weight = weight + jnp.where(hit, jnp.broadcast_to(gv[k : k + 1], (2 * N, TOKS)), 0.0)
    before = dot(named.astype(BF), jnp.where(ri < ci, 1.0, 0.0).astype(BF))
    turn = lax.rem(line, 2).astype(F32)
    taken = (named > 0.5) & (jnp.abs(before - turn) < 0.5)
    sel_ref[...] = jnp.where(taken, 1.0, 0.0).astype(BF)
    comb_ref[...] = jnp.where(taken, weight, 0.0)

    for k in range(4):
        come(("s", k, 0), r1.at[k, top_half])
        s2[k, 0, 0:16] = (pup[k, 0:16] + r1[k, 0:16].astype(F32)).astype(BF)
        s2[k, 0, 16:32] = pup[k, 16:32].astype(BF)
        go(("t", k, 0), s2.at[k, 0], r2.at[k, 0], up_a)
        come(("s", k, 1), r1.at[k, low_half])
        s2[k, 1, 0:16] = pdown[k, 0:16].astype(BF)
        s2[k, 1, 16:32] = (pdown[k, 16:32] + r1[k, 16:32].astype(F32)).astype(BF)
        go(("t", k, 1), s2.at[k, 1], r2.at[k, 1], down_a)
    for k, b_ in enumerate(order):
        come(("t", k, 0), r2.at[k, 0])
        come(("t", k, 1), r2.at[k, 1])
        rs = pown[k] + r2[k, 0].astype(F32) + r2[k, 1].astype(F32)
        if k < 3:
            v1[k] = rs.astype(BF)
            go(("v", k), v1.at[k], v2.at[k], dev(a, b_))
        else:
            hid[...] = res[...].astype(F32) + rs
    for k in range(3):
        come(("v", k), v2.at[k])
    hidden = hid[...] + (v2[0].astype(F32) + v2[1].astype(F32) + v2[2].astype(F32))
    hid[...] = hidden
    inv = lax.rsqrt(jnp.mean(hidden * hidden, axis=-1, keepdims=True) + EPSILON)
    normed = (hidden * inv * ffn_gain[...][None, :]).astype(BF)

    picked = dot(sel_ref[...], normed)
    for j in range(16):
        fs[pl.ds(j, 64, stride=16), :] = picked[:, HD * j : HD * (j + 1)]
    dsend[...] = fs[...].astype(BF).reshape(N, 32, HD)

    def post(src, dst, ssem, rsem):
        for da, db in FAR_FIRST:
            for other in range(2):
                if (da, db, other) == (0, 0, 0):
                    continue
                to = dev(ring(a, da), ring(b, db)) + other * (1 - 2 * core)
                remote(src.at[to], dst.at[t], ssem, rsem, to).start()

    pl.semaphore_wait(meet, 1)
    post(dsend, drecv, ds, dr)
    drecv[t] = dsend[t]
    loads[9].wait()
    await_bytes(drecv.at[pl.ds(0, N - 1)], dr)
    fs[...] = drecv[...].reshape(1024, HD).astype(F32)
    for j in range(16):
        xs[:, HD * j : HD * (j + 1)] = fs[pl.ds(j, 64, stride=16), :].astype(BF)
    gate = dot(xs[...], wgt[...])
    up = dot(xs[...], wut[...])
    inner = (gate / (1.0 + jnp.exp(-gate)) * up).astype(BF)
    y = dot(inner, wd[...])
    for j in range(16):
        fs[pl.ds(j, 64, stride=16), :] = y[:, HD * j : HD * (j + 1)]
    ysend[...] = fs[...].astype(BF).reshape(N, 32, HD)
    post(ysend, yrecv, ys, yr)
    yrecv[t] = ysend[t]
    for copy in sends:
        copy.wait_send()
    await_bytes(qsend.at[pl.ds(0, 15)], qs)
    await_bytes(asend.at[pl.ds(0, 15)], asem)
    await_bytes(dsend.at[pl.ds(0, N - 1)], ds)
    comb = comb_ref[...]
    comb_hi = comb.astype(BF)
    comb_lo = (comb - comb_hi.astype(F32)).astype(BF)
    await_bytes(yrecv.at[pl.ds(0, N - 1)], yr)
    fs[...] = yrecv[...].reshape(1024, HD).astype(F32)
    for j in range(16):
        yj = fs[pl.ds(j, 64, stride=16), :].astype(BF)
        moe = dot(comb_hi, yj, TN) + dot(comb_lo, yj, TN)
        cols = slice(HD * j, HD * (j + 1))
        out_ref[:, cols] = (hid[:, cols] + moe).astype(BF)
    await_bytes(ysend.at[pl.ds(0, N - 1)], ys)


def body(
    residual_in, attn_gain, w_query, w_keyval, query_gain, key_gain, w_out, ffn_gain,
    w_gate, w_up, w_down, key_cache, value_cache, prefix_lens, accepted, accept_path,
    parents, slot_kinds, expert_ids, gate_probs,
):
    half = np.arange(HD // 2, dtype=np.float64)
    freq = np.exp(-(2.0 * half / HD) * math.log(ROPE_BASE)).astype(np.float32)
    freq = jnp.asarray(np.concatenate([freq, freq])[None, :])
    vmem = pl.BlockSpec(memory_space=pltpu.VMEM)
    sm = pltpu.SMEM
    hbm = pl.BlockSpec(memory_space=pltpu.HBM)
    dma = pltpu.SemaphoreType.DMA
    vm = pltpu.VMEM
    return pl.pallas_call(
        layer_kernel,
        out_shape=pltpu.VMEM((TOKS, D), BF),
        in_specs=[hbm] * 21,
        out_specs=vmem,
        scratch_shapes=[
            vm((1, HD), F32),
            vm((D,), F32), vm((HD,), F32), vm((HD,), F32), vm((D,), F32),
            vm((1, TOKS), jnp.int32),
            sm((1,), jnp.int32), sm((1,), jnp.int32), sm((1, 8), jnp.int32), sm((1,), jnp.int32),
            vm((TOKS, D), BF),
            vm((D, 2 * HD), BF),
            vm((HD, D), BF),
            vm((2 * HD, D), BF),
            vm((FF, D), BF),
            vm((FF, D), BF),
            vm((FF, D), BF),
            vm((D, FF), BF),
            vm((D, FF), BF),
            vm((CACHE, 4 * HD), BF),
            vm((CACHE, 4 * HD), BF),
            vm((8, HD), jnp.int32),
            vm((8, HD), F32),
            vm((16, TOKS, D), BF),
            vm((16, TOKS, 3 * HD), BF),
            vm((16, TOKS, 3 * HD), BF),
            vm((16, TOKS, 2 * HD), BF),
            vm((16, TOKS, 2 * HD), BF),
            vm((4, TOKS, D), F32),
            vm((4, TOKS, D), F32),
            vm((4, TOKS, D), F32),
            vm((4, TOKS, D), BF),
            vm((4, TOKS, D), BF),
            vm((4, 2, TOKS, D), BF),
            vm((4, 2, TOKS, D), BF),
            vm((3, TOKS, D), BF),
            vm((3, TOKS, D), BF),
            vm((TOKS, D), F32),
            vm((1024, HD), F32),
            vm((2 * N, D), BF),
            vm((N, 32, HD), BF),
            vm((N, 32, HD), BF),
            vm((N, 32, HD), BF),
            vm((N, 32, HD), BF),
            vm((2 * N, TOKS), BF),
            vm((2 * N, TOKS), F32),
            vm((TOKS, HD), F32), vm((TOKS, HD), F32), vm((TOKS, HD), F32), vm((TOKS, HD), F32),
            vm((TOKS, TOKS), F32),
            vm((1, CACHE), F32),
            dma((11,)),
            dma((10,)),
            pltpu.SemaphoreType.REGULAR,
            dma((40,)), dma((40,)),
            dma(()), dma(()),
            dma(()), dma((4,)),
            dma(()), dma(()), dma(()), dma(()),
        ],
        compiler_params=pltpu.CompilerParams(
            collective_id=0, has_side_effects=True, vmem_limit_bytes=56 * 1024 * 1024
        ),
        name="layer",
    )(
        freq, attn_gain, query_gain, key_gain, ffn_gain, parents,
        prefix_lens, accepted, accept_path, slot_kinds,
        residual_in, w_query, w_keyval, w_out, w_gate, w_up, w_down,
        key_cache, value_cache, expert_ids.T, gate_probs.T,
    )


def solution(mesh):
    in_specs = (
        P(("group", "tensor"), None),
        P(),
        P(None, "tensor"),
        P("tensor", None),
        P(),
        P(),
        P("tensor", None),
        P(),
        P("tensor", None, None),
        P("tensor", None, None),
        P("tensor", None, None),
        P(("group", "tensor"), None, None),
        P(("group", "tensor"), None, None),
        P(("group", "tensor")),
        P(("group", "tensor")),
        P(("group", "tensor"), None),
        P(("group", "tensor"), None),
        P(("group", "tensor")),
        P("group", None),
        P("group", None),
    )
    out_specs = P(("group", "tensor"), None)
    return jax.shard_map(body, mesh=mesh, in_specs=in_specs, out_specs=out_specs, check_vma=False)
```

```python
import functools
import math

import jax
import jax.numpy as jnp
import numpy as np
from jax import lax
from jax.experimental import pallas as pl
from jax.experimental.pallas import tpu as pltpu
from jax.sharding import PartitionSpec as P

SINK = 4
WIN = 512
EPSILON = 1e-06
NEG_FILL = -1e30
ROPE_BASE = 1000000.0

N = 32
TOKS = 32
D = 2048
HD = 128
FF = 768
CACHE = 1024
SCALE = HD**-0.5
LOG2E = math.log2(math.e)

BF = jnp.bfloat16
F32 = jnp.float32
MESH = pl.DeviceIdType.MESH
FAR_FIRST = sorted(
    ((i, j) for i in range(4) for j in range(4)),
    key=lambda ij: -(min(ij[0], 4 - ij[0]) + min(ij[1], 4 - ij[1])),
)
NT = (((1,), (1,)), ((), ()))
TN = (((0,), (0,)), ((), ()))


def dot(a, b, dims=(((1,), (0,)), ((), ()))):
    return lax.dot_general(a, b, dims, preferred_element_type=F32)


def layer_kernel(
    freq_hbm, again_hbm, qgain_hbm, kgain_hbm, fgain_hbm, par_hbm, prefix_hbm, acc_hbm, path_hbm, kind_hbm,
    res_hbm, wq_hbm, wkv_hbm, wo_hbm, wg_hbm, wu_hbm, wd_hbm, kc_hbm, vc_hbm, ids_hbm, gates_hbm,
    out_ref,
    freq_ref, attn_gain, query_gain, key_gain, ffn_gain, parents, prefix, accepted, path, kind,
    res, wq, wkv, wo, wg, wu, wd, wgt, wut, kc, vc, ids, gates,
    ag, qsend, qrecv, asend, ain,
    pup, pdown, pown, s1, r1, s2, r2, v1, v2, hid,
    fs, xs, dsend, drecv, ysend, yrecv, sel_ref, comb_ref,
    qcos, qsin, kcos, ksin, allow_ref, seen_ref,
    lsem, isem, meet, snd, rcv, qs, qr, asem, ar, ds, dr, ys, yr,
):
    t = lax.axis_index("tensor")
    core = lax.rem(t, 2)
    chip = t // 2
    cx = chip // 4
    cy = lax.rem(chip, 4)
    a = cx * (1 - core) + cy * core
    b = cy * (1 - core) + cx * core
    step_a = 8 - 6 * core
    step_b = 2 + 6 * core

    def dev(a_, b_):
        return a_ * step_a + b_ * step_b + core

    def ring(v, k):
        return lax.rem(v + k, 4)

    def remote(src, dst, ssem, rsem, to):
        return pltpu.make_async_remote_copy(
            src_ref=src, dst_ref=dst, send_sem=ssem, recv_sem=rsem,
            device_id={"tensor": to}, device_id_type=MESH,
        )

    def await_bytes(ref, sem):
        pltpu.make_async_copy(ref, ref, sem).wait()

    sends = []
    slots = {}

    def slot(key):
        return slots.setdefault(key, len(slots))

    def go(key, src, dst, to):
        copy = remote(src, dst, snd.at[len(sends)], rcv.at[slot(key)], to)
        copy.start()
        sends.append(copy)

    def come(key, ref):
        await_bytes(ref, rcv.at[slot(key)])

    load_res = pltpu.make_async_copy(res_hbm, res, lsem.at[0])
    load_res.start()
    small = [
        pltpu.make_async_copy(src, dst, isem.at[i])
        for i, (src, dst) in enumerate(
            (
                (again_hbm, attn_gain), (freq_hbm, freq_ref), (qgain_hbm, query_gain),
                (kgain_hbm, key_gain), (fgain_hbm, ffn_gain), (par_hbm, parents),
                (prefix_hbm, prefix), (acc_hbm, accepted), (path_hbm, path), (kind_hbm, kind),
            )
        )
    ]
    small[0].start()
    wkv[...] = jnp.zeros_like(wkv)
    lane0 = pl.multiple_of(core * HD, HD)
    kv_row = pl.multiple_of(lax.rem(chip, 2) * 64 + core * 32, 32)
    lane_win = pl.multiple_of((t // 4) * HD, HD)
    loads = [
        pltpu.make_async_copy(wq_hbm, wq.at[:, pl.ds(lane0, HD)], lsem.at[1]),
        pltpu.make_async_copy(wkv_hbm, wkv.at[pl.ds(kv_row, 32)], lsem.at[2]),
        pltpu.make_async_copy(ids_hbm.at[:, pl.ds(lane_win, HD)], ids, lsem.at[3]),
        pltpu.make_async_copy(gates_hbm.at[:, pl.ds(lane_win, HD)], gates, lsem.at[4]),
        pltpu.make_async_copy(wo_hbm, wo.at[pl.ds(lane0, HD)], lsem.at[5]),
        pltpu.make_async_copy(kc_hbm.at[0], kc, lsem.at[6]),
        pltpu.make_async_copy(vc_hbm.at[0], vc, lsem.at[7]),
        pltpu.make_async_copy(wg_hbm.at[0], wg, lsem.at[8]),
        pltpu.make_async_copy(wu_hbm.at[0], wu, lsem.at[9]),
        pltpu.make_async_copy(wd_hbm.at[0], wd, lsem.at[10]),
    ]
    for load in loads[2:4] + small[1:] + loads[:2] + loads[4:]:
        load.start()

    barrier = pltpu.get_barrier_semaphore()

    sibling = t + 1 - 2 * core
    line = [dev(ring(a, k), b) for k in (1, 2, 3)] + [dev(a, ring(b, k)) for k in (1, 2, 3)]
    for to in line + [sibling]:
        pl.semaphore_signal(barrier, inc=1, device_id={"tensor": to}, device_id_type=MESH)

    load_res.wait()
    small[0].wait()
    own = b * 4 + a
    xv = res[...].astype(F32)
    inv = lax.rsqrt(jnp.mean(xv * xv, axis=-1, keepdims=True) + EPSILON)
    ag[own] = (xv * inv * attn_gain[...][None, :]).astype(BF)

    pl.semaphore_wait(barrier, 7)

    up_a, down_a = dev(ring(a, 1), b), dev(ring(a, 3), b)
    up_b, down_b = dev(a, ring(b, 1)), dev(a, ring(b, 3))

    def blk(a_, b_):
        return ag.at[b_ * 4 + a_]

    def half(a_, b_, h):
        return ag.at[b_ * 4 + a_, pl.ds(16 * h, 16)]

    def spread_b(j, a_):
        go(("b", j, 0), blk(a_, b), blk(a_, b), up_b)
        go(("b", j, 1), blk(a_, b), blk(a_, b), down_b)

    am, ap, af = ring(a, 3), ring(a, 1), ring(a, 2)
    bm, bp, bf = ring(b, 3), ring(b, 1), ring(b, 2)
    go(("a", 0), blk(a, b), blk(a, b), up_a)
    go(("a", 1), blk(a, b), blk(a, b), down_a)
    go(("a", 2), blk(a, b), blk(a, b), dev(af, b))
    spread_b(0, a)
    go("wq", wq_hbm, wq.at[:, pl.ds(lane0, HD)], sibling)
    go("wkv", wkv_hbm, wkv.at[pl.ds(kv_row, 32)], sibling)
    go("wo", wo_hbm, wo.at[pl.ds(lane0, HD)], sibling)

    for load in small[1:]:
        load.wait()
    ri = lax.broadcasted_iota(jnp.int32, (TOKS, TOKS), 0)
    ci = lax.broadcasted_iota(jnp.int32, (TOKS, TOKS), 1)
    link = jnp.where((ri == jnp.broadcast_to(parents[...], (TOKS, TOKS))) | (ri == ci), 1.0, 0.0)
    for unused in range(5):
        link = jnp.minimum(dot(link.astype(BF), link.astype(BF)), 1.0)
    eye = jnp.where(ri == ci, 1.0, 0.0).astype(BF)
    reach = dot(link.astype(BF), eye, TN)
    allowed = jnp.where(kind[0] == 1, reach, jnp.where(ci <= ri, 1.0, 0.0))
    allow_ref[...] = jnp.where(allowed > 0.5, 0.0, NEG_FILL)
    depth = jnp.sum(allowed, axis=1, keepdims=True) - 1.0
    total = prefix[0] + accepted[0]
    angle = (total.astype(F32) + depth) * freq_ref[...]
    cosine = jnp.cos(angle)
    lane = lax.broadcasted_iota(jnp.int32, (TOKS, HD), 1)
    sine = jnp.sin(angle)
    sine = jnp.where(lane < HD // 2, -sine, sine)
    for gain_ref, cos_ref, sin_ref in ((query_gain, qcos, qsin), (key_gain, kcos, ksin)):
        gain = jnp.broadcast_to(gain_ref[...][None, :], (TOKS, HD))
        cos_ref[...] = cosine * gain
        sin_ref[...] = sine * pltpu.roll(gain, HD // 2, 1)
    row = lax.broadcasted_iota(jnp.int32, (1, CACHE), 1)
    seen = (row < prefix[0]) & ((row < SINK) | (row >= total - WIN))
    for m in range(8):
        seen = seen | ((row == prefix[0] + path[0, m]) & (accepted[0] > m))
    seen_ref[...] = jnp.where(seen, 0.0, NEG_FILL)

    come(("a", 0), blk(am, b))
    spread_b(1, am)
    come(("a", 1), blk(ap, b))
    spread_b(2, ap)

    def relay_b(j, a_):
        come(("b", j, 0), blk(a_, bm))
        go(("bh", j, 0), half(a_, bm, 0), half(a_, bm, 0), up_b)
        come(("b", j, 1), blk(a_, bp))
        go(("bh", j, 1), half(a_, bp, 1), half(a_, bp, 1), down_b)

    relay_b(0, a)
    come(("a", 2), blk(af, b))
    spread_b(3, af)
    go(("b", 3, 2), blk(af, b), blk(af, b), dev(a, bf))

    for load in loads[:2]:
        load.wait()
    other_lane = pl.multiple_of(HD - core * HD, HD)
    other_row = pl.multiple_of(lax.rem(chip, 2) * 64 + 32 - core * 32, 32)
    come("wq", wq.at[:, pl.ds(other_lane, HD)])
    come("wkv", wkv.at[pl.ds(other_row, 32)])

    def project(blocks):
        count = len(blocks)
        rows = jnp.concatenate([ag[b_ * 4 + a_] for a_, b_ in blocks], axis=0)
        q = dot(rows, wq[...]).astype(BF)
        kv = dot(rows, wkv[...], NT).astype(BF)
        for i in range(count):
            a_, b_ = blocks[i]
            r = slice(TOKS * i, TOKS * (i + 1))
            qsend[b_ * 4 + a_, :, 0 : 2 * HD] = q[r]
            qsend[b_ * 4 + a_, :, 2 * HD :] = kv[r]

    def post_queries(blocks):
        for a_, b_ in blocks:
            remote(qsend.at[b_ * 4 + a_], qrecv.at[chip], qs, qr, dev(a_, b_)).start()

    near = [(af, b), (ap, b), (am, b)]
    project(near + [(a, b)])
    qrecv[chip] = qsend[own]
    post_queries(near)

    relay_b(1, am)
    relay_b(2, ap)
    near = [(a_, b_) for a_ in (ap, am, a) for b_ in (bm, bp)]
    project(near)
    post_queries(near)
    come(("b", 3, 0), blk(af, bm))
    come(("b", 3, 1), blk(af, bp))
    for j, a_ in enumerate((a, am, ap)):
        come(("bh", j, 0), half(a_, bf, 0))
        come(("bh", j, 1), half(a_, bf, 1))
    come(("b", 3, 2), blk(af, bf))
    rest = [(af, bf), (ap, bf), (am, bf), (af, bm), (af, bp), (a, bf)]
    pl.semaphore_signal(meet, inc=1, device_id={"tensor": sibling}, device_id_type=MESH)
    project(rest)
    post_queries(rest)

    def turn_weights(src, dst):
        for i in range(FF // HD):
            dst[:, HD * i : HD * (i + 1)] = src[HD * i : HD * (i + 1), :].T

    loads[7].wait()
    turn_weights(wg, wgt)

    for load in loads[5:7]:
        load.wait()
    await_bytes(qrecv.at[pl.ds(0, 15)], qr)

    ones = jnp.ones((HD, HD), BF)

    def rope(v, cosv, sinv):
        count = v.shape[0]
        v = v.reshape(count * TOKS, HD)
        square = v * v
        upper = square.astype(BF)
        lower = (square - upper.astype(F32)).astype(BF)
        mean = (dot(upper, ones) + dot(lower, ones)) * (1.0 / HD)
        turned = (
            v.reshape(count, TOKS, HD) * cosv[...][None]
            + pltpu.roll(v, HD // 2, 1).reshape(count, TOKS, HD) * sinv[...][None]
        )
        return (turned.reshape(count * TOKS, HD) * lax.rsqrt(mean + EPSILON)).astype(BF)

    def heads(off):
        g = ring(cx, off)
        qraw = [
            qrecv[4 * g + i, :, HD * j : HD * (j + 1)] for i in range(4) for j in range(2)
        ]
        qg = rope(jnp.stack(qraw, axis=0).astype(F32), qcos, qsin)
        kraw = qrecv[2 * g, :, 2 * HD :].astype(F32) + qrecv[2 * g + 1, :, 2 * HD :].astype(F32)
        knew = rope(kraw[None], kcos, ksin)
        vnew = qrecv[8 + 2 * g, :, 2 * HD :] + qrecv[9 + 2 * g, :, 2 * HD :]
        cols = pl.ds(pl.multiple_of(g * HD, HD), HD)
        s_old = dot(qg, kc[:, cols], NT) + seen_ref[...]
        s_new = dot(qg, knew, NT)
        s_new = (s_new.reshape(8, TOKS, TOKS) + allow_ref[...][None]).reshape(8 * TOKS, TOKS)
        top = jnp.maximum(
            jnp.max(s_old, axis=-1, keepdims=True), jnp.max(s_new, axis=-1, keepdims=True)
        )
        e_old = jnp.exp2((s_old - top) * (SCALE * LOG2E))
        e_new = jnp.exp2((s_new - top) * (SCALE * LOG2E))
        denom = jnp.sum(e_old, axis=-1, keepdims=True) + jnp.sum(e_new, axis=-1, keepdims=True)
        o = dot(e_old.astype(BF), vc[:, cols]) + dot(e_new.astype(BF), vnew)
        o = (o / denom).astype(BF)
        for i in range(4):
            to = 4 * g + i
            for j in range(2):
                r0 = (2 * i + j) * TOKS
                asend[to, :, HD * j : HD * (j + 1)] = o[r0 : r0 + TOKS]

            def send():
                remote(asend.at[to], ain.at[own], asem, ar.at[b], 2 * to + core).start()

            if off == 0:
                pl.when(to != chip)(send)
            else:
                send()

    for off in (2, 1, 3, 0):
        heads(off)
    ain[own] = asend[chip]
    loads[8].wait()
    turn_weights(wu, wut)

    loads[4].wait()
    come("wo", wo.at[pl.ds(other_lane, HD)])
    order = (bf, bp, bm, b)
    for k, b_ in enumerate(order):
        await_bytes(ain.at[pl.ds(b_ * 4, 3 if k == 3 else 4)], ar.at[b_])

    def share(a_):
        rows = jnp.concatenate([ain[b_ * 4 + a_] for b_ in order], axis=0)
        return dot(rows, wo[...])

    s1[...] = share(af).astype(BF).reshape(4, TOKS, D)
    top_half, low_half = pl.ds(0, 16), pl.ds(16, 16)
    for k in range(4):
        go(("s", k, 0), s1.at[k, top_half], r1.at[k, top_half], up_a)
        go(("s", k, 1), s1.at[k, low_half], r1.at[k, low_half], down_a)
    pup[...] = share(ap).reshape(4, TOKS, D)
    pdown[...] = share(am).reshape(4, TOKS, D)
    pown[...] = share(a).reshape(4, TOKS, D)

    for load in loads[2:4]:
        load.wait()
    line = lax.broadcasted_iota(jnp.int32, (2 * N, TOKS), 0)
    expert = line // 2
    named = jnp.zeros((2 * N, TOKS), F32)
    weight = jnp.zeros((2 * N, TOKS), F32)
    turn_lanes = lax.rem(HD - lax.rem(t, 4) * TOKS, HD)
    idv = pltpu.roll(ids[...], turn_lanes, 1)[:, 0:TOKS]
    gv = pltpu.roll(gates[...], turn_lanes, 1)[:, 0:TOKS]
    for k in range(8):
        hit = jnp.broadcast_to(idv[k : k + 1], (2 * N, TOKS)) == expert
        named = jnp.where(hit, 1.0, named)
        weight = weight + jnp.where(hit, jnp.broadcast_to(gv[k : k + 1], (2 * N, TOKS)), 0.0)
    before = dot(named.astype(BF), jnp.where(ri < ci, 1.0, 0.0).astype(BF))
    turn = lax.rem(line, 2).astype(F32)
    taken = (named > 0.5) & (jnp.abs(before - turn) < 0.5)
    sel_ref[...] = jnp.where(taken, 1.0, 0.0).astype(BF)
    comb_ref[...] = jnp.where(taken, weight, 0.0)

    for k in range(4):
        come(("s", k, 0), r1.at[k, top_half])
        s2[k, 0, 0:16] = (pup[k, 0:16] + r1[k, 0:16].astype(F32)).astype(BF)
        s2[k, 0, 16:32] = pup[k, 16:32].astype(BF)
        go(("t", k, 0), s2.at[k, 0], r2.at[k, 0], up_a)
        come(("s", k, 1), r1.at[k, low_half])
        s2[k, 1, 0:16] = pdown[k, 0:16].astype(BF)
        s2[k, 1, 16:32] = (pdown[k, 16:32] + r1[k, 16:32].astype(F32)).astype(BF)
        go(("t", k, 1), s2.at[k, 1], r2.at[k, 1], down_a)
    for k, b_ in enumerate(order):
        come(("t", k, 0), r2.at[k, 0])
        come(("t", k, 1), r2.at[k, 1])
        rs = pown[k] + r2[k, 0].astype(F32) + r2[k, 1].astype(F32)
        if k < 3:
            v1[k] = rs.astype(BF)
            go(("v", k), v1.at[k], v2.at[k], dev(a, b_))
        else:
            hid[...] = res[...].astype(F32) + rs
    for k in range(3):
        come(("v", k), v2.at[k])
    hidden = hid[...] + (v2[0].astype(F32) + v2[1].astype(F32) + v2[2].astype(F32))
    hid[...] = hidden
    inv = lax.rsqrt(jnp.mean(hidden * hidden, axis=-1, keepdims=True) + EPSILON)
    normed = (hidden * inv * ffn_gain[...][None, :]).astype(BF)

    picked = dot(sel_ref[...], normed)
    for j in range(16):
        fs[pl.ds(j, 64, stride=16), :] = picked[:, HD * j : HD * (j + 1)]
    dsend[...] = fs[...].astype(BF).reshape(N, 32, HD)

    def post(src, dst, ssem, rsem):
        for da, db in FAR_FIRST:
            for other in range(2):
                if (da, db, other) == (0, 0, 0):
                    continue
                to = dev(ring(a, da), ring(b, db)) + other * (1 - 2 * core)
                remote(src.at[to], dst.at[t], ssem, rsem, to).start()

    pl.semaphore_wait(meet, 1)
    post(dsend, drecv, ds, dr)
    drecv[t] = dsend[t]
    loads[9].wait()
    await_bytes(drecv.at[pl.ds(0, N - 1)], dr)
    fs[...] = drecv[...].reshape(1024, HD).astype(F32)
    for j in range(16):
        xs[:, HD * j : HD * (j + 1)] = fs[pl.ds(j, 64, stride=16), :].astype(BF)
    gate = dot(xs[...], wgt[...])
    up = dot(xs[...], wut[...])
    inner = (gate / (1.0 + jnp.exp(-gate)) * up).astype(BF)
    y = dot(inner, wd[...])
    for j in range(16):
        fs[pl.ds(j, 64, stride=16), :] = y[:, HD * j : HD * (j + 1)]
    ysend[...] = fs[...].astype(BF).reshape(N, 32, HD)
    post(ysend, yrecv, ys, yr)
    yrecv[t] = ysend[t]
    for copy in sends:
        copy.wait_send()
    await_bytes(qsend.at[pl.ds(0, 15)], qs)
    await_bytes(asend.at[pl.ds(0, 15)], asem)
    await_bytes(dsend.at[pl.ds(0, N - 1)], ds)
    comb = comb_ref[...]
    comb_hi = comb.astype(BF)
    comb_lo = (comb - comb_hi.astype(F32)).astype(BF)
    await_bytes(yrecv.at[pl.ds(0, N - 1)], yr)
    fs[...] = yrecv[...].reshape(1024, HD).astype(F32)
    for j in range(16):
        yj = fs[pl.ds(j, 64, stride=16), :].astype(BF)
        moe = dot(comb_hi, yj, TN) + dot(comb_lo, yj, TN)
        cols = slice(HD * j, HD * (j + 1))
        out_ref[:, cols] = (hid[:, cols] + moe).astype(BF)
    await_bytes(ysend.at[pl.ds(0, N - 1)], ys)


def body(
    residual_in, attn_gain, w_query, w_keyval, query_gain, key_gain, w_out, ffn_gain,
    w_gate, w_up, w_down, key_cache, value_cache, prefix_lens, accepted, accept_path,
    parents, slot_kinds, expert_ids, gate_probs,
):
    half = np.arange(HD // 2, dtype=np.float64)
    freq = np.exp(-(2.0 * half / HD) * math.log(ROPE_BASE)).astype(np.float32)
    freq = jnp.asarray(np.concatenate([freq, freq])[None, :])
    vmem = pl.BlockSpec(memory_space=pltpu.VMEM)
    sm = pltpu.SMEM
    hbm = pl.BlockSpec(memory_space=pltpu.HBM)
    dma = pltpu.SemaphoreType.DMA
    vm = pltpu.VMEM
    return pl.pallas_call(
        layer_kernel,
        out_shape=pltpu.VMEM((TOKS, D), BF),
        in_specs=[hbm] * 21,
        out_specs=vmem,
        scratch_shapes=[
            vm((1, HD), F32),
            vm((D,), F32), vm((HD,), F32), vm((HD,), F32), vm((D,), F32),
            vm((1, TOKS), jnp.int32),
            sm((1,), jnp.int32), sm((1,), jnp.int32), sm((1, 8), jnp.int32), sm((1,), jnp.int32),
            vm((TOKS, D), BF),
            vm((D, 2 * HD), BF),
            vm((HD, D), BF),
            vm((2 * HD, D), BF),
            vm((FF, D), BF),
            vm((FF, D), BF),
            vm((FF, D), BF),
            vm((D, FF), BF),
            vm((D, FF), BF),
            vm((CACHE, 4 * HD), BF),
            vm((CACHE, 4 * HD), BF),
            vm((8, HD), jnp.int32),
            vm((8, HD), F32),
            vm((16, TOKS, D), BF),
            vm((16, TOKS, 3 * HD), BF),
            vm((16, TOKS, 3 * HD), BF),
            vm((16, TOKS, 2 * HD), BF),
            vm((16, TOKS, 2 * HD), BF),
            vm((4, TOKS, D), F32),
            vm((4, TOKS, D), F32),
            vm((4, TOKS, D), F32),
            vm((4, TOKS, D), BF),
            vm((4, TOKS, D), BF),
            vm((4, 2, TOKS, D), BF),
            vm((4, 2, TOKS, D), BF),
            vm((3, TOKS, D), BF),
            vm((3, TOKS, D), BF),
            vm((TOKS, D), F32),
            vm((1024, HD), F32),
            vm((2 * N, D), BF),
            vm((N, 32, HD), BF),
            vm((N, 32, HD), BF),
            vm((N, 32, HD), BF),
            vm((N, 32, HD), BF),
            vm((2 * N, TOKS), BF),
            vm((2 * N, TOKS), F32),
            vm((TOKS, HD), F32), vm((TOKS, HD), F32), vm((TOKS, HD), F32), vm((TOKS, HD), F32),
            vm((TOKS, TOKS), F32),
            vm((1, CACHE), F32),
            dma((11,)),
            dma((10,)),
            pltpu.SemaphoreType.REGULAR,
            dma((40,)), dma((40,)),
            dma(()), dma(()),
            dma(()), dma((4,)),
            dma(()), dma(()), dma(()), dma(()),
        ],
        compiler_params=pltpu.CompilerParams(
            collective_id=0, has_side_effects=True, vmem_limit_bytes=56 * 1024 * 1024
        ),
        name="layer",
    )(
        freq, attn_gain, query_gain, key_gain, ffn_gain, parents,
        prefix_lens, accepted, accept_path, slot_kinds,
        residual_in, w_query, w_keyval, w_out, w_gate, w_up, w_down,
        key_cache, value_cache, expert_ids.T, gate_probs.T,
    )


def solution(mesh):
    in_specs = (
        P(("group", "tensor"), None),
        P(),
        P(None, "tensor"),
        P("tensor", None),
        P(),
        P(),
        P("tensor", None),
        P(),
        P("tensor", None, None),
        P("tensor", None, None),
        P("tensor", None, None),
        P(("group", "tensor"), None, None),
        P(("group", "tensor"), None, None),
        P(("group", "tensor")),
        P(("group", "tensor")),
        P(("group", "tensor"), None),
        P(("group", "tensor"), None),
        P(("group", "tensor")),
        P("group", None),
        P("group", None),
    )
    out_specs = P(("group", "tensor"), None)
    return jax.shard_map(body, mesh=mesh, in_specs=in_specs, out_specs=out_specs, check_vma=False)
```
